32 devices in a mesh: dp: 8 (over z, x), tensor: 4 (over y, core).
Axes of the slice: x: 2, y: 2, z: 4, core: 2. Of those that a mesh axis runs over, the one named last changes fastest.
Arguments:
- query_states: bfloat16 [1, 8192, 1024], P(None, 'dp', 'tensor'), may hold values from -6 to 6
- key_states: bfloat16 [1, 8192, 1024], P(None, 'dp', 'tensor'), may hold values from -6 to 6
- value_states: bfloat16 [1, 8192, 1024], P(None, 'dp', 'tensor'), may hold values from -6 to 6
- joining_weight: bfloat16 [1, 1024, 2048], P(None, 'tensor'), may hold values from -0.1875 to 0.1875
- norm_gain: float32 [2048], replicated, may hold values from 0.1 to 1.9
- next_hidden: bfloat16 [8192, 2048], P(('dp', 'tensor')), may hold values from -6 to 6
- lengths: int32 [8], P('dp'), may hold values from 256 to 1024
- vote_counts: int32 [8], P('dp'), may hold values from 1 to 8
Outputs:
- draft_hidden: bfloat16 [8192, 2048], P(('dp', 'tensor'))
- weight_grad: bfloat16 [1, 1024, 2048], P(None, 'tensor', 'dp')
- gain_grad: float32 [2048], replicated
- draft_loss: float32 [], replicated
The draws below stay inside these ranges and needn't reach their ends.
All inputs are finite; a program needn't handle non-finite values.
Results may differ from the reference program's by a relative error of at most 0.014.
Values may be sent and summed in bfloat16 or wider, within the bound.
No kernel may reach another device: no remote copies, remote signals or barrier semaphores. Data moves between devices by JAX's collectives and lax.ppermute only.
A program may use at most 64 MiB of HBM per device.

```python
import math
import jax
import jax.numpy as jnp
from jax import lax

LAYERS = 1
LEN = 1024
HD = 128
DOUT = 2048
HC = 1024
TOK_G = 1024
CHAINS = 8
TOKENS = 8192
N_DP = 8
N_TENSOR = 4


def draw_query_states(key, part):
    baseline = jax.random.truncated_normal(jax.random.fold_in(key, 13), -6.0, 6.0, (LAYERS, TOKENS, HC), jnp.float32)
    return baseline.astype(jnp.bfloat16)


def draw_key_states(key, part):
    baseline = jax.random.truncated_normal(jax.random.fold_in(key, 11), -6.0, 6.0, (LAYERS, TOKENS, HC), jnp.float32)
    return baseline.astype(jnp.bfloat16)


def with_ends(values, rng, low, top_value):
    dims = values.shape
    place = [jax.random.randint(jax.random.fold_in(rng, axis), (), 0, dims[axis]) for axis in range(len(dims))]
    values = values.at[tuple(place)].set(low)
    longest = dims.index(max(dims))
    place[longest] = (place[longest] + 1) % dims[longest]
    return values.at[tuple(place)].set(top_value)


def level_of(rng, shape, split, smallest, largest):
    level = 1.0
    for position, blocks in split:
        draws = jax.random.uniform(jax.random.fold_in(jax.random.fold_in(rng, 6), position), (blocks,), jnp.float32, smallest / len(split), largest / len(split))
        level = level * jnp.repeat(jnp.exp(draws), shape[position] // blocks).reshape((-1,) + (1,) * (len(shape) - 1 - position))
    return level


def centred(stream_key, extent, scale, reach, shards=(), held_as=jnp.bfloat16):
    gain = level_of(stream_key, extent, shards, -0.22, 0.18) if shards else 1.0
    values = jax.random.normal(stream_key, extent, jnp.float32) * scale * gain
    return jnp.minimum(jnp.maximum(values, -reach), reach).astype(held_as)


def setup_inputs(seed: int = 0) -> dict:
    keys = jax.random.split(jax.random.key(seed), 9)
    query_states = draw_query_states(jax.random.fold_in(keys[8], 71), 0)
    key_states = draw_key_states(jax.random.fold_in(keys[8], 71), 0)
    value_states = centred(keys[2], (LAYERS, TOKENS, HC), 1.0, 6.0, ((1, 8), (2, 4)))
    joining_weight = centred(keys[3], (LAYERS, HC, DOUT), (LAYERS * HC) ** -0.5, 0.1875, ((1, 4),))
    norm_gain = jnp.clip(1.0 + 0.18 * jax.random.normal(keys[4], (DOUT,), jnp.float32), 0.1, 1.9)
    next_hidden = centred(keys[5], (TOKENS, DOUT), 1.0, 6.0, ((0, 32),))
    lengths = with_ends(jax.random.randint(keys[6], (CHAINS,), LEN // 4, LEN + 1), jax.random.fold_in(keys[6], 1), LEN // 4, LEN).astype(jnp.int32)
    vote_counts = with_ends(jax.random.randint(keys[7], (CHAINS,), 1, 9), jax.random.fold_in(keys[7], 1), 1, 8).astype(jnp.int32)
    return {"query_states": query_states, "key_states": key_states, "value_states": value_states, "joining_weight": joining_weight, "norm_gain": norm_gain, "next_hidden": next_hidden, "lengths": lengths, "vote_counts": vote_counts}


loss_scale = 65536.0
neg_large = -1e+30

def attend_chain(operands):
    chain_queries, chain_keys, chain_values, length = operands
    shaped = (LAYERS, LEN, HC // HD, HD)
    scores = jnp.einsum('lqhd,lkhd->lhqk', chain_queries.reshape(shaped).astype(jnp.float32), chain_keys.reshape(shaped).astype(jnp.float32)) / math.sqrt(HD)
    query_pos = jnp.arange(LEN)[:, None]
    key_pos = jnp.arange(LEN)[None, :]
    visible = (key_pos <= query_pos) & (key_pos < length)
    scores = jnp.where(visible, scores, neg_large)
    row_peak = lax.optimization_barrier(jnp.max(scores, axis=-1, keepdims=True))
    exponent = jnp.exp(scores - row_peak)
    attn_probs = (exponent / lax.optimization_barrier(jnp.sum(exponent, axis=-1, keepdims=True))).astype(jnp.bfloat16)
    context = jnp.einsum('lhqk,lkhd->lqhd', attn_probs.astype(jnp.float32), chain_values.reshape(shaped).astype(jnp.float32))
    return context.astype(jnp.bfloat16).reshape(LAYERS, LEN, HC)

def chain_view(states):
    return states.reshape(LAYERS, CHAINS, LEN, HC).transpose(1, 0, 2, 3)

def reference(query_states, key_states, value_states, joining_weight, norm_gain, next_hidden, lengths, vote_counts):
    context = lax.map(attend_chain, (chain_view(query_states), chain_view(key_states), chain_view(value_states), lengths))
    context = context.transpose(1, 0, 2, 3).reshape(LAYERS, TOKENS, HC)
    group_cols = HC // N_TENSOR
    joined = jnp.zeros((TOKENS, DOUT), jnp.float32)
    for group_idx in range(N_TENSOR):
        first_col = group_idx * group_cols
        partial_sum = jnp.zeros((TOKENS, DOUT), jnp.float32)
        for layer_idx in range(LAYERS):
            partial_sum = partial_sum + jnp.dot(context[layer_idx][:, first_col:first_col + group_cols], joining_weight[layer_idx][first_col:first_col + group_cols], preferred_element_type=jnp.float32)
        rounded = lax.optimization_barrier(partial_sum.astype(jnp.bfloat16))
        joined = joined + rounded.astype(jnp.float32)
    token_pos = jnp.arange(TOKENS, dtype=jnp.int32)
    chain_of = token_pos // LEN
    in_chain = token_pos % LEN
    tok_votes = vote_counts[chain_of].astype(jnp.float32)
    token_weight = jnp.where(in_chain < lengths[chain_of] - 1, tok_votes, 0.0).astype(jnp.float32)
    inv_rms = lax.rsqrt(lax.optimization_barrier(jnp.mean(joined * joined, axis=-1, keepdims=True)) + 1e-06)
    normed = joined * inv_rms
    predicted = normed * norm_gain
    draft_hidden = predicted.astype(jnp.bfloat16)
    misfit = predicted - next_hidden.astype(jnp.float32)
    weight_total = jnp.sum(token_weight)
    draft_loss = jnp.sum(token_weight * lax.optimization_barrier(jnp.mean(misfit * misfit, axis=-1))) / weight_total
    grad_pred = loss_scale * 2.0 / DOUT * token_weight[:, None] * misfit
    gain_grad = lax.optimization_barrier(jnp.sum(grad_pred * normed, axis=0)) / weight_total
    grad_normed = grad_pred * norm_gain
    grad_joined = (inv_rms * (grad_normed - normed * lax.optimization_barrier(jnp.mean(grad_normed * normed, axis=-1, keepdims=True)))).astype(jnp.bfloat16)
    accumulated = jnp.zeros((LAYERS, HC, DOUT), jnp.float32)
    for group_idx in range(N_DP):
        first_row = group_idx * TOK_G
        part_grad = jnp.einsum('ltc,td->lcd', context[:, first_row:first_row + TOK_G].astype(jnp.float32), grad_joined[first_row:first_row + TOK_G].astype(jnp.float32))
        accumulated = accumulated + lax.optimization_barrier(part_grad.astype(jnp.bfloat16)).astype(jnp.float32)
    weight_grad = (accumulated / weight_total).astype(jnp.bfloat16)
    return (draft_hidden, weight_grad, gain_grad, draft_loss)
```

```python
import functools
import math

import jax
import jax.numpy as jnp
from jax import lax
from jax.experimental import pallas as pl
from jax.experimental.pallas import tpu as pltpu
from jax.sharding import PartitionSpec as P

HD = 128
QB = 256
ROWS = 16
COLS = 512

loss_scale = 65536.0
neg_large = -1e30
MIB = 1 << 20


def dot(a, b, dims):
    return lax.dot_general(a, b, (dims, ((), ())), preferred_element_type=jnp.float32)


def attend(len_ref, q_ref, k_ref, v_ref, o_ref):
    seq = q_ref.shape[0]
    rate = math.log2(math.e) / math.sqrt(HD)
    length = len_ref[0]
    for i in range(seq // QB):
        rows = slice(i * QB, (i + 1) * QB)
        keys = (i + 1) * QB
        scores = dot(q_ref[rows, :], k_ref[:keys, :], ((1,), (1,)))
        col = lax.broadcasted_iota(jnp.int32, (1, keys), 1)
        scores = scores + jnp.where(col < length, 0.0, neg_large)
        r = lax.broadcasted_iota(jnp.int32, (QB, QB), 0)
        c = lax.broadcasted_iota(jnp.int32, (QB, QB), 1)
        last = jnp.where(c <= r, scores[:, keys - QB :], neg_large)
        scores = last if i == 0 else jnp.concatenate([scores[:, : keys - QB], last], 1)
        peak = jnp.max(scores, axis=1, keepdims=True)
        e = jnp.exp2((scores - peak) * rate)
        total = jnp.sum(e, axis=1, keepdims=True)
        out = dot(e.astype(jnp.bfloat16), v_ref[:keys, :], ((1,), (0,)))
        o_ref[rows, :] = (out / total).astype(jnp.bfloat16)


def attention(q, k, v, lengths):
    seq, width = q.shape
    heads = width // HD
    block = pl.BlockSpec((seq, HD), lambda h: (0, h))
    return pl.pallas_call(
        attend,
        grid=(heads,),
        in_specs=[pl.BlockSpec(memory_space=pltpu.SMEM), block, block, block],
        out_specs=block,
        out_shape=jax.ShapeDtypeStruct((seq, width), jnp.bfloat16),
        compiler_params=pltpu.CompilerParams(vmem_limit_bytes=32 * MIB),
        cost_estimate=pl.CostEstimate(
            flops=4 * seq * seq * width, bytes_accessed=8 * seq * width, transcendentals=heads * seq * seq
        ),
        name="attend",
    )(lengths, q, k, v)


def join_body(n_tensor, n_dp, chunks, seq, info_ref, ctx_ref, gain_ref, next_ref, *refs):
    w_refs = refs[:n_tensor]
    hidden_ref = refs[n_tensor]
    grad_refs = refs[n_tensor + 1 : n_tensor + 1 + chunks]
    stat_ref, joined_ref, square_ref, acc_ref = refs[n_tensor + 1 + chunks :]
    rows, dout = joined_ref.shape
    me, length, votes = info_ref[0], info_ref[1], info_ref[2]
    for c in range(0, dout, COLS):
        total = None
        for m in range(n_tensor):
            part = dot(ctx_ref[me ^ m], w_refs[m][:, c : c + COLS], ((1,), (0,)))
            part = part.astype(jnp.bfloat16).astype(jnp.float32)
            total = part if total is None else total + part
        joined_ref[:, c : c + COLS] = total
        sq = total * total
        lanes = sum(sq[:, i : i + 128] for i in range(0, COLS, 128))
        square_ref[...] = lanes if c == 0 else square_ref[...] + lanes
    acc_ref[...] = jnp.zeros_like(acc_ref)
    slice_w = dout // n_dp
    cw = slice_w // chunks

    def body(r, carry):
        loss, weights = carry
        at = pl.ds(pl.multiple_of(r * ROWS, ROWS), ROWS)
        inv = lax.rsqrt(jnp.sum(square_ref[at, :], axis=1, keepdims=True) * (1.0 / dout) + 1e-06)
        pos = (me * rows + r * ROWS) % seq + lax.broadcasted_iota(jnp.int32, (ROWS, 1), 0)
        weight = jnp.where(pos < length - 1, votes.astype(jnp.float32), 0.0)
        scaled = weight * (loss_scale * 2.0 / dout)
        miss = jnp.zeros((ROWS, 128), jnp.float32)
        lean = jnp.zeros((ROWS, 128), jnp.float32)
        for c in range(0, dout, COLS):
            cs = slice(c, c + COLS)
            normed = joined_ref[at, cs] * inv
            gain = gain_ref[:, cs]
            predicted = normed * gain
            hidden_ref[at, cs] = predicted.astype(jnp.bfloat16)
            misfit = predicted - next_ref[at, cs].astype(jnp.float32)
            grad = scaled * misfit
            both = grad * normed
            acc_ref[:, cs] += both
            sq = misfit * misfit
            ln = both * gain
            miss += sum(sq[:, i : i + 128] for i in range(0, COLS, 128))
            lean += sum(ln[:, i : i + 128] for i in range(0, COLS, 128))
            joined_ref[at, cs] = normed
        lean = jnp.sum(lean, axis=1, keepdims=True) * (1.0 / dout)
        for d in range(n_dp):
            for j in range(chunks):
                at0 = d * slice_w + j * cw
                cs = slice(at0, at0 + cw)
                normed = joined_ref[at, cs]
                gain = gain_ref[:, cs]
                misfit = normed * gain - next_ref[at, cs].astype(jnp.float32)
                g = inv * (scaled * misfit * gain - normed * lean)
                grad_refs[j][at, d * cw : (d + 1) * cw] = g.astype(jnp.bfloat16)
        loss = loss + weight * (jnp.sum(miss, axis=1, keepdims=True) * (1.0 / dout))
        return loss, weights + weight

    zero = jnp.zeros((ROWS, 1), jnp.float32)
    loss, weights = lax.fori_loop(0, rows // ROWS, body, (zero, zero))
    stat_ref[:, :dout] = jnp.sum(acc_ref[...], axis=0, keepdims=True)
    lane = lax.broadcasted_iota(jnp.int32, (1, 128), 1)
    loss = jnp.sum(loss, axis=0, keepdims=True)
    weights = jnp.sum(weights, axis=0, keepdims=True)
    stat_ref[:, dout:] = jnp.where(lane == 0, loss, jnp.where(lane == 1, weights, 0.0))


def join(info, ctx, gain, next_hidden, weights, n_dp, chunks, seq):
    n_tensor, rows, _ = ctx.shape
    dout = gain.shape[1]
    vmem = pl.BlockSpec(memory_space=pltpu.VMEM)
    out = pl.pallas_call(
        functools.partial(join_body, n_tensor, n_dp, chunks, seq),
        in_specs=[pl.BlockSpec(memory_space=pltpu.SMEM)] + [vmem] * (3 + n_tensor),
        out_specs=[vmem] * (2 + chunks),
        out_shape=[jax.ShapeDtypeStruct((rows, dout), jnp.bfloat16)]
        + [jax.ShapeDtypeStruct((rows, dout // chunks), jnp.bfloat16)] * chunks
        + [jax.ShapeDtypeStruct((1, dout + 128), jnp.float32)],
        scratch_shapes=[
            pltpu.VMEM((rows, dout), jnp.float32),
            pltpu.VMEM((rows, 128), jnp.float32),
            pltpu.VMEM((ROWS, dout), jnp.float32),
        ],
        compiler_params=pltpu.CompilerParams(vmem_limit_bytes=48 * MIB),
        cost_estimate=pl.CostEstimate(
            flops=2 * rows * dout * ctx.shape[2] * n_tensor,
            bytes_accessed=2 * dout * (ctx.shape[2] * n_tensor + 3 * rows),
            transcendentals=rows,
        ),
        name="join",
    )(info, ctx, gain, next_hidden, *weights)
    return out[0], out[1 : 1 + chunks], out[1 + chunks]


def grad_body(n_tensor, info_ref, ctx_ref, *refs):
    g_refs, out_ref = refs[:n_tensor], refs[n_tensor]
    n_dp, _, cw = out_ref.shape
    me = info_ref[0]
    step = max(1, 256 // cw)
    for d in range(0, n_dp, step):
        total = None
        for m in range(n_tensor):
            part = dot(ctx_ref[me ^ m], g_refs[m][:, d * cw : (d + step) * cw], ((0,), (0,)))
            total = part if total is None else total + part
        total = total.astype(jnp.bfloat16)
        for i in range(step):
            out_ref[d + i] = total[:, i * cw : (i + 1) * cw]


def gradient(info, ctx, grads, n_dp):
    n_tensor, rows, feats = ctx.shape
    cols = grads[0].shape[1]
    vmem = pl.BlockSpec(memory_space=pltpu.VMEM)
    return pl.pallas_call(
        functools.partial(grad_body, n_tensor),
        in_specs=[pl.BlockSpec(memory_space=pltpu.SMEM)] + [vmem] * (1 + n_tensor),
        out_specs=vmem,
        out_shape=jax.ShapeDtypeStruct((n_dp, feats, cols // n_dp), jnp.bfloat16),
        compiler_params=pltpu.CompilerParams(vmem_limit_bytes=48 * MIB),
        cost_estimate=pl.CostEstimate(
            flops=2 * n_tensor * rows * feats * cols,
            bytes_accessed=2 * (n_tensor * rows * (feats + cols) + feats * cols),
            transcendentals=0,
        ),
        name="gradient",
    )(info, ctx, *grads)


def swap(x, axis, n, mask):
    return lax.ppermute(x, axis, [(i, i ^ mask) for i in range(n)])


def gather_xor(x, axis, n):
    held = {0: x}
    bit = n // 2
    while bit:
        held.update({m | bit: swap(p, axis, n, bit) for m, p in list(held.items())})
        bit //= 2
    return [held[m] for m in range(n)]


def on_device(
    n_dp,
    n_tensor,
    query_states,
    key_states,
    value_states,
    joining_weight,
    norm_gain,
    next_hidden,
    lengths,
    vote_counts,
):
    _, tokens, width = query_states.shape
    seq = tokens // lengths.shape[0]
    dout = norm_gain.shape[0]
    rows = next_hidden.shape[0]
    chunks = 2 if dout // n_dp >= 256 else 1
    me = lax.axis_index("tensor").astype(jnp.int32)
    info = jnp.stack([me, lengths[0], vote_counts[0]])
    weights = gather_xor(joining_weight[0], "tensor", n_tensor)
    context = attention(query_states[0], key_states[0], value_states[0], lengths)
    context = context.reshape(n_tensor, rows, width)
    ctx = lax.all_to_all(context, "tensor", 0, 0, tiled=True)
    hidden, grads, stats = join(info, ctx, norm_gain[None, :], next_hidden, weights, n_dp, chunks, seq)
    parts = []
    for j in range(chunks):
        every = gather_xor(grads[j], "tensor", n_tensor)
        slabs = gradient(info, context, every, n_dp)
        parts.append(lax.all_to_all(slabs, "dp", 0, 0, tiled=True))
    for axis, n in (("tensor", n_tensor), ("dp", n_dp)):
        bit = 1
        while bit < n:
            stats = stats + swap(stats, axis, n, bit)
            bit *= 2
    stats = stats[0]
    weight_total = stats[dout + 1]
    cols = [jnp.sum(p.astype(jnp.float32), axis=0) for p in parts]
    weight_grad = (jnp.concatenate(cols, axis=1) / weight_total).astype(jnp.bfloat16)
    return (hidden, weight_grad[None], stats[:dout] / weight_total, stats[dout] / weight_total)


def solution(mesh):
    return jax.shard_map(
        functools.partial(on_device, mesh.shape["dp"], mesh.shape["tensor"]),
        mesh=mesh,
        in_specs=(
            P(None, "dp", "tensor"),
            P(None, "dp", "tensor"),
            P(None, "dp", "tensor"),
            P(None, "tensor", None),
            P(),
            P(("dp", "tensor"), None),
            P("dp"),
            P("dp"),
        ),
        out_specs=(P(("dp", "tensor"), None), P(None, "tensor", "dp"), P(), P()),
        check_vma=False,
    )
```

```python
import functools
import math

import jax
import jax.numpy as jnp
from jax import lax
from jax.experimental import pallas as pl
from jax.experimental.pallas import tpu as pltpu
from jax.sharding import PartitionSpec as P

HD = 128
QB = 256
ROWS = 16
COLS = 512

loss_scale = 65536.0
neg_large = -1e30
MIB = 1 << 20


def dot(a, b, dims):
    return lax.dot_general(a, b, (dims, ((), ())), preferred_element_type=jnp.float32)


def attend(len_ref, q_ref, k_ref, v_ref, o_ref):
    seq = q_ref.shape[0]
    rate = math.log2(math.e) / math.sqrt(HD)
    length = len_ref[0]
    for i in range(seq // QB):
        rows = slice(i * QB, (i + 1) * QB)
        keys = (i + 1) * QB
        scores = dot(q_ref[rows, :], k_ref[:keys, :], ((1,), (1,)))
        col = lax.broadcasted_iota(jnp.int32, (1, keys), 1)
        scores = scores + jnp.where(col < length, 0.0, neg_large)
        r = lax.broadcasted_iota(jnp.int32, (QB, QB), 0)
        c = lax.broadcasted_iota(jnp.int32, (QB, QB), 1)
        last = jnp.where(c <= r, scores[:, keys - QB :], neg_large)
        scores = last if i == 0 else jnp.concatenate([scores[:, : keys - QB], last], 1)
        peak = jnp.max(scores, axis=1, keepdims=True)
        e = jnp.exp2((scores - peak) * rate)
        total = jnp.sum(e, axis=1, keepdims=True)
        out = dot(e.astype(jnp.bfloat16), v_ref[:keys, :], ((1,), (0,)))
        o_ref[rows, :] = (out / total).astype(jnp.bfloat16)


def attention(q, k, v, lengths):
    seq, width = q.shape
    heads = width // HD
    block = pl.BlockSpec((seq, HD), lambda h: (0, h))
    return pl.pallas_call(
        attend,
        grid=(heads,),
        in_specs=[pl.BlockSpec(memory_space=pltpu.SMEM), block, block, block],
        out_specs=block,
        out_shape=jax.ShapeDtypeStruct((seq, width), jnp.bfloat16),
        compiler_params=pltpu.CompilerParams(vmem_limit_bytes=32 * MIB),
        cost_estimate=pl.CostEstimate(
            flops=4 * seq * seq * width, bytes_accessed=8 * seq * width, transcendentals=heads * seq * seq
        ),
        name="attend",
    )(lengths, q, k, v)


def join_body(n_tensor, n_dp, chunks, seq, info_ref, ctx_ref, gain_ref, next_ref, *refs):
    w_refs = refs[:n_tensor]
    hidden_ref = refs[n_tensor]
    grad_refs = refs[n_tensor + 1 : n_tensor + 1 + chunks]
    stat_ref, joined_ref, square_ref, acc_ref = refs[n_tensor + 1 + chunks :]
    rows, dout = joined_ref.shape
    me, length, votes = info_ref[0], info_ref[1], info_ref[2]
    for c in range(0, dout, COLS):
        total = None
        for m in range(n_tensor):
            part = dot(ctx_ref[me ^ m], w_refs[m][:, c : c + COLS], ((1,), (0,)))
            part = part.astype(jnp.bfloat16).astype(jnp.float32)
            total = part if total is None else total + part
        joined_ref[:, c : c + COLS] = total
        sq = total * total
        lanes = sum(sq[:, i : i + 128] for i in range(0, COLS, 128))
        square_ref[...] = lanes if c == 0 else square_ref[...] + lanes
    acc_ref[...] = jnp.zeros_like(acc_ref)
    slice_w = dout // n_dp
    cw = slice_w // chunks

    def body(r, carry):
        loss, weights = carry
        at = pl.ds(pl.multiple_of(r * ROWS, ROWS), ROWS)
        inv = lax.rsqrt(jnp.sum(square_ref[at, :], axis=1, keepdims=True) * (1.0 / dout) + 1e-06)
        pos = (me * rows + r * ROWS) % seq + lax.broadcasted_iota(jnp.int32, (ROWS, 1), 0)
        weight = jnp.where(pos < length - 1, votes.astype(jnp.float32), 0.0)
        scaled = weight * (loss_scale * 2.0 / dout)
        miss = jnp.zeros((ROWS, 128), jnp.float32)
        lean = jnp.zeros((ROWS, 128), jnp.float32)
        for c in range(0, dout, COLS):
            cs = slice(c, c + COLS)
            normed = joined_ref[at, cs] * inv
            gain = gain_ref[:, cs]
            predicted = normed * gain
            hidden_ref[at, cs] = predicted.astype(jnp.bfloat16)
            misfit = predicted - next_ref[at, cs].astype(jnp.float32)
            grad = scaled * misfit
            both = grad * normed
            acc_ref[:, cs] += both
            sq = misfit * misfit
            ln = both * gain
            miss += sum(sq[:, i : i + 128] for i in range(0, COLS, 128))
            lean += sum(ln[:, i : i + 128] for i in range(0, COLS, 128))
            joined_ref[at, cs] = normed
        lean = jnp.sum(lean, axis=1, keepdims=True) * (1.0 / dout)
        for d in range(n_dp):
            for j in range(chunks):
                at0 = d * slice_w + j * cw
                cs = slice(at0, at0 + cw)
                normed = joined_ref[at, cs]
                gain = gain_ref[:, cs]
                misfit = normed * gain - next_ref[at, cs].astype(jnp.float32)
                g = inv * (scaled * misfit * gain - normed * lean)
                grad_refs[j][at, d * cw : (d + 1) * cw] = g.astype(jnp.bfloat16)
        loss = loss + weight * (jnp.sum(miss, axis=1, keepdims=True) * (1.0 / dout))
        return loss, weights + weight

    zero = jnp.zeros((ROWS, 1), jnp.float32)
    loss, weights = lax.fori_loop(0, rows // ROWS, body, (zero, zero))
    stat_ref[:, :dout] = jnp.sum(acc_ref[...], axis=0, keepdims=True)
    lane = lax.broadcasted_iota(jnp.int32, (1, 128), 1)
    loss = jnp.sum(loss, axis=0, keepdims=True)
    weights = jnp.sum(weights, axis=0, keepdims=True)
    stat_ref[:, dout:] = jnp.where(lane == 0, loss, jnp.where(lane == 1, weights, 0.0))


def join(info, ctx, gain, next_hidden, weights, n_dp, chunks, seq):
    n_tensor, rows, _ = ctx.shape
    dout = gain.shape[1]
    vmem = pl.BlockSpec(memory_space=pltpu.VMEM)
    out = pl.pallas_call(
        functools.partial(join_body, n_tensor, n_dp, chunks, seq),
        in_specs=[pl.BlockSpec(memory_space=pltpu.SMEM)] + [vmem] * (3 + n_tensor),
        out_specs=[vmem] * (2 + chunks),
        out_shape=[jax.ShapeDtypeStruct((rows, dout), jnp.bfloat16)]
        + [jax.ShapeDtypeStruct((rows, dout // chunks), jnp.bfloat16)] * chunks
        + [jax.ShapeDtypeStruct((1, dout + 128), jnp.float32)],
        scratch_shapes=[
            pltpu.VMEM((rows, dout), jnp.float32),
            pltpu.VMEM((rows, 128), jnp.float32),
            pltpu.VMEM((ROWS, dout), jnp.float32),
        ],
        compiler_params=pltpu.CompilerParams(vmem_limit_bytes=48 * MIB),
        cost_estimate=pl.CostEstimate(
            flops=2 * rows * dout * ctx.shape[2] * n_tensor,
            bytes_accessed=2 * dout * (ctx.shape[2] * n_tensor + 3 * rows),
            transcendentals=rows,
        ),
        name="join",
    )(info, ctx, gain, next_hidden, *weights)
    return out[0], out[1 : 1 + chunks], out[1 + chunks]


def grad_body(n_tensor, info_ref, ctx_ref, *refs):
    g_refs, out_ref = refs[:n_tensor], refs[n_tensor]
    n_dp, _, cw = out_ref.shape
    me = info_ref[0]
    step = max(1, 256 // cw)
    for d in range(0, n_dp, step):
        total = None
        for m in range(n_tensor):
            part = dot(ctx_ref[me ^ m], g_refs[m][:, d * cw : (d + step) * cw], ((0,), (0,)))
            total = part if total is None else total + part
        total = total.astype(jnp.bfloat16)
        for i in range(step):
            out_ref[d + i] = total[:, i * cw : (i + 1) * cw]


def gradient(info, ctx, grads, n_dp):
    n_tensor, rows, feats = ctx.shape
    cols = grads[0].shape[1]
    vmem = pl.BlockSpec(memory_space=pltpu.VMEM)
    return pl.pallas_call(
        functools.partial(grad_body, n_tensor),
        in_specs=[pl.BlockSpec(memory_space=pltpu.SMEM)] + [vmem] * (1 + n_tensor),
        out_specs=vmem,
        out_shape=jax.ShapeDtypeStruct((n_dp, feats, cols // n_dp), jnp.bfloat16),
        compiler_params=pltpu.CompilerParams(vmem_limit_bytes=48 * MIB),
        cost_estimate=pl.CostEstimate(
            flops=2 * n_tensor * rows * feats * cols,
            bytes_accessed=2 * (n_tensor * rows * (feats + cols) + feats * cols),
            transcendentals=0,
        ),
        name="gradient",
    )(info, ctx, *grads)


def swap(x, axis, n, mask):
    return lax.ppermute(x, axis, [(i, i ^ mask) for i in range(n)])


def gather_xor(held, axis, n, bit):
    held = dict(held)
    while bit:
        held.update({m | bit: swap(p, axis, n, bit) for m, p in list(held.items())})
        bit //= 2
    return [held[m] for m in range(n)]


def on_device(
    n_dp,
    n_tensor,
    query_states,
    key_states,
    value_states,
    joining_weight,
    norm_gain,
    next_hidden,
    lengths,
    vote_counts,
):
    _, tokens, width = query_states.shape
    seq = tokens // lengths.shape[0]
    dout = norm_gain.shape[0]
    rows = next_hidden.shape[0]
    chunks = 2 if dout // n_dp >= 256 else 1
    me = lax.axis_index("tensor").astype(jnp.int32)
    info = jnp.stack([me, lengths[0], vote_counts[0]])
    held = {0: joining_weight[0]}
    held[n_tensor // 2] = swap(held[0], "tensor", n_tensor, n_tensor // 2)
    context = attention(query_states[0], key_states[0], value_states[0], lengths)
    context = context.reshape(n_tensor, rows, width)
    ctx = lax.all_to_all(context, "tensor", 0, 0, tiled=True)
    held[n_tensor // 2], ctx = lax.optimization_barrier((held[n_tensor // 2], ctx))
    weights = gather_xor(held, "tensor", n_tensor, n_tensor // 4)
    hidden, grads, stats = join(info, ctx, norm_gain[None, :], next_hidden, weights, n_dp, chunks, seq)
    half = n_tensor // 2
    far = [swap(g, "tensor", n_tensor, half) for g in grads]
    steps = [("dp", n_dp, 1 << i) for i in reversed(range(n_dp.bit_length() - 1))]
    steps += [("tensor", n_tensor, 1 << i) for i in range(n_tensor.bit_length() - 1)]
    parts = []
    for j in range(chunks):
        take = 3 if j + 1 < chunks else len(steps)
        for axis, n, bit in steps[:take]:
            stats = stats + swap(stats, axis, n, bit)
        steps = steps[take:]
        far[j], stats = lax.optimization_barrier((far[j], stats))
        every = gather_xor({0: grads[j], half: far[j]}, "tensor", n_tensor, half // 2)
        slabs = gradient(info, context, every, n_dp)
        parts.append(lax.all_to_all(slabs, "dp", 0, 0, tiled=True))
    stats = stats[0]
    weight_total = stats[dout + 1]
    cols = [jnp.sum(p.astype(jnp.float32), axis=0) for p in parts]
    weight_grad = (jnp.concatenate(cols, axis=1) / weight_total).astype(jnp.bfloat16)
    return (hidden, weight_grad[None], stats[:dout] / weight_total, stats[dout] / weight_total)


def solution(mesh):
    return jax.shard_map(
        functools.partial(on_device, mesh.shape["dp"], mesh.shape["tensor"]),
        mesh=mesh,
        in_specs=(
            P(None, "dp", "tensor"),
            P(None, "dp", "tensor"),
            P(None, "dp", "tensor"),
            P(None, "tensor", None),
            P(),
            P(("dp", "tensor"), None),
            P("dp"),
            P("dp"),
        ),
        out_specs=(P(("dp", "tensor"), None), P(None, "tensor", "dp"), P(), P()),
        check_vma=False,
    )
```

```python
import functools
import math

import jax
import jax.numpy as jnp
from jax import lax
from jax.experimental import pallas as pl
from jax.experimental.pallas import tpu as pltpu
from jax.sharding import PartitionSpec as P

HD = 128
QB = 256
ROWS = 16
COLS = 256
NEAR = 4
STAT_ROWS = 32

loss_scale = 65536.0
neg_large = -1e30
MIB = 1 << 20
BF = jnp.bfloat16
F32 = jnp.float32


def dot(a, b, dims):
    return lax.dot_general(a, b, (dims, ((), ())), preferred_element_type=F32)


def split_words(x):
    high = x.astype(BF).astype(F32)
    return high, (x - high).astype(BF).astype(F32)


def shape(dims, dtype=BF):
    return jax.ShapeDtypeStruct(dims, dtype)


def params():
    return pltpu.CompilerParams(vmem_limit_bytes=48 * MIB)


VM = pl.BlockSpec(memory_space=pltpu.VMEM)
SM = pl.BlockSpec(memory_space=pltpu.SMEM)


def attend_body(info_ref, q_ref, k_ref, v_ref, o_ref):
    seq = q_ref.shape[0]
    rows = o_ref.shape[2]
    rate = math.log2(math.e) / math.sqrt(HD)
    length = info_ref[2]
    for i in range(seq // QB):
        keys = (i + 1) * QB
        scores = dot(q_ref[i * QB : keys, :], k_ref[:keys, :], ((1,), (1,)))
        col = lax.broadcasted_iota(jnp.int32, (1, keys), 1)
        scores = scores + jnp.where(col < length, 0.0, neg_large)
        r = lax.broadcasted_iota(jnp.int32, (QB, QB), 0)
        c = lax.broadcasted_iota(jnp.int32, (QB, QB), 1)
        last = jnp.where(c <= r, scores[:, keys - QB :], neg_large)
        scores = last if i == 0 else jnp.concatenate([scores[:, : keys - QB], last], 1)
        peak = jnp.max(scores, axis=1, keepdims=True)
        e = jnp.exp2((scores - peak) * rate)
        total = jnp.sum(e, axis=1, keepdims=True)
        out = dot(e.astype(BF), v_ref[:keys, :], ((1,), (0,))) / total
        out = out.T.astype(BF)
        for n in range(QB // rows):
            o_ref[i * (QB // rows) + n] = out[:, n * rows : (n + 1) * rows]


def attend(info, q, k, v, rows):
    seq, width = q.shape
    heads = width // HD
    block = pl.BlockSpec((seq, HD), lambda h: (0, h))
    return pl.pallas_call(
        attend_body,
        grid=(heads,),
        in_specs=[SM, block, block, block],
        out_specs=pl.BlockSpec((seq // rows, HD, rows), lambda h: (0, h, 0)),
        out_shape=shape((seq // rows, width, rows)),
        compiler_params=params(),
        cost_estimate=pl.CostEstimate(
            flops=4 * seq * seq * width, bytes_accessed=8 * seq * width, transcendentals=heads * seq * seq
        ),
        name="attend",
    )(info, q, k, v)


def join_body(plan, counts, info_ref, ctx_ref, gain_ref, next_ref, *refs):
    n_dp, n_tensor, chunks, seq, xor_far = plan
    w_refs, at = [], 0
    for n in counts:
        w_refs.append(refs[at : at + n])
        at += n
    hidden_ref, grad_refs = refs[at], refs[at + 1 : -4]
    turned_ref, joined_ref, square_ref, acc_ref = refs[-4:]
    rows, dout = joined_ref.shape
    me, group, length, votes = info_ref[0], info_ref[1], info_ref[2], info_ref[3]
    for m in range(n_tensor):
        turned_ref[m] = ctx_ref[me ^ m].T
    for c in range(0, dout, COLS):
        total = None
        for m in range(n_tensor):
            first = 0
            for ref in w_refs[m]:
                if first <= c < first + ref.shape[1]:
                    w = ref[:, c - first : c - first + COLS]
                first += ref.shape[1]
            part = dot(turned_ref[m], w, ((1,), (0,)))
            part = part.astype(BF).astype(F32)
            total = part if total is None else total + part
        joined_ref[:, c : c + COLS] = total
        sq = total * total
        lanes = sum(sq[:, i : i + 128] for i in range(0, COLS, 128))
        square_ref[...] = lanes if c == 0 else square_ref[...] + lanes
    acc_ref[...] = jnp.zeros_like(acc_ref)
    slice_w = dout // n_dp
    cw = slice_w // chunks
    near, far = group % NEAR, group // NEAR
    n_far = n_dp // NEAR

    def body(r, carry):
        loss, weights = carry
        at = pl.ds(pl.multiple_of(r * ROWS, ROWS), ROWS)
        inv = lax.rsqrt(jnp.sum(square_ref[at, :], axis=1, keepdims=True) * (1.0 / dout) + 1e-06)
        pos = (me * rows + r * ROWS) % seq + lax.broadcasted_iota(jnp.int32, (ROWS, 1), 0)
        weight = jnp.where(pos < length - 1, votes.astype(F32), 0.0)
        scaled = weight * (loss_scale * 2.0 / dout)
        miss = jnp.zeros((ROWS, 128), F32)
        lean = jnp.zeros((ROWS, 128), F32)
        for c in range(0, dout, 512):
            cs = slice(c, c + 512)
            normed = joined_ref[at, cs] * inv
            gain = gain_ref[:, cs]
            predicted = normed * gain
            hidden_ref[at, cs] = predicted.astype(BF)
            misfit = predicted - next_ref[at, cs].astype(F32)
            both = scaled * misfit * normed
            acc_ref[:, cs] += both
            sq = misfit * misfit
            ln = both * gain
            miss += sum(sq[:, i : i + 128] for i in range(0, 512, 128))
            lean += sum(ln[:, i : i + 128] for i in range(0, 512, 128))
            joined_ref[at, cs] = normed
        lean = jnp.sum(lean, axis=1, keepdims=True) * (1.0 / dout)

        def gradient_at(cs):
            normed = joined_ref[at, cs]
            gain = gain_ref[:, cs]
            misfit = normed * gain - next_ref[at, cs].astype(F32)
            return (inv * (scaled * misfit * gain - normed * lean)).astype(BF)

        for j in range(chunks):
            for q in range(NEAR):
                for b in range(n_far):
                    to = slice(b * cw, (b + 1) * cw)
                    if cw % 128 == 0:
                        other = (far ^ b if xor_far else b) * NEAR + (near ^ q)
                        start = pl.multiple_of(other * slice_w + j * cw, 128)
                        grad_refs[j * NEAR + q][at, to] = gradient_at(pl.ds(start, cw))
                    else:
                        start = (b * NEAR + q) * slice_w + j * cw
                        grad_refs[j][near ^ q, at, to] = gradient_at(slice(start, start + cw))
        loss = loss + weight * (jnp.sum(miss, axis=1, keepdims=True) * (1.0 / dout))
        return loss, weights + weight

    zero = jnp.zeros((ROWS, 1), F32)
    loss, weights = lax.fori_loop(0, rows // ROWS, body, (zero, zero))
    wide = n_far * cw
    gain_sum = jnp.sum(acc_ref[...], axis=0, keepdims=True)
    gain_sum = jnp.concatenate([gain_sum[:, i : i + wide] for i in range(0, dout, wide)], 0)
    lane = lax.broadcasted_iota(jnp.int32, (1, wide), 1)
    loss = jnp.sum(loss, axis=0, keepdims=True)
    weights = jnp.sum(weights, axis=0, keepdims=True)
    scalars = jnp.where(lane == 0, loss, jnp.where(lane == 1, weights, 0.0))
    words = [*split_words(gain_sum), *split_words(scalars)]
    left = STAT_ROWS - sum(w.shape[0] for w in words)
    words = jnp.concatenate([*words, jnp.zeros((left, wide), F32)], 0).astype(BF)
    if cw % 128 == 0:
        for q in range(NEAR):
            grad_refs[q][rows:, :] = words
    else:
        for q in range(NEAR):
            grad_refs[0][q, rows:, :] = words


def join(plan, info, ctx, gain, next_hidden, weights):
    n_dp, n_tensor, chunks, _, _ = plan
    _, width, rows = ctx.shape
    dout = gain.shape[1]
    wide = dout // NEAR // chunks
    tall = [rows + STAT_ROWS] + [rows] * (chunks - 1)
    aligned = dout // n_dp // chunks % 128 == 0
    if aligned:
        grads = [shape((n, wide)) for n in tall for _ in range(NEAR)]
    else:
        grads = [shape((NEAR, n, wide)) for n in tall]
    out = pl.pallas_call(
        functools.partial(join_body, plan, [len(w) for w in weights]),
        in_specs=[SM] + [VM] * (3 + sum(len(w) for w in weights)),
        out_specs=[VM] * (1 + len(grads)),
        out_shape=[shape((rows, dout)), *grads],
        scratch_shapes=[
            pltpu.VMEM((n_tensor, rows, width), BF),
            pltpu.VMEM((rows, dout), F32),
            pltpu.VMEM((rows, 128), F32),
            pltpu.VMEM((ROWS, dout), F32),
        ],
        compiler_params=params(),
        cost_estimate=pl.CostEstimate(
            flops=2 * rows * dout * width * n_tensor,
            bytes_accessed=2 * dout * (width * n_tensor + 3 * rows),
            transcendentals=rows,
        ),
        name="join",
    )(info, ctx, gain, next_hidden, *[w for held in weights for w in held])
    if aligned:
        return out[0], [out[1 + j * NEAR : 1 + (j + 1) * NEAR] for j in range(chunks)]
    return out[0], [[g[q] for q in range(NEAR)] for g in out[1:]]


def stat_sizes(dout, wide, cw):
    in_block = dout // cw
    return dout // wide, in_block, -(-(2 * in_block + 2) // 16) * 16


def block_words(gains, scalars, tall, cw):
    words = [*split_words(gains), *split_words(scalars)]
    left = tall - sum(w.shape[0] for w in words)
    return jnp.concatenate([*words, jnp.zeros((left, cw), F32)], 0).astype(BF)


def block_sums(words, n):
    words = words.astype(F32)
    return words[:n] + words[n : 2 * n], words[2 * n : 2 * n + 1] + words[2 * n + 1 : 2 * n + 2]


def grad_body(plan, dout, info_ref, *refs):
    n_dp, n_tensor, _, _, xor_far = plan
    ctx_refs, g_refs, (keep_ref, send_ref) = refs[:NEAR], refs[NEAR : 2 * NEAR], refs[2 * NEAR :]
    n_y, n_far, tall, cw = keep_ref.shape
    feats, rows = ctx_refs[0].shape[1:]
    wide = n_far * cw
    me = info_ref[0]
    core, y = me % 2, me // 2
    if tall > feats:
        in_piece, in_block, stat_rows = stat_sizes(dout, wide, cw)
        sums = sum(ref[rows:, :].astype(F32) for ref in g_refs)
        gains, scalars = block_sums(sums, in_piece)
        gains = jnp.concatenate([gains[:, b * cw : (b + 1) * cw] for b in range(n_far)], 0)
        words = block_words(gains, scalars[:, :cw], stat_rows, cw)
    for s, ref in ((1, send_ref), (0, keep_ref)):
        for a in range(n_y):
            m = (y ^ a if xor_far else a) * 2 + (core ^ s)
            total = sum(dot(c[m], g[:rows, :], ((1,), (0,))) for c, g in zip(ctx_refs, g_refs))
            total = total.astype(BF)
            for b in range(n_far):
                ref[a, b, :feats, :] = total[:, b * cw : (b + 1) * cw]
                if tall > feats:
                    ref[a, b, feats:, :] = words


def gradient(plan, dout, info, ctxs, grads):
    n_dp, n_tensor, chunks, _, _ = plan
    _, feats, rows = ctxs[0].shape
    wide = grads[0].shape[1]
    cw = dout // n_dp // chunks
    tall = feats
    if grads[0].shape[0] > rows:
        tall += stat_sizes(dout, wide, cw)[2]
    block = shape((n_tensor // 2, n_dp // NEAR, tall, cw))
    return pl.pallas_call(
        functools.partial(grad_body, plan, dout),
        in_specs=[SM] + [VM] * (2 * NEAR),
        out_specs=[VM, VM],
        out_shape=[block, block],
        compiler_params=params(),
        cost_estimate=pl.CostEstimate(
            flops=2 * NEAR * n_tensor * rows * feats * wide,
            bytes_accessed=2 * (NEAR * rows * (n_tensor * feats + wide) + n_tensor * feats * wide),
            transcendentals=0,
        ),
        name="gradient",
    )(info, *ctxs, *grads)


def merge_body(in_block, feats, keep_ref, got_ref, *out_refs):
    n_y, n_far, tall, cw = keep_ref.shape
    if tall > feats:
        gains, scalars = block_sums(keep_ref[0, 0, feats:, :], in_block)
        more, others = block_sums(got_ref[0, 0, feats:, :], in_block)
        words = block_words(gains + more, scalars + others, tall - feats, cw)
    for i in range(n_y * n_far):
        a, b = divmod(i, n_far)
        total = keep_ref[a, b, :feats, :].astype(F32) + got_ref[a, b, :feats, :].astype(F32)
        ref, at = (out_refs[0], (a, b)) if len(out_refs) == 1 else (out_refs[i], (0, 0))
        ref[(*at, slice(0, feats), slice(None))] = total.astype(BF)
        if tall > feats:
            ref[(*at, slice(feats, tall), slice(None))] = words


def merge(plan, dout, feats, keep, got):
    n_y, n_far, tall, cw = keep.shape
    if plan[4]:
        outs = [shape((1, 1, tall, cw))] * (n_y * n_far)
    else:
        outs = [shape(keep.shape)]
    return pl.pallas_call(
        functools.partial(merge_body, dout // cw, feats),
        in_specs=[VM, VM],
        out_specs=[VM] * len(outs),
        out_shape=outs,
        compiler_params=params(),
        cost_estimate=pl.CostEstimate(flops=keep.size, bytes_accessed=6 * keep.size, transcendentals=0),
        name="merge",
    )(keep, got)


def finish_body(counts, in_piece, n_far, *refs):
    grad_ref, gain_ref, loss_ref = refs[-3:]
    feats = grad_ref.shape[0]
    chunks, at = [], 0
    for n in counts:
        chunks.append(refs[at : at + n])
        at += n
    tall, cw = chunks[0][0].shape[2:]

    def total(blocks, rows):
        parts = [
            r[a, b, rows, :].astype(F32) for r in blocks for a in range(r.shape[0]) for b in range(r.shape[1])
        ]
        return sum(parts[1:], parts[0])

    gains, scalars = block_sums(total(chunks[0], slice(feats, tall)), in_piece * n_far)
    lane = lax.broadcasted_iota(jnp.int32, (1, cw), 1)
    weight = jnp.sum(jnp.where(lane == 1, scalars, 0.0), axis=1, keepdims=True)
    loss_ref[0, 0] = jnp.sum(jnp.where(lane == 0, scalars / weight, 0.0))
    gains = gains / weight
    for r in range(in_piece):
        for b in range(n_far):
            gain_ref[pl.ds(r * n_far + b, 1), :] = gains[b * in_piece + r : b * in_piece + r + 1, :]
    for j, blocks in enumerate(chunks):
        grad_ref[:, j * cw : (j + 1) * cw] = (total(blocks, slice(0, feats)) / weight).astype(BF)


def finish(plan, dout, feats, chunks):
    n_dp = plan[0]
    cw = chunks[0][0].shape[3]
    n_far = n_dp // NEAR
    return pl.pallas_call(
        functools.partial(finish_body, [len(c) for c in chunks], dout // (n_far * cw), n_far),
        in_specs=[VM] * sum(len(c) for c in chunks),
        out_specs=[VM, VM, SM],
        out_shape=[shape((feats, dout // n_dp)), shape((dout // cw, cw), F32), shape((1, 1), F32)],
        compiler_params=params(),
        name="finish",
    )(*[b for c in chunks for b in c])


def swap(x, axis, n, mask):
    return lax.ppermute(x, axis, [(i, i ^ mask) for i in range(n)])


def swap_far(x, n_dp, n_tensor, a, b):
    mask = b * NEAR * n_tensor + a * 2
    return lax.ppermute(x, ("dp", "tensor"), [(i, i ^ mask) for i in range(n_dp * n_tensor)])


def exchange_far(plan, blocks):
    n_dp, n_tensor, _, _, xor_far = plan
    n_far = n_dp // NEAR
    if xor_far:
        return [blocks[0]] + [
            swap_far(block, n_dp, n_tensor, *divmod(i, n_far)) for i, block in enumerate(blocks) if i
        ]
    cores = [[2 * y + c for y in range(n_tensor // 2)] for c in range(2)]
    nears = [[NEAR * f + q for f in range(n_far)] for q in range(NEAR)]
    x = lax.all_to_all(blocks[0], "tensor", 0, 0, tiled=True, axis_index_groups=cores)
    return [lax.all_to_all(x, "dp", 1, 1, tiled=True, axis_index_groups=nears)]


def on_device(
    n_dp,
    n_tensor,
    query_states,
    key_states,
    value_states,
    joining_weight,
    norm_gain,
    next_hidden,
    lengths,
    vote_counts,
):
    _, tokens, width = query_states.shape
    seq = tokens // lengths.shape[0]
    dout = norm_gain.shape[0]
    rows = next_hidden.shape[0]
    chunks = 2 if dout // n_dp >= 256 else 1
    xor_far = (n_tensor // 2) * (n_dp // NEAR) <= 4
    plan = (n_dp, n_tensor, chunks, seq, xor_far)
    me = lax.axis_index("tensor").astype(jnp.int32)
    group = lax.axis_index("dp").astype(jnp.int32)
    info = jnp.stack([me, group, lengths[0], vote_counts[0]])

    weight = joining_weight[0]
    half = n_tensor // 2
    cut = dout * 3 // 8 // COLS * COLS
    first, second = weight[:, :cut], weight[:, cut:]
    first = swap(first, "tensor", n_tensor, half)
    context = attend(info, query_states[0], key_states[0], value_states[0], rows)
    second, context = lax.optimization_barrier((second, context))
    ctx = lax.all_to_all(context, "tensor", 0, 0, tiled=True)
    second = swap(second, "tensor", n_tensor, half)
    first, ctx = lax.optimization_barrier((first, ctx))
    ctxs = [ctx] + [swap(ctx, "dp", n_dp, q) for q in range(1, NEAR)]
    held = {0: [weight], half: [first, second]}
    bit = half // 2
    while bit:
        held.update({m | bit: [swap(p, "tensor", n_tensor, bit) for p in w] for m, w in list(held.items())})
        bit //= 2
    weights = [held[m] for m in range(n_tensor)]

    hidden, grads = join(plan, info, ctx, norm_gain[None, :], next_hidden, weights)
    parts = []
    for j in range(chunks):
        near = [grads[j][0]] + [swap(grads[j][q], "dp", n_dp, q) for q in range(1, NEAR)]
        keep, send = gradient(plan, dout, info, ctxs, near)
        blocks = merge(plan, dout, width, keep, swap(send, "tensor", n_tensor, 1))
        parts.append(exchange_far(plan, blocks))
    weight_grad, gain_grad, loss = finish(plan, dout, width, parts)
    return (hidden, weight_grad[None], gain_grad.reshape(dout), loss.reshape(()))


def solution(mesh):
    return jax.shard_map(
        functools.partial(on_device, mesh.shape["dp"], mesh.shape["tensor"]),
        mesh=mesh,
        in_specs=(
            P(None, "dp", "tensor"),
            P(None, "dp", "tensor"),
            P(None, "dp", "tensor"),
            P(None, "tensor", None),
            P(),
            P(("dp", "tensor"), None),
            P("dp"),
            P("dp"),
        ),
        out_specs=(P(("dp", "tensor"), None), P(None, "tensor", "dp"), P(), P()),
        check_vma=False,
    )
```

```python
import functools
import math

import jax
import jax.numpy as jnp
from jax import lax
from jax.experimental import pallas as pl
from jax.experimental.pallas import tpu as pltpu
from jax.sharding import PartitionSpec as P

HD = 128
QB = 256
ROWS = 16
COLS = 256
NEAR = 4
STAT_ROWS = 32

loss_scale = 65536.0
neg_large = -1e30
MIB = 1 << 20
BF = jnp.bfloat16
F32 = jnp.float32


def dot(a, b, dims):
    return lax.dot_general(a, b, (dims, ((), ())), preferred_element_type=F32)


def split_words(x):
    high = x.astype(BF).astype(F32)
    return high, (x - high).astype(BF).astype(F32)


def shape(dims, dtype=BF):
    return jax.ShapeDtypeStruct(dims, dtype)


def params():
    return pltpu.CompilerParams(vmem_limit_bytes=48 * MIB)


VM = pl.BlockSpec(memory_space=pltpu.VMEM)
SM = pl.BlockSpec(memory_space=pltpu.SMEM)


def attend_body(info_ref, q_ref, k_ref, v_ref, o_ref):
    seq = q_ref.shape[0]
    rows = o_ref.shape[2]
    rate = math.log2(math.e) / math.sqrt(HD)
    length = info_ref[2]
    for i in range(seq // QB):
        keys = (i + 1) * QB
        scores = dot(q_ref[i * QB : keys, :], k_ref[:keys, :], ((1,), (1,)))
        col = lax.broadcasted_iota(jnp.int32, (1, keys), 1)
        scores = scores + jnp.where(col < length, 0.0, neg_large)
        r = lax.broadcasted_iota(jnp.int32, (QB, QB), 0)
        c = lax.broadcasted_iota(jnp.int32, (QB, QB), 1)
        last = jnp.where(c <= r, scores[:, keys - QB :], neg_large)
        scores = last if i == 0 else jnp.concatenate([scores[:, : keys - QB], last], 1)
        peak = jnp.max(scores, axis=1, keepdims=True)
        e = jnp.exp2((scores - peak) * rate)
        total = jnp.sum(e, axis=1, keepdims=True)
        out = dot(e.astype(BF), v_ref[:keys, :], ((1,), (0,))) / total
        out = out.T.astype(BF)
        for n in range(QB // rows):
            o_ref[i * (QB // rows) + n] = out[:, n * rows : (n + 1) * rows]


def attend(info, q, k, v, rows):
    seq, width = q.shape
    heads = width // HD
    block = pl.BlockSpec((seq, HD), lambda h: (0, h))
    return pl.pallas_call(
        attend_body,
        grid=(heads,),
        in_specs=[SM, block, block, block],
        out_specs=pl.BlockSpec((seq // rows, HD, rows), lambda h: (0, h, 0)),
        out_shape=shape((seq // rows, width, rows)),
        compiler_params=params(),
        cost_estimate=pl.CostEstimate(
            flops=4 * seq * seq * width, bytes_accessed=8 * seq * width, transcendentals=heads * seq * seq
        ),
        name="attend",
    )(info, q, k, v)


def join_body(plan, counts, info_ref, ctx_ref, gain_ref, next_ref, *refs):
    n_dp, n_tensor, chunks, seq, xor_far = plan
    w_refs, at = [], 0
    for n in counts:
        w_refs.append(refs[at : at + n])
        at += n
    hidden_ref, grad_refs = refs[at], refs[at + 1 : -4]
    turned_ref, joined_ref, square_ref, acc_ref = refs[-4:]
    rows, dout = joined_ref.shape
    me, group, length, votes = info_ref[0], info_ref[1], info_ref[2], info_ref[3]
    for m in range(n_tensor):
        turned_ref[m] = ctx_ref[me ^ m].T
    for c in range(0, dout, COLS):
        total = None
        for m in range(n_tensor):
            first = 0
            for ref in w_refs[m]:
                if first <= c < first + ref.shape[1]:
                    w = ref[:, c - first : c - first + COLS]
                first += ref.shape[1]
            part = dot(turned_ref[m], w, ((1,), (0,)))
            part = part.astype(BF).astype(F32)
            total = part if total is None else total + part
        joined_ref[:, c : c + COLS] = total
        sq = total * total
        lanes = sum(sq[:, i : i + 128] for i in range(0, COLS, 128))
        square_ref[...] = lanes if c == 0 else square_ref[...] + lanes
    acc_ref[...] = jnp.zeros_like(acc_ref)
    slice_w = dout // n_dp
    cw = slice_w // chunks
    near, far = group % NEAR, group // NEAR
    n_far = n_dp // NEAR

    def body(r, carry):
        loss, weights = carry
        at = pl.ds(pl.multiple_of(r * ROWS, ROWS), ROWS)
        inv = lax.rsqrt(jnp.sum(square_ref[at, :], axis=1, keepdims=True) * (1.0 / dout) + 1e-06)
        pos = (me * rows + r * ROWS) % seq + lax.broadcasted_iota(jnp.int32, (ROWS, 1), 0)
        weight = jnp.where(pos < length - 1, votes.astype(F32), 0.0)
        scaled = weight * (loss_scale * 2.0 / dout)
        miss = jnp.zeros((ROWS, 128), F32)
        lean = jnp.zeros((ROWS, 128), F32)
        for c in range(0, dout, 512):
            cs = slice(c, c + 512)
            normed = joined_ref[at, cs] * inv
            gain = gain_ref[:, cs]
            predicted = normed * gain
            hidden_ref[at, cs] = predicted.astype(BF)
            misfit = predicted - next_ref[at, cs].astype(F32)
            both = scaled * misfit * normed
            acc_ref[:, cs] += both
            sq = misfit * misfit
            ln = both * gain
            miss += sum(sq[:, i : i + 128] for i in range(0, 512, 128))
            lean += sum(ln[:, i : i + 128] for i in range(0, 512, 128))
            joined_ref[at, cs] = normed
        lean = jnp.sum(lean, axis=1, keepdims=True) * (1.0 / dout)

        def gradient_at(cs):
            normed = joined_ref[at, cs]
            gain = gain_ref[:, cs]
            misfit = normed * gain - next_ref[at, cs].astype(F32)
            return (inv * (scaled * misfit * gain - normed * lean)).astype(BF)

        for j in range(chunks):
            for q in range(NEAR):
                for b in range(n_far):
                    to = slice(b * cw, (b + 1) * cw)
                    if cw % 128 == 0:
                        other = (far ^ b if xor_far else b) * NEAR + (near ^ q)
                        start = pl.multiple_of(other * slice_w + j * cw, 128)
                        grad_refs[j * NEAR + q][at, to] = gradient_at(pl.ds(start, cw))
                    else:
                        start = (b * NEAR + q) * slice_w + j * cw
                        grad_refs[j][near ^ q, at, to] = gradient_at(slice(start, start + cw))
        loss = loss + weight * (jnp.sum(miss, axis=1, keepdims=True) * (1.0 / dout))
        return loss, weights + weight

    zero = jnp.zeros((ROWS, 1), F32)
    loss, weights = lax.fori_loop(0, rows // ROWS, body, (zero, zero))
    wide = n_far * cw
    gain_sum = jnp.sum(acc_ref[...], axis=0, keepdims=True)
    gain_sum = jnp.concatenate([gain_sum[:, i : i + wide] for i in range(0, dout, wide)], 0)
    lane = lax.broadcasted_iota(jnp.int32, (1, wide), 1)
    loss = jnp.sum(loss, axis=0, keepdims=True)
    weights = jnp.sum(weights, axis=0, keepdims=True)
    scalars = jnp.where(lane == 0, loss, jnp.where(lane == 1, weights, 0.0))
    words = [*split_words(gain_sum), *split_words(scalars)]
    left = STAT_ROWS - sum(w.shape[0] for w in words)
    words = jnp.concatenate([*words, jnp.zeros((left, wide), F32)], 0).astype(BF)
    if cw % 128 == 0:
        for q in range(NEAR):
            grad_refs[q][rows:, :] = words
    else:
        for q in range(NEAR):
            grad_refs[0][q, rows:, :] = words


def join(plan, info, ctx, gain, next_hidden, weights):
    n_dp, n_tensor, chunks, _, _ = plan
    _, width, rows = ctx.shape
    dout = gain.shape[1]
    wide = dout // NEAR // chunks
    tall = [rows + STAT_ROWS] + [rows] * (chunks - 1)
    aligned = dout // n_dp // chunks % 128 == 0
    if aligned:
        grads = [shape((n, wide)) for n in tall for _ in range(NEAR)]
    else:
        grads = [shape((NEAR, n, wide)) for n in tall]
    out = pl.pallas_call(
        functools.partial(join_body, plan, [len(w) for w in weights]),
        in_specs=[SM] + [VM] * (3 + sum(len(w) for w in weights)),
        out_specs=[VM] * (1 + len(grads)),
        out_shape=[shape((rows, dout)), *grads],
        scratch_shapes=[
            pltpu.VMEM((n_tensor, rows, width), BF),
            pltpu.VMEM((rows, dout), F32),
            pltpu.VMEM((rows, 128), F32),
            pltpu.VMEM((ROWS, dout), F32),
        ],
        compiler_params=params(),
        cost_estimate=pl.CostEstimate(
            flops=2 * rows * dout * width * n_tensor,
            bytes_accessed=2 * dout * (width * n_tensor + 3 * rows),
            transcendentals=rows,
        ),
        name="join",
    )(info, ctx, gain, next_hidden, *[w for held in weights for w in held])
    if aligned:
        return out[0], [out[1 + j * NEAR : 1 + (j + 1) * NEAR] for j in range(chunks)]
    return out[0], [[g[q] for q in range(NEAR)] for g in out[1:]]


def stat_sizes(dout, wide, cw):
    in_block = dout // cw
    return dout // wide, in_block, -(-(2 * in_block + 2) // 16) * 16


def block_words(gains, scalars, tall, cw):
    words = [*split_words(gains), *split_words(scalars)]
    left = tall - sum(w.shape[0] for w in words)
    return jnp.concatenate([*words, jnp.zeros((left, cw), F32)], 0).astype(BF)


def block_sums(words, n):
    words = words.astype(F32)
    return words[:n] + words[n : 2 * n], words[2 * n : 2 * n + 1] + words[2 * n + 1 : 2 * n + 2]


def grad_body(plan, dout, info_ref, *refs):
    n_dp, n_tensor, _, _, xor_far = plan
    ctx_refs, g_refs, (keep_ref, send_ref) = refs[:NEAR], refs[NEAR : 2 * NEAR], refs[2 * NEAR :]
    n_y, n_far, tall, cw = keep_ref.shape
    feats, rows = ctx_refs[0].shape[1:]
    wide = n_far * cw
    me = info_ref[0]
    core, y = me % 2, me // 2
    if tall > feats:
        in_piece, in_block, stat_rows = stat_sizes(dout, wide, cw)
        sums = sum(ref[rows:, :].astype(F32) for ref in g_refs)
        gains, scalars = block_sums(sums, in_piece)
        gains = jnp.concatenate([gains[:, b * cw : (b + 1) * cw] for b in range(n_far)], 0)
        words = block_words(gains, scalars[:, :cw], stat_rows, cw)
    for s, ref in ((1, send_ref), (0, keep_ref)):
        for a in range(n_y):
            m = (y ^ a if xor_far else a) * 2 + (core ^ s)
            total = sum(dot(c[m], g[:rows, :], ((1,), (0,))) for c, g in zip(ctx_refs, g_refs))
            total = total.astype(BF)
            for b in range(n_far):
                ref[a, b, :feats, :] = total[:, b * cw : (b + 1) * cw]
                if tall > feats:
                    ref[a, b, feats:, :] = words


def gradient(plan, dout, info, ctxs, grads):
    n_dp, n_tensor, chunks, _, _ = plan
    _, feats, rows = ctxs[0].shape
    wide = grads[0].shape[1]
    cw = dout // n_dp // chunks
    tall = feats
    if grads[0].shape[0] > rows:
        tall += stat_sizes(dout, wide, cw)[2]
    block = shape((n_tensor // 2, n_dp // NEAR, tall, cw))
    return pl.pallas_call(
        functools.partial(grad_body, plan, dout),
        in_specs=[SM] + [VM] * (2 * NEAR),
        out_specs=[VM, VM],
        out_shape=[block, block],
        compiler_params=params(),
        cost_estimate=pl.CostEstimate(
            flops=2 * NEAR * n_tensor * rows * feats * wide,
            bytes_accessed=2 * (NEAR * rows * (n_tensor * feats + wide) + n_tensor * feats * wide),
            transcendentals=0,
        ),
        name="gradient",
    )(info, *ctxs, *grads)


def merge_body(in_block, feats, keep_ref, got_ref, *out_refs):
    n_y, n_far, tall, cw = keep_ref.shape
    if tall > feats:
        gains, scalars = block_sums(keep_ref[0, 0, feats:, :], in_block)
        more, others = block_sums(got_ref[0, 0, feats:, :], in_block)
        words = block_words(gains + more, scalars + others, tall - feats, cw)
    for i in range(n_y * n_far):
        a, b = divmod(i, n_far)
        total = keep_ref[a, b, :feats, :].astype(F32) + got_ref[a, b, :feats, :].astype(F32)
        ref, at = (out_refs[0], (a, b)) if len(out_refs) == 1 else (out_refs[i], (0, 0))
        ref[(*at, slice(0, feats), slice(None))] = total.astype(BF)
        if tall > feats:
            ref[(*at, slice(feats, tall), slice(None))] = words


def merge(plan, dout, feats, keep, got):
    n_y, n_far, tall, cw = keep.shape
    if plan[4]:
        outs = [shape((1, 1, tall, cw))] * (n_y * n_far)
    else:
        outs = [shape(keep.shape)]
    return pl.pallas_call(
        functools.partial(merge_body, dout // cw, feats),
        in_specs=[VM, VM],
        out_specs=[VM] * len(outs),
        out_shape=outs,
        compiler_params=params(),
        cost_estimate=pl.CostEstimate(flops=keep.size, bytes_accessed=6 * keep.size, transcendentals=0),
        name="merge",
    )(keep, got)


def finish_body(counts, in_piece, n_far, *refs):
    grad_ref, gain_ref, loss_ref = refs[-3:]
    feats = grad_ref.shape[0]
    chunks, at = [], 0
    for n in counts:
        chunks.append(refs[at : at + n])
        at += n
    tall, cw = chunks[0][0].shape[2:]

    def total(blocks, rows):
        parts = [
            r[a, b, rows, :].astype(F32) for r in blocks for a in range(r.shape[0]) for b in range(r.shape[1])
        ]
        return sum(parts[1:], parts[0])

    gains, scalars = block_sums(total(chunks[0], slice(feats, tall)), in_piece * n_far)
    lane = lax.broadcasted_iota(jnp.int32, (1, cw), 1)
    weight = jnp.sum(jnp.where(lane == 1, scalars, 0.0), axis=1, keepdims=True)
    loss_ref[0, 0] = jnp.sum(jnp.where(lane == 0, scalars / weight, 0.0))
    gains = gains / weight
    for r in range(in_piece):
        for b in range(n_far):
            gain_ref[pl.ds(r * n_far + b, 1), :] = gains[b * in_piece + r : b * in_piece + r + 1, :]
    for j, blocks in enumerate(chunks):
        grad_ref[:, j * cw : (j + 1) * cw] = (total(blocks, slice(0, feats)) / weight).astype(BF)


def finish(plan, dout, feats, chunks):
    n_dp = plan[0]
    cw = chunks[0][0].shape[3]
    n_far = n_dp // NEAR
    return pl.pallas_call(
        functools.partial(finish_body, [len(c) for c in chunks], dout // (n_far * cw), n_far),
        in_specs=[VM] * sum(len(c) for c in chunks),
        out_specs=[VM, VM, SM],
        out_shape=[shape((feats, dout // n_dp)), shape((dout // cw, cw), F32), shape((1, 1), F32)],
        compiler_params=params(),
        name="finish",
    )(*[b for c in chunks for b in c])


def swap(x, axis, n, mask):
    return lax.ppermute(x, axis, [(i, i ^ mask) for i in range(n)])


def swap_far(x, n_dp, n_tensor, a, b):
    mask = b * NEAR * n_tensor + a * 2
    return lax.ppermute(x, ("dp", "tensor"), [(i, i ^ mask) for i in range(n_dp * n_tensor)])


def exchange_far(plan, blocks):
    n_dp, n_tensor, _, _, xor_far = plan
    n_far = n_dp // NEAR
    if xor_far:
        return [blocks[0]] + [
            swap_far(block, n_dp, n_tensor, *divmod(i, n_far)) for i, block in enumerate(blocks) if i
        ]
    cores = [[2 * y + c for y in range(n_tensor // 2)] for c in range(2)]
    nears = [[NEAR * f + q for f in range(n_far)] for q in range(NEAR)]
    x = lax.all_to_all(blocks[0], "tensor", 0, 0, tiled=True, axis_index_groups=cores)
    return [lax.all_to_all(x, "dp", 1, 1, tiled=True, axis_index_groups=nears)]


def on_device(
    n_dp,
    n_tensor,
    query_states,
    key_states,
    value_states,
    joining_weight,
    norm_gain,
    next_hidden,
    lengths,
    vote_counts,
):
    _, tokens, width = query_states.shape
    seq = tokens // lengths.shape[0]
    dout = norm_gain.shape[0]
    rows = next_hidden.shape[0]
    chunks = 2 if dout // n_dp >= 256 else 1
    xor_far = (n_tensor // 2) * (n_dp // NEAR) <= 4
    plan = (n_dp, n_tensor, chunks, seq, xor_far)
    me = lax.axis_index("tensor").astype(jnp.int32)
    group = lax.axis_index("dp").astype(jnp.int32)
    info = jnp.stack([me, group, lengths[0], vote_counts[0]])

    weight = joining_weight[0]
    half = n_tensor // 2
    cut = dout * 3 // 8 // COLS * COLS
    first, second = weight[:, :cut], weight[:, cut:]
    first = swap(first, "tensor", n_tensor, half)
    beside = swap(weight, "tensor", n_tensor, 1)
    context = attend(info, query_states[0], key_states[0], value_states[0], rows)
    first, beside, context = lax.optimization_barrier((first, beside, context))
    ctx = lax.all_to_all(context, "tensor", 0, 0, tiled=True)
    across = swap(first, "tensor", n_tensor, 1)
    across, second, ctx = lax.optimization_barrier((across, second, ctx))
    second = swap(second, "tensor", n_tensor, half)
    ctxs = [ctx] + [swap(ctx, "dp", n_dp, q) for q in range(1, NEAR)]
    held = {0: [weight], 1: [beside], half: [first, second]}
    held[half + 1] = [across, swap(second, "tensor", n_tensor, 1)]
    bit = half // 2
    while bit > 1:
        held.update({m ^ bit: [swap(p, "tensor", n_tensor, bit) for p in w] for m, w in list(held.items())})
        bit //= 2
    weights = [held[m] for m in range(n_tensor)]

    hidden, grads = join(plan, info, ctx, norm_gain[None, :], next_hidden, weights)
    parts = []
    for j in range(chunks):
        near = [grads[j][0]] + [swap(grads[j][q], "dp", n_dp, q) for q in range(1, NEAR)]
        keep, send = gradient(plan, dout, info, ctxs, near)
        blocks = merge(plan, dout, width, keep, swap(send, "tensor", n_tensor, 1))
        parts.append(exchange_far(plan, blocks))
    weight_grad, gain_grad, loss = finish(plan, dout, width, parts)
    return (hidden, weight_grad[None], gain_grad.reshape(dout), loss.reshape(()))


def solution(mesh):
    return jax.shard_map(
        functools.partial(on_device, mesh.shape["dp"], mesh.shape["tensor"]),
        mesh=mesh,
        in_specs=(
            P(None, "dp", "tensor"),
            P(None, "dp", "tensor"),
            P(None, "dp", "tensor"),
            P(None, "tensor", None),
            P(),
            P(("dp", "tensor"), None),
            P("dp"),
            P("dp"),
        ),
        out_specs=(P(("dp", "tensor"), None), P(None, "tensor", "dp"), P(), P()),
        check_vma=False,
    )
```

```python
import functools
import math

import jax
import jax.numpy as jnp
from jax import lax
from jax.experimental import pallas as pl
from jax.experimental.pallas import tpu as pltpu
from jax.sharding import PartitionSpec as P

HD = 128
QB = 256
ROWS = 16
COLS = 256
NEAR = 4
STAT_ROWS = 32

loss_scale = 65536.0
neg_large = -1e30
MIB = 1 << 20
BF = jnp.bfloat16
F32 = jnp.float32


def dot(a, b, dims):
    return lax.dot_general(a, b, (dims, ((), ())), preferred_element_type=F32)


def split_words(x):
    high = x.astype(BF).astype(F32)
    return high, (x - high).astype(BF).astype(F32)


def shape(dims, dtype=BF):
    return jax.ShapeDtypeStruct(dims, dtype)


def params():
    return pltpu.CompilerParams(vmem_limit_bytes=48 * MIB)


VM = pl.BlockSpec(memory_space=pltpu.VMEM)
SM = pl.BlockSpec(memory_space=pltpu.SMEM)


def attend_body(info_ref, q_ref, k_ref, v_ref, o_ref):
    seq = q_ref.shape[0]
    rows = o_ref.shape[2]
    rate = math.log2(math.e) / math.sqrt(HD)
    length = info_ref[2]
    for i in range(seq // QB):
        keys = (i + 1) * QB
        scores = dot(q_ref[i * QB : keys, :], k_ref[:keys, :], ((1,), (1,)))
        col = lax.broadcasted_iota(jnp.int32, (1, keys), 1)
        scores = scores + jnp.where(col < length, 0.0, neg_large)
        r = lax.broadcasted_iota(jnp.int32, (QB, QB), 0)
        c = lax.broadcasted_iota(jnp.int32, (QB, QB), 1)
        last = jnp.where(c <= r, scores[:, keys - QB :], neg_large)
        scores = last if i == 0 else jnp.concatenate([scores[:, : keys - QB], last], 1)
        peak = jnp.max(scores, axis=1, keepdims=True)
        e = jnp.exp2((scores - peak) * rate)
        total = jnp.sum(e, axis=1, keepdims=True)
        out = dot(e.astype(BF), v_ref[:keys, :], ((1,), (0,))) / total
        out = out.T.astype(BF)
        for n in range(QB // rows):
            o_ref[i * (QB // rows) + n] = out[:, n * rows : (n + 1) * rows]


def attend(info, q, k, v, rows):
    seq, width = q.shape
    heads = width // HD
    block = pl.BlockSpec((seq, HD), lambda h: (0, h))
    return pl.pallas_call(
        attend_body,
        grid=(heads,),
        in_specs=[SM, block, block, block],
        out_specs=pl.BlockSpec((seq // rows, HD, rows), lambda h: (0, h, 0)),
        out_shape=shape((seq // rows, width, rows)),
        compiler_params=params(),
        cost_estimate=pl.CostEstimate(
            flops=4 * seq * seq * width, bytes_accessed=8 * seq * width, transcendentals=heads * seq * seq
        ),
        name="attend",
    )(info, q, k, v)


def join_body(plan, counts, info_ref, ctx_ref, gain_ref, next_ref, *refs):
    n_dp, n_tensor, chunks, seq, xor_far = plan
    w_refs, at = [], 0
    for n in counts:
        w_refs.append(refs[at : at + n])
        at += n
    hidden_ref, grad_refs = refs[at], refs[at + 1 : -5]
    turned_ref, joined_ref, square_ref, acc_ref, slope_ref = refs[-5:]
    rows, dout = joined_ref.shape
    me, group, length, votes = info_ref[0], info_ref[1], info_ref[2], info_ref[3]
    for m in range(n_tensor):
        turned_ref[m] = ctx_ref[me ^ m].T
    for c in range(0, dout, COLS):
        total = None
        for m in range(n_tensor):
            first = 0
            for ref in w_refs[m]:
                if first <= c < first + ref.shape[1]:
                    w = ref[:, c - first : c - first + COLS]
                first += ref.shape[1]
            part = dot(turned_ref[m], w, ((1,), (0,)))
            total = part if total is None else total + part
        joined_ref[:, c : c + COLS] = total
        sq = total * total
        lanes = sum(sq[:, i : i + 128] for i in range(0, COLS, 128))
        square_ref[...] = lanes if c == 0 else square_ref[...] + lanes
    acc_ref[...] = jnp.zeros_like(acc_ref)
    slice_w = dout // n_dp
    cw = slice_w // chunks
    near, far = group % NEAR, group // NEAR
    n_far = n_dp // NEAR

    def body(r, carry):
        loss, weights = carry
        at = pl.ds(pl.multiple_of(r * ROWS, ROWS), ROWS)
        inv = lax.rsqrt(jnp.sum(square_ref[at, :], axis=1, keepdims=True) * (1.0 / dout) + 1e-06)
        pos = (me * rows + r * ROWS) % seq + lax.broadcasted_iota(jnp.int32, (ROWS, 1), 0)
        weight = jnp.where(pos < length - 1, votes.astype(F32), 0.0)
        scaled = weight * (loss_scale * 2.0 / dout)
        miss = jnp.zeros((ROWS, 128), F32)
        lean = jnp.zeros((ROWS, 128), F32)
        for c in range(0, dout, 512):
            cs = slice(c, c + 512)
            normed = joined_ref[at, cs] * inv
            gain = gain_ref[:, cs]
            predicted = normed * gain
            hidden_ref[at, cs] = predicted.astype(BF)
            misfit = predicted - next_ref[at, cs].astype(F32)
            grad = scaled * misfit
            slope = grad * gain
            acc_ref[:, cs] += grad * normed
            slope_ref[:, cs] = slope
            sq = misfit * misfit
            ln = slope * normed
            miss += sum(sq[:, i : i + 128] for i in range(0, 512, 128))
            lean += sum(ln[:, i : i + 128] for i in range(0, 512, 128))
            joined_ref[at, cs] = normed
        lean = jnp.sum(lean, axis=1, keepdims=True) * (1.0 / dout)

        def gradient_at(cs):
            return (inv * (slope_ref[:, cs] - joined_ref[at, cs] * lean)).astype(BF)

        for j in range(chunks):
            for q in range(NEAR):
                for b in range(n_far):
                    to = slice(b * cw, (b + 1) * cw)
                    if cw % 128 == 0:
                        other = (far ^ b if xor_far else b) * NEAR + (near ^ q)
                        start = pl.multiple_of(other * slice_w + j * cw, 128)
                        grad_refs[j * NEAR + q][at, to] = gradient_at(pl.ds(start, cw))
                    else:
                        start = (b * NEAR + q) * slice_w + j * cw
                        grad_refs[j][near ^ q, at, to] = gradient_at(slice(start, start + cw))
        loss = loss + weight * (jnp.sum(miss, axis=1, keepdims=True) * (1.0 / dout))
        return loss, weights + weight

    zero = jnp.zeros((ROWS, 1), F32)
    loss, weights = lax.fori_loop(0, rows // ROWS, body, (zero, zero))
    wide = n_far * cw
    gain_sum = jnp.sum(acc_ref[...], axis=0, keepdims=True)
    gain_sum = jnp.concatenate([gain_sum[:, i : i + wide] for i in range(0, dout, wide)], 0)
    lane = lax.broadcasted_iota(jnp.int32, (1, wide), 1)
    loss = jnp.sum(loss, axis=0, keepdims=True)
    weights = jnp.sum(weights, axis=0, keepdims=True)
    scalars = jnp.where(lane == 0, loss, jnp.where(lane == 1, weights, 0.0))
    words = [*split_words(gain_sum), *split_words(scalars)]
    left = STAT_ROWS - sum(w.shape[0] for w in words)
    words = jnp.concatenate([*words, jnp.zeros((left, wide), F32)], 0).astype(BF)
    if cw % 128 == 0:
        for q in range(NEAR):
            grad_refs[q][rows:, :] = words
    else:
        for q in range(NEAR):
            grad_refs[0][q, rows:, :] = words


def join(plan, info, ctx, gain, next_hidden, weights):
    n_dp, n_tensor, chunks, _, _ = plan
    _, width, rows = ctx.shape
    dout = gain.shape[1]
    wide = dout // NEAR // chunks
    tall = [rows + STAT_ROWS] + [rows] * (chunks - 1)
    aligned = dout // n_dp // chunks % 128 == 0
    if aligned:
        grads = [shape((n, wide)) for n in tall for _ in range(NEAR)]
    else:
        grads = [shape((NEAR, n, wide)) for n in tall]
    out = pl.pallas_call(
        functools.partial(join_body, plan, [len(w) for w in weights]),
        in_specs=[SM] + [VM] * (3 + sum(len(w) for w in weights)),
        out_specs=[VM] * (1 + len(grads)),
        out_shape=[shape((rows, dout)), *grads],
        scratch_shapes=[
            pltpu.VMEM((n_tensor, rows, width), BF),
            pltpu.VMEM((rows, dout), F32),
            pltpu.VMEM((rows, 128), F32),
            pltpu.VMEM((ROWS, dout), F32),
            pltpu.VMEM((ROWS, dout), F32),
        ],
        compiler_params=params(),
        cost_estimate=pl.CostEstimate(
            flops=2 * rows * dout * width * n_tensor,
            bytes_accessed=2 * dout * (width * n_tensor + 3 * rows),
            transcendentals=rows,
        ),
        name="join",
    )(info, ctx, gain, next_hidden, *[w for held in weights for w in held])
    if aligned:
        return out[0], [out[1 + j * NEAR : 1 + (j + 1) * NEAR] for j in range(chunks)]
    return out[0], [[g[q] for q in range(NEAR)] for g in out[1:]]


def stat_sizes(dout, wide, cw):
    in_block = dout // cw
    return dout // wide, in_block, -(-(2 * in_block + 2) // 16) * 16


def block_words(gains, scalars, tall, cw):
    words = [*split_words(gains), *split_words(scalars)]
    left = tall - sum(w.shape[0] for w in words)
    return jnp.concatenate([*words, jnp.zeros((left, cw), F32)], 0).astype(BF)


def block_sums(words, n):
    words = words.astype(F32)
    return words[:n] + words[n : 2 * n], words[2 * n : 2 * n + 1] + words[2 * n + 1 : 2 * n + 2]


def grad_body(plan, dout, info_ref, *refs):
    n_dp, n_tensor, _, _, xor_far = plan
    ctx_refs, g_refs, (keep_ref, send_ref) = refs[: NEAR + 1], refs[NEAR + 1 : -2], refs[-2:]
    n_y, n_far, tall, cw = keep_ref.shape
    feats, rows = ctx_refs[0].shape[1:]
    wide = n_far * cw
    me = info_ref[0]
    core, y = me % 2, me // 2
    if tall > feats:
        in_piece, in_block, stat_rows = stat_sizes(dout, wide, cw)
        sums = sum(ref[rows:, :].astype(F32) for ref in g_refs)
        gains, scalars = block_sums(sums, in_piece)
        gains = jnp.concatenate([gains[:, b * cw : (b + 1) * cw] for b in range(n_far)], 0)
        words = block_words(gains, scalars[:, :cw], stat_rows, cw)
    for s, ref in ((1, send_ref), (0, keep_ref)):
        for a in range(n_y):
            m = (y ^ a if xor_far else a) * 2 + (core ^ s)
            total = sum(dot(c[m], g[:rows, :], ((1,), (0,))) for c, g in zip(ctx_refs[:-2], g_refs))
            last = [dot(c[m], g_refs[-1][:rows, :], ((1,), (0,))) for c in ctx_refs[-2:]]
            total = (total + jnp.concatenate(last, 0)).astype(BF)
            for b in range(n_far):
                ref[a, b, :feats, :] = total[:, b * cw : (b + 1) * cw]
                if tall > feats:
                    ref[a, b, feats:, :] = words


def gradient(plan, dout, info, ctxs, grads):
    n_dp, n_tensor, chunks, _, _ = plan
    _, feats, rows = ctxs[0].shape
    wide = grads[0].shape[1]
    cw = dout // n_dp // chunks
    tall = feats
    if grads[0].shape[0] > rows:
        tall += stat_sizes(dout, wide, cw)[2]
    block = shape((n_tensor // 2, n_dp // NEAR, tall, cw))
    return pl.pallas_call(
        functools.partial(grad_body, plan, dout),
        in_specs=[SM] + [VM] * (2 * NEAR + 1),
        out_specs=[VM, VM],
        out_shape=[block, block],
        compiler_params=params(),
        cost_estimate=pl.CostEstimate(
            flops=2 * NEAR * n_tensor * rows * feats * wide,
            bytes_accessed=2 * (NEAR * rows * (n_tensor * feats + wide) + n_tensor * feats * wide),
            transcendentals=0,
        ),
        name="gradient",
    )(info, *ctxs, *grads)


def merge_body(in_block, feats, keep_ref, got_ref, *out_refs):
    n_y, n_far, tall, cw = keep_ref.shape
    if tall > feats:
        gains, scalars = block_sums(keep_ref[0, 0, feats:, :], in_block)
        more, others = block_sums(got_ref[0, 0, feats:, :], in_block)
        words = block_words(gains + more, scalars + others, tall - feats, cw)
    for i in range(n_y * n_far):
        a, b = divmod(i, n_far)
        total = keep_ref[a, b, :feats, :].astype(F32) + got_ref[a, b, :feats, :].astype(F32)
        ref, at = (out_refs[0], (a, b)) if len(out_refs) == 1 else (out_refs[i], (0, 0))
        ref[(*at, slice(0, feats), slice(None))] = total.astype(BF)
        if tall > feats:
            ref[(*at, slice(feats, tall), slice(None))] = words


def merge(plan, dout, feats, keep, got):
    n_y, n_far, tall, cw = keep.shape
    if plan[4]:
        outs = [shape((1, 1, tall, cw))] * (n_y * n_far)
    else:
        outs = [shape(keep.shape)]
    return pl.pallas_call(
        functools.partial(merge_body, dout // cw, feats),
        in_specs=[VM, VM],
        out_specs=[VM] * len(outs),
        out_shape=outs,
        compiler_params=params(),
        cost_estimate=pl.CostEstimate(flops=keep.size, bytes_accessed=6 * keep.size, transcendentals=0),
        name="merge",
    )(keep, got)


def finish_body(counts, in_piece, n_far, *refs):
    grad_ref, gain_ref, loss_ref = refs[-3:]
    feats = grad_ref.shape[0]
    chunks, at = [], 0
    for n in counts:
        chunks.append(refs[at : at + n])
        at += n
    tall, cw = chunks[0][0].shape[2:]

    def total(blocks, rows):
        parts = [
            r[a, b, rows, :].astype(F32) for r in blocks for a in range(r.shape[0]) for b in range(r.shape[1])
        ]
        return sum(parts[1:], parts[0])

    gains, scalars = block_sums(total(chunks[0], slice(feats, tall)), in_piece * n_far)
    lane = lax.broadcasted_iota(jnp.int32, (1, cw), 1)
    weight = jnp.sum(jnp.where(lane == 1, scalars, 0.0), axis=1, keepdims=True)
    loss_ref[0, 0] = jnp.sum(jnp.where(lane == 0, scalars / weight, 0.0))
    gains = gains / weight
    for r in range(in_piece):
        for b in range(n_far):
            gain_ref[pl.ds(r * n_far + b, 1), :] = gains[b * in_piece + r : b * in_piece + r + 1, :]
    for j, blocks in enumerate(chunks):
        grad_ref[:, j * cw : (j + 1) * cw] = (total(blocks, slice(0, feats)) / weight).astype(BF)


def finish(plan, dout, feats, chunks):
    n_dp = plan[0]
    cw = chunks[0][0].shape[3]
    n_far = n_dp // NEAR
    return pl.pallas_call(
        functools.partial(finish_body, [len(c) for c in chunks], dout // (n_far * cw), n_far),
        in_specs=[VM] * sum(len(c) for c in chunks),
        out_specs=[VM, VM, SM],
        out_shape=[shape((feats, dout // n_dp)), shape((dout // cw, cw), F32), shape((1, 1), F32)],
        compiler_params=params(),
        name="finish",
    )(*[b for c in chunks for b in c])


def swap(x, axis, n, mask):
    return lax.ppermute(x, axis, [(i, i ^ mask) for i in range(n)])


def swap_far(x, n_dp, n_tensor, a, b):
    mask = b * NEAR * n_tensor + a * 2
    return lax.ppermute(x, ("dp", "tensor"), [(i, i ^ mask) for i in range(n_dp * n_tensor)])


def exchange_far(plan, blocks):
    n_dp, n_tensor, _, _, xor_far = plan
    n_far = n_dp // NEAR
    if xor_far:
        return [blocks[0]] + [
            swap_far(block, n_dp, n_tensor, *divmod(i, n_far)) for i, block in enumerate(blocks) if i
        ]
    cores = [[2 * y + c for y in range(n_tensor // 2)] for c in range(2)]
    nears = [[NEAR * f + q for f in range(n_far)] for q in range(NEAR)]
    x = lax.all_to_all(blocks[0], "tensor", 0, 0, tiled=True, axis_index_groups=cores)
    return [lax.all_to_all(x, "dp", 1, 1, tiled=True, axis_index_groups=nears)]


def on_device(
    n_dp,
    n_tensor,
    query_states,
    key_states,
    value_states,
    joining_weight,
    norm_gain,
    next_hidden,
    lengths,
    vote_counts,
):
    _, tokens, width = query_states.shape
    seq = tokens // lengths.shape[0]
    dout = norm_gain.shape[0]
    rows = next_hidden.shape[0]
    chunks = 2 if dout // n_dp >= 256 else 1
    xor_far = (n_tensor // 2) * (n_dp // NEAR) <= 4
    plan = (n_dp, n_tensor, chunks, seq, xor_far)
    me = lax.axis_index("tensor").astype(jnp.int32)
    group = lax.axis_index("dp").astype(jnp.int32)
    info = jnp.stack([me, group, lengths[0], vote_counts[0]])

    weight = joining_weight[0]
    half = n_tensor // 2
    cut = dout // 2
    first, second = weight[:, :cut], weight[:, cut:]
    first = swap(first, "tensor", n_tensor, half)
    beside = swap(weight, "tensor", n_tensor, 1)
    context = attend(info, query_states[0], key_states[0], value_states[0], rows)
    first, beside, context = lax.optimization_barrier((first, beside, context))
    ctx = lax.all_to_all(context, "tensor", 0, 0, tiled=True)
    across = swap(first, "tensor", n_tensor, 1)
    across, second, ctx = lax.optimization_barrier((across, second, ctx))
    second = swap(second, "tensor", n_tensor, half)
    beside_x, beside_z = (swap(ctx, "dp", n_dp, q) for q in (1, 2))
    second, beside_x, beside_z = lax.optimization_barrier((second, beside_x, beside_z))
    diagonal = [swap(beside_x[:, : width // 2], "dp", n_dp, 2), swap(beside_z[:, width // 2 :], "dp", n_dp, 1)]
    ctxs = [ctx, beside_x, beside_z, *diagonal]
    held = {0: [weight], 1: [beside], half: [first, second]}
    held[half + 1] = [across, swap(second, "tensor", n_tensor, 1)]
    bit = half // 2
    while bit > 1:
        held.update({m ^ bit: [swap(p, "tensor", n_tensor, bit) for p in w] for m, w in list(held.items())})
        bit //= 2
    weights = [held[m] for m in range(n_tensor)]

    hidden, grads = join(plan, info, ctx, norm_gain[None, :], next_hidden, weights)
    parts = []
    for j in range(chunks):
        near = [grads[j][0]] + [swap(grads[j][q], "dp", n_dp, q) for q in range(1, NEAR)]
        keep, send = gradient(plan, dout, info, ctxs, near)
        blocks = merge(plan, dout, width, keep, swap(send, "tensor", n_tensor, 1))
        parts.append(exchange_far(plan, blocks))
    weight_grad, gain_grad, loss = finish(plan, dout, width, parts)
    return (hidden, weight_grad[None], gain_grad.reshape(dout), loss.reshape(()))


def solution(mesh):
    return jax.shard_map(
        functools.partial(on_device, mesh.shape["dp"], mesh.shape["tensor"]),
        mesh=mesh,
        in_specs=(
            P(None, "dp", "tensor"),
            P(None, "dp", "tensor"),
            P(None, "dp", "tensor"),
            P(None, "tensor", None),
            P(),
            P(("dp", "tensor"), None),
            P("dp"),
            P("dp"),
        ),
        out_specs=(P(("dp", "tensor"), None), P(None, "tensor", "dp"), P(), P()),
        check_vma=False,
    )
```

```python
import functools
import math

import jax
import jax.numpy as jnp
from jax import lax
from jax.experimental import pallas as pl
from jax.experimental.pallas import tpu as pltpu
from jax.sharding import PartitionSpec as P

HD = 128
QB = 128
ROWS = 128
COLS = 256
NEAR = 4
STAT_ROWS = 32

loss_scale = 65536.0
neg_large = -1e30
MIB = 1 << 20
BF = jnp.bfloat16
F32 = jnp.float32


def dot(a, b, dims):
    return lax.dot_general(a, b, (dims, ((), ())), preferred_element_type=F32)


def split_words(x):
    high = x.astype(BF).astype(F32)
    return high, (x - high).astype(BF).astype(F32)


def shape(dims, dtype=BF):
    return jax.ShapeDtypeStruct(dims, dtype)


def params():
    return pltpu.CompilerParams(vmem_limit_bytes=48 * MIB)


VM = pl.BlockSpec(memory_space=pltpu.VMEM)
SM = pl.BlockSpec(memory_space=pltpu.SMEM)


def attend_body(info_ref, q_ref, k_ref, v_ref, o_ref):
    seq = q_ref.shape[0]
    rows = o_ref.shape[2]
    rate = math.log2(math.e) / math.sqrt(HD)
    length = info_ref[2]
    key = lax.broadcasted_iota(jnp.int32, (seq, 1), 0)
    hide = jnp.where(key < length, 0.0, neg_large)
    r = lax.broadcasted_iota(jnp.int32, (QB, QB), 0)
    c = lax.broadcasted_iota(jnp.int32, (QB, QB), 1)
    for h in range(q_ref.shape[1] // HD):
        at = slice(h * HD, (h + 1) * HD)
        q_t, v_t = q_ref[:, at].T, v_ref[:, at].T
        for i in range(seq // QB):
            keys = (i + 1) * QB
            scores = dot(k_ref[:keys, at], q_t[:, i * QB : keys], ((1,), (0,))) + hide[:keys]
            last = jnp.where(r <= c, scores[keys - QB :], neg_large)
            scores = last if i == 0 else jnp.concatenate([scores[: keys - QB], last], 0)
            peak = jnp.max(scores, axis=0, keepdims=True)
            e = jnp.exp2((scores - peak) * rate)
            total = jnp.sum(e, axis=0, keepdims=True)
            out = (dot(v_t[:, :keys], e.astype(BF), ((1,), (0,))) / total).astype(BF)
            for n in range(0, QB, min(rows, QB)):
                block, first = divmod(i * QB + n, rows)
                o_ref[block, at, first : first + min(rows, QB)] = out[:, n : n + rows]


def attend(info, q, k, v, rows):
    seq, width = q.shape
    heads = width // HD
    block = VM
    return pl.pallas_call(
        attend_body,
                in_specs=[SM, block, block, block],
        out_specs=VM,
        out_shape=shape((seq // rows, width, rows)),
        compiler_params=params(),
        cost_estimate=pl.CostEstimate(
            flops=4 * seq * seq * width, bytes_accessed=8 * seq * width, transcendentals=heads * seq * seq
        ),
        name="attend",
    )(info, q, k, v)


def join_body(plan, counts, info_ref, ctx_ref, gain_ref, next_ref, *refs):
    n_dp, n_tensor, chunks, seq, xor_far = plan
    w_refs, at = [], 0
    for n in counts:
        w_refs.append(refs[at : at + n])
        at += n
    hidden_ref, grad_refs = refs[at], refs[at + 1 : -5]
    turned_ref, joined_ref, square_ref, acc_ref, slope_ref = refs[-5:]
    rows, dout = joined_ref.shape
    me, group, length, votes = info_ref[0], info_ref[1], info_ref[2], info_ref[3]
    for m in range(n_tensor):
        turned_ref[m] = ctx_ref[me ^ m].T
    near, far = group % NEAR, group // NEAR
    columns = [(c, 0, c) for c in range(0, dout, COLS)]
    if xor_far:
        cut, spare = w_refs[-1][0].shape[1], w_refs[-1][2].shape[1]
        own, other = near % 2 * cut, (1 - near % 2) * cut
        columns = [(pl.multiple_of(own + c, COLS), 0, c) for c in range(0, cut, COLS)]
        columns += [(pl.multiple_of(other + c, COLS), 1, c) for c in range(0, cut, COLS)]
        columns += [(2 * cut + c, 2, c) for c in range(0, spare, COLS)]
    for step, (start, piece, first) in enumerate(columns):
        to = pl.ds(start, COLS)
        total = None
        for m in range(n_tensor):
            whole = len(w_refs[m]) == 1
            w = w_refs[m][0][:, to] if whole else w_refs[m][piece][:, first : first + COLS]
            part = dot(turned_ref[m], w, ((1,), (0,)))
            total = part if total is None else total + part
        joined_ref[:, to] = total
        sq = total * total
        lanes = sum(sq[:, i : i + 128] for i in range(0, COLS, 128))
        square_ref[...] = lanes if step == 0 else square_ref[...] + lanes
    acc_ref[...] = jnp.zeros_like(acc_ref)
    slice_w = dout // n_dp
    cw = slice_w // chunks
    n_far = n_dp // NEAR

    def body(r, carry):
        loss, weights = carry
        at = pl.ds(pl.multiple_of(r * ROWS, ROWS), ROWS)
        inv = lax.rsqrt(jnp.sum(square_ref[at, :], axis=1, keepdims=True) * (1.0 / dout) + 1e-06)
        pos = (me * rows + r * ROWS) % seq + lax.broadcasted_iota(jnp.int32, (ROWS, 1), 0)
        weight = jnp.where(pos < length - 1, votes.astype(F32), 0.0)
        scaled = weight * (loss_scale * 2.0 / dout)
        miss = jnp.zeros((ROWS, 128), F32)
        lean = jnp.zeros((ROWS, 128), F32)
        for c in range(0, dout, 512):
            cs = slice(c, c + 512)
            normed = joined_ref[at, cs] * inv
            gain = gain_ref[:, cs]
            predicted = normed * gain
            hidden_ref[at, cs] = predicted.astype(BF)
            misfit = predicted - next_ref[at, cs].astype(F32)
            grad = scaled * misfit
            slope = grad * gain
            acc_ref[:, cs] += grad * normed
            slope_ref[:, cs] = slope
            sq = misfit * misfit
            ln = slope * normed
            miss += sum(sq[:, i : i + 128] for i in range(0, 512, 128))
            lean += sum(ln[:, i : i + 128] for i in range(0, 512, 128))
            joined_ref[at, cs] = normed
        lean = jnp.sum(lean, axis=1, keepdims=True) * (1.0 / dout)

        def gradient_at(cs):
            return (inv * (slope_ref[:, cs] - joined_ref[at, cs] * lean)).astype(BF)

        for j in range(chunks):
            for q in range(NEAR):
                for b in range(n_far):
                    to = slice(b * cw, (b + 1) * cw)
                    if cw % 128 == 0:
                        other = (far ^ b if xor_far else b) * NEAR + (near ^ q)
                        start = pl.multiple_of(other * slice_w + j * cw, 128)
                        grad_refs[j * NEAR + q][at, to] = gradient_at(pl.ds(start, cw))
                    else:
                        start = (b * NEAR + q) * slice_w + j * cw
                        grad_refs[j][near ^ q, at, to] = gradient_at(slice(start, start + cw))
        loss = loss + weight * (jnp.sum(miss, axis=1, keepdims=True) * (1.0 / dout))
        return loss, weights + weight

    zero = jnp.zeros((ROWS, 1), F32)
    loss, weights = lax.fori_loop(0, rows // ROWS, body, (zero, zero))
    wide = n_far * cw
    gain_sum = jnp.sum(acc_ref[...], axis=0, keepdims=True)
    gain_sum = jnp.concatenate([gain_sum[:, i : i + wide] for i in range(0, dout, wide)], 0)
    lane = lax.broadcasted_iota(jnp.int32, (1, wide), 1)
    loss = jnp.sum(loss, axis=0, keepdims=True)
    weights = jnp.sum(weights, axis=0, keepdims=True)
    scalars = jnp.where(lane == 0, loss, jnp.where(lane == 1, weights, 0.0))
    words = [*split_words(gain_sum), *split_words(scalars)]
    left = STAT_ROWS - sum(w.shape[0] for w in words)
    words = jnp.concatenate([*words, jnp.zeros((left, wide), F32)], 0).astype(BF)
    if cw % 128 == 0:
        for q in range(NEAR):
            grad_refs[q][rows:, :] = words
    else:
        for q in range(NEAR):
            grad_refs[0][q, rows:, :] = words


def join(plan, info, ctx, gain, next_hidden, weights):
    n_dp, n_tensor, chunks, _, _ = plan
    _, width, rows = ctx.shape
    dout = gain.shape[1]
    wide = dout // NEAR // chunks
    tall = [rows + STAT_ROWS] + [rows] * (chunks - 1)
    aligned = dout // n_dp // chunks % 128 == 0
    if aligned:
        grads = [shape((n, wide)) for n in tall for _ in range(NEAR)]
    else:
        grads = [shape((NEAR, n, wide)) for n in tall]
    out = pl.pallas_call(
        functools.partial(join_body, plan, [len(w) for w in weights]),
        in_specs=[SM] + [VM] * (3 + sum(len(w) for w in weights)),
        out_specs=[VM] * (1 + len(grads)),
        out_shape=[shape((rows, dout)), *grads],
        scratch_shapes=[
            pltpu.VMEM((n_tensor, rows, width), BF),
            pltpu.VMEM((rows, dout), F32),
            pltpu.VMEM((rows, 128), F32),
            pltpu.VMEM((ROWS, dout), F32),
            pltpu.VMEM((ROWS, dout), F32),
        ],
        compiler_params=params(),
        cost_estimate=pl.CostEstimate(
            flops=2 * rows * dout * width * n_tensor,
            bytes_accessed=2 * dout * (width * n_tensor + 3 * rows),
            transcendentals=rows,
        ),
        name="join",
    )(info, ctx, gain, next_hidden, *[w for held in weights for w in held])
    if aligned:
        return out[0], [out[1 + j * NEAR : 1 + (j + 1) * NEAR] for j in range(chunks)]
    return out[0], [[g[q] for q in range(NEAR)] for g in out[1:]]


def stat_sizes(dout, wide, cw):
    in_block = dout // cw
    return dout // wide, in_block, -(-(2 * in_block + 2) // 16) * 16


def block_words(gains, scalars, tall, cw):
    words = [*split_words(gains), *split_words(scalars)]
    left = tall - sum(w.shape[0] for w in words)
    return jnp.concatenate([*words, jnp.zeros((left, cw), F32)], 0).astype(BF)


def block_sums(words, n):
    words = words.astype(F32)
    return words[:n] + words[n : 2 * n], words[2 * n : 2 * n + 1] + words[2 * n + 1 : 2 * n + 2]


def grad_body(plan, dout, counts, info_ref, *refs):
    n_dp, n_tensor, _, _, xor_far = plan
    keep_ref, send_ref = refs[-2:]
    ctx_refs, at = [], 0
    for n in counts:
        ctx_refs.append(refs[at : at + n])
        at += n
    g_refs = refs[at:-2]
    n_y, n_far, tall, cw = keep_ref.shape
    feats, rows = ctx_refs[0][0].shape[1:]
    wide = n_far * cw
    me = info_ref[0]
    core, y = me % 2, me // 2
    if tall > feats:
        in_piece, in_block, stat_rows = stat_sizes(dout, wide, cw)
        sums = sum(ref[rows:, :].astype(F32) for ref in g_refs)
        gains, scalars = block_sums(sums, in_piece)
        gains = jnp.concatenate([gains[:, b * cw : (b + 1) * cw] for b in range(n_far)], 0)
        words = block_words(gains, scalars[:, :cw], stat_rows, cw)
    for s, ref in ((1, send_ref), (0, keep_ref)):
        for a in range(n_y):
            m = (y ^ a if xor_far else a) * 2 + (core ^ s)
            total = None
            for parts, g in zip(ctx_refs, g_refs):
                c = jnp.concatenate([part[m] for part in parts], 0) if len(parts) > 1 else parts[0][m]
                part = dot(c, g[:rows, :], ((1,), (0,)))
                total = part if total is None else total + part
            total = total.astype(BF)
            for b in range(n_far):
                ref[a, b, :feats, :] = total[:, b * cw : (b + 1) * cw]
                if tall > feats:
                    ref[a, b, feats:, :] = words


def gradient(plan, dout, info, ctxs, grads):
    n_dp, n_tensor, chunks, _, _ = plan
    _, feats, rows = ctxs[0][0].shape
    wide = grads[0].shape[1]
    cw = dout // n_dp // chunks
    tall = feats
    if grads[0].shape[0] > rows:
        tall += stat_sizes(dout, wide, cw)[2]
    block = shape((n_tensor // 2, n_dp // NEAR, tall, cw))
    return pl.pallas_call(
        functools.partial(grad_body, plan, dout, [len(c) for c in ctxs]),
        in_specs=[SM] + [VM] * (NEAR + sum(len(c) for c in ctxs)),
        out_specs=[VM, VM],
        out_shape=[block, block],
        compiler_params=params(),
        cost_estimate=pl.CostEstimate(
            flops=2 * NEAR * n_tensor * rows * feats * wide,
            bytes_accessed=2 * (NEAR * rows * (n_tensor * feats + wide) + n_tensor * feats * wide),
            transcendentals=0,
        ),
        name="gradient",
    )(info, *[part for parts in ctxs for part in parts], *grads)


def merge_body(in_block, feats, keep_ref, got_ref, *out_refs):
    n_y, n_far, tall, cw = keep_ref.shape
    if tall > feats:
        gains, scalars = block_sums(keep_ref[0, 0, feats:, :], in_block)
        more, others = block_sums(got_ref[0, 0, feats:, :], in_block)
        words = block_words(gains + more, scalars + others, tall - feats, cw)
    for i in range(n_y * n_far):
        a, b = divmod(i, n_far)
        total = keep_ref[a, b, :feats, :].astype(F32) + got_ref[a, b, :feats, :].astype(F32)
        ref, at = (out_refs[0], (a, b)) if len(out_refs) == 1 else (out_refs[i], (0, 0))
        ref[(*at, slice(0, feats), slice(None))] = total.astype(BF)
        if tall > feats:
            ref[(*at, slice(feats, tall), slice(None))] = words


def merge(plan, dout, feats, keep, got):
    n_y, n_far, tall, cw = keep.shape
    if plan[4]:
        outs = [shape((1, 1, tall, cw))] * (n_y * n_far)
    else:
        outs = [shape(keep.shape)]
    return pl.pallas_call(
        functools.partial(merge_body, dout // cw, feats),
        in_specs=[VM, VM],
        out_specs=[VM] * len(outs),
        out_shape=outs,
        compiler_params=params(),
        cost_estimate=pl.CostEstimate(flops=keep.size, bytes_accessed=6 * keep.size, transcendentals=0),
        name="merge",
    )(keep, got)


def finish_body(counts, in_piece, n_far, *refs):
    grad_ref, gain_ref, loss_ref = refs[-3:]
    feats = grad_ref.shape[0]
    chunks, at = [], 0
    for n in counts:
        chunks.append(refs[at : at + n])
        at += n
    tall, cw = chunks[0][0].shape[2:]

    def total(blocks, rows):
        parts = [
            r[a, b, rows, :].astype(F32) for r in blocks for a in range(r.shape[0]) for b in range(r.shape[1])
        ]
        return sum(parts[1:], parts[0])

    gains, scalars = block_sums(total(chunks[0], slice(feats, tall)), in_piece * n_far)
    lane = lax.broadcasted_iota(jnp.int32, (1, cw), 1)
    weight = jnp.sum(jnp.where(lane == 1, scalars, 0.0), axis=1, keepdims=True)
    loss_ref[0, 0] = jnp.sum(jnp.where(lane == 0, scalars / weight, 0.0))
    gains = gains / weight
    for r in range(in_piece):
        for b in range(n_far):
            gain_ref[pl.ds(r * n_far + b, 1), :] = gains[b * in_piece + r : b * in_piece + r + 1, :]
    for j, blocks in enumerate(chunks):
        grad_ref[:, j * cw : (j + 1) * cw] = (total(blocks, slice(0, feats)) / weight).astype(BF)


def finish(plan, dout, feats, chunks):
    n_dp = plan[0]
    cw = chunks[0][0].shape[3]
    n_far = n_dp // NEAR
    return pl.pallas_call(
        functools.partial(finish_body, [len(c) for c in chunks], dout // (n_far * cw), n_far),
        in_specs=[VM] * sum(len(c) for c in chunks),
        out_specs=[VM, VM, SM],
        out_shape=[shape((feats, dout // n_dp)), shape((dout // cw, cw), F32), shape((1, 1), F32)],
        compiler_params=params(),
        name="finish",
    )(*[b for c in chunks for b in c])


def swap(x, axis, n, mask):
    return lax.ppermute(x, axis, [(i, i ^ mask) for i in range(n)])


def swap_far(x, n_dp, n_tensor, a, b):
    mask = b * NEAR * n_tensor + a * 2
    return lax.ppermute(x, ("dp", "tensor"), [(i, i ^ mask) for i in range(n_dp * n_tensor)])


def exchange_far(plan, blocks):
    n_dp, n_tensor, _, _, xor_far = plan
    n_far = n_dp // NEAR
    if xor_far:
        return [blocks[0]] + [
            swap_far(block, n_dp, n_tensor, *divmod(i, n_far)) for i, block in enumerate(blocks) if i
        ]
    cores = [[2 * y + c for y in range(n_tensor // 2)] for c in range(2)]
    nears = [[NEAR * f + q for f in range(n_far)] for q in range(NEAR)]
    x = lax.all_to_all(blocks[0], "tensor", 0, 0, tiled=True, axis_index_groups=cores)
    return [lax.all_to_all(x, "dp", 1, 1, tiled=True, axis_index_groups=nears)]


def gather_large(n_dp, n_tensor, _, weight, context):
    ctx = lax.all_to_all(context, "tensor", 0, 0, tiled=True)
    held = {0: weight}
    bit = n_tensor // 2
    while bit:
        held.update({m | bit: swap(w, "tensor", n_tensor, bit) for m, w in list(held.items())})
        bit //= 2
    ctxs = [[ctx]] + [[swap(ctx, "dp", n_dp, q)] for q in range(1, NEAR)]
    return ctx, ctxs, [[held[m]] for m in range(n_tensor)]


def gather_small(n_dp, n_tensor, side, weight, context):
    barrier = lax.optimization_barrier

    def dp(x, mask):
        return swap(x, "dp", n_dp, mask)

    def tensor(x, mask):
        return swap(x, "tensor", n_tensor, mask)

    dout = weight.shape[1]
    cut = dout * 3 // 8
    mine = tensor(lax.dynamic_slice_in_dim(weight, side * cut, cut, 1), 2)
    beside = tensor(weight, 1)
    rest = weight[:, 2 * cut :]
    mine, beside, context = barrier((mine, beside, context))
    other, mine_beside = dp(mine, 1), tensor(mine, 1)
    ctx = lax.all_to_all(context, "tensor", 0, 0, tiled=True)
    rest, other, mine_beside, ctx = barrier((rest, other, mine_beside, ctx))
    rest, other_beside = tensor(rest, 2), tensor(other, 1)
    half = ctx.shape[1] // 2
    low, high = ctx[:, :half], ctx[:, half:]
    low_x, high_z = dp(low, 1), dp(high, 2)
    rest, low_x, high_z = barrier((rest, low_x, high_z))
    ctxs = [[ctx], [low_x, dp(high, 1)], [dp(low, 2), high_z], [dp(low_x, 2), dp(high_z, 1)]]
    far = [mine, other, rest]
    return ctx, ctxs, [[weight], [beside], far, [mine_beside, other_beside, tensor(rest, 1)]]


def on_device(
    n_dp,
    n_tensor,
    query_states,
    key_states,
    value_states,
    joining_weight,
    norm_gain,
    next_hidden,
    lengths,
    vote_counts,
):
    _, tokens, width = query_states.shape
    seq = tokens // lengths.shape[0]
    dout = norm_gain.shape[0]
    rows = next_hidden.shape[0]
    chunks = 2 if dout // n_dp >= 256 else 1
    xor_far = (n_tensor // 2) * (n_dp // NEAR) <= 4
    plan = (n_dp, n_tensor, chunks, seq, xor_far)
    me = lax.axis_index("tensor").astype(jnp.int32)
    group = lax.axis_index("dp").astype(jnp.int32)
    info = jnp.stack([me, group, lengths[0], vote_counts[0]])

    attended = attend(info, query_states[0], key_states[0], value_states[0], rows)
    gather = gather_small if xor_far else gather_large
    ctx, ctxs, weights = gather(n_dp, n_tensor, group & 1, joining_weight[0], attended)
    hidden, grads = join(plan, info, ctx, norm_gain[None, :], next_hidden, weights)
    parts = []
    for j in range(chunks):
        near = [grads[j][0]] + [swap(grads[j][q], "dp", n_dp, q) for q in range(1, NEAR)]
        keep, send = gradient(plan, dout, info, ctxs, near)
        blocks = merge(plan, dout, width, keep, swap(send, "tensor", n_tensor, 1))
        parts.append(exchange_far(plan, blocks))
    weight_grad, gain_grad, loss = finish(plan, dout, width, parts)
    return (hidden, weight_grad[None], gain_grad.reshape(dout), loss.reshape(()))


def solution(mesh):
    return jax.shard_map(
        functools.partial(on_device, mesh.shape["dp"], mesh.shape["tensor"]),
        mesh=mesh,
        in_specs=(
            P(None, "dp", "tensor"),
            P(None, "dp", "tensor"),
            P(None, "dp", "tensor"),
            P(None, "tensor", None),
            P(),
            P(("dp", "tensor"), None),
            P("dp"),
            P("dp"),
        ),
        out_specs=(P(("dp", "tensor"), None), P(None, "tensor", "dp"), P(), P()),
        check_vma=False,
    )
```

```python
import functools
import math

import jax
import jax.numpy as jnp
from jax import lax
from jax.experimental import pallas as pl
from jax.experimental.pallas import tpu as pltpu
from jax.sharding import PartitionSpec as P

HD = 128
QB = 128
ROWS = 128
COLS = 256
NEAR = 4
STAT_ROWS = 32

loss_scale = 65536.0
neg_large = -1e30
MIB = 1 << 20
BF = jnp.bfloat16
F32 = jnp.float32


def dot(a, b, dims):
    return lax.dot_general(a, b, (dims, ((), ())), preferred_element_type=F32)


def split_words(x):
    high = x.astype(BF).astype(F32)
    return high, (x - high).astype(BF).astype(F32)


def shape(dims, dtype=BF):
    return jax.ShapeDtypeStruct(dims, dtype)


def params():
    return pltpu.CompilerParams(vmem_limit_bytes=48 * MIB)


VM = pl.BlockSpec(memory_space=pltpu.VMEM)
SM = pl.BlockSpec(memory_space=pltpu.SMEM)


def attend_body(info_ref, q_ref, k_ref, v_ref, o_ref):
    seq = q_ref.shape[0]
    rows = o_ref.shape[2]
    rate = math.log2(math.e) / math.sqrt(HD)
    length = info_ref[2]
    key = lax.broadcasted_iota(jnp.int32, (seq, 1), 0)
    hide = jnp.where(key < length, 0.0, neg_large)
    r = lax.broadcasted_iota(jnp.int32, (QB, QB), 0)
    c = lax.broadcasted_iota(jnp.int32, (QB, QB), 1)
    for h in range(q_ref.shape[1] // HD):
        at = slice(h * HD, (h + 1) * HD)
        q_t, v_t = q_ref[:, at].T, v_ref[:, at].T
        for i in range(seq // QB):
            keys = (i + 1) * QB
            scores = dot(k_ref[:keys, at], q_t[:, i * QB : keys], ((1,), (0,))) + hide[:keys]
            last = jnp.where(r <= c, scores[keys - QB :], neg_large)
            scores = last if i == 0 else jnp.concatenate([scores[: keys - QB], last], 0)
            peak = jnp.max(scores, axis=0, keepdims=True)
            e = jnp.exp2((scores - peak) * rate)
            total = jnp.sum(e, axis=0, keepdims=True)
            out = (dot(v_t[:, :keys], e.astype(BF), ((1,), (0,))) / total).astype(BF)
            for n in range(0, QB, min(rows, QB)):
                block, first = divmod(i * QB + n, rows)
                o_ref[block, at, first : first + min(rows, QB)] = out[:, n : n + rows]


def attend(info, q, k, v, rows):
    seq, width = q.shape
    heads = width // HD
    block = VM
    return pl.pallas_call(
        attend_body,
                in_specs=[SM, block, block, block],
        out_specs=VM,
        out_shape=shape((seq // rows, width, rows)),
        compiler_params=pltpu.CompilerParams(vmem_limit_bytes=60 * MIB),
        cost_estimate=pl.CostEstimate(
            flops=4 * seq * seq * width, bytes_accessed=8 * seq * width, transcendentals=heads * seq * seq
        ),
        name="attend",
    )(info, q, k, v)


def join_body(plan, counts, info_ref, ctx_ref, gain_ref, next_ref, *refs):
    n_dp, n_tensor, chunks, seq, xor_far = plan
    w_refs, at = [], 0
    for n in counts:
        w_refs.append(refs[at : at + n])
        at += n
    hidden_ref, grad_refs = refs[at], refs[at + 1 : -5]
    turned_ref, joined_ref, square_ref, acc_ref, slope_ref = refs[-5:]
    rows, dout = joined_ref.shape
    me, group, length, votes = info_ref[0], info_ref[1], info_ref[2], info_ref[3]
    for m in range(n_tensor):
        turned_ref[m] = ctx_ref[me ^ m].T
    near, far = group % NEAR, group // NEAR
    columns = [(c, 0, c) for c in range(0, dout, COLS)]
    if xor_far:
        cut, spare = w_refs[-1][0].shape[1], w_refs[-1][2].shape[1]
        own, other = near % 2 * cut, (1 - near % 2) * cut
        columns = [(pl.multiple_of(own + c, COLS), 0, c) for c in range(0, cut, COLS)]
        columns += [(pl.multiple_of(other + c, COLS), 1, c) for c in range(0, cut, COLS)]
        columns += [(2 * cut + c, 2, c) for c in range(0, spare, COLS)]
    for step, (start, piece, first) in enumerate(columns):
        to = pl.ds(start, COLS)
        total = None
        for m in range(n_tensor):
            whole = len(w_refs[m]) == 1
            w = w_refs[m][0][:, to] if whole else w_refs[m][piece][:, first : first + COLS]
            part = dot(turned_ref[m], w, ((1,), (0,)))
            total = part if total is None else total + part
        joined_ref[:, to] = total
        sq = total * total
        lanes = sum(sq[:, i : i + 128] for i in range(0, COLS, 128))
        square_ref[...] = lanes if step == 0 else square_ref[...] + lanes
    acc_ref[...] = jnp.zeros_like(acc_ref)
    slice_w = dout // n_dp
    cw = slice_w // chunks
    n_far = n_dp // NEAR

    def body(r, carry):
        loss, weights = carry
        at = pl.ds(pl.multiple_of(r * ROWS, ROWS), ROWS)
        inv = lax.rsqrt(jnp.sum(square_ref[at, :], axis=1, keepdims=True) * (1.0 / dout) + 1e-06)
        pos = (me * rows + r * ROWS) % seq + lax.broadcasted_iota(jnp.int32, (ROWS, 1), 0)
        weight = jnp.where(pos < length - 1, votes.astype(F32), 0.0)
        scaled = weight * (loss_scale * 2.0 / dout)
        miss = jnp.zeros((ROWS, 128), F32)
        lean = jnp.zeros((ROWS, 128), F32)
        for c in range(0, dout, 512):
            cs = slice(c, c + 512)
            normed = joined_ref[at, cs] * inv
            gain = gain_ref[:, cs]
            predicted = normed * gain
            hidden_ref[at, cs] = predicted.astype(BF)
            misfit = predicted - next_ref[at, cs].astype(F32)
            grad = scaled * misfit
            slope = grad * gain
            acc_ref[:, cs] += grad * normed
            slope_ref[:, cs] = slope
            sq = misfit * misfit
            ln = slope * normed
            miss += sum(sq[:, i : i + 128] for i in range(0, 512, 128))
            lean += sum(ln[:, i : i + 128] for i in range(0, 512, 128))
            joined_ref[at, cs] = normed
        lean = jnp.sum(lean, axis=1, keepdims=True) * (1.0 / dout)

        def gradient_at(cs):
            return (inv * (slope_ref[:, cs] - joined_ref[at, cs] * lean)).astype(BF)

        for j in range(chunks):
            for q in range(NEAR):
                for b in range(n_far):
                    to = slice(b * cw, (b + 1) * cw)
                    if cw % 128 == 0:
                        other = (far ^ b if xor_far else b) * NEAR + (near ^ q)
                        start = pl.multiple_of(other * slice_w + j * cw, 128)
                        grad_refs[j * NEAR + q][at, to] = gradient_at(pl.ds(start, cw))
                    else:
                        start = (b * NEAR + q) * slice_w + j * cw
                        grad_refs[j][near ^ q, at, to] = gradient_at(slice(start, start + cw))
        loss = loss + weight * (jnp.sum(miss, axis=1, keepdims=True) * (1.0 / dout))
        return loss, weights + weight

    zero = jnp.zeros((ROWS, 1), F32)
    loss, weights = lax.fori_loop(0, rows // ROWS, body, (zero, zero))
    wide = n_far * cw
    gain_sum = jnp.sum(acc_ref[...], axis=0, keepdims=True)
    gain_sum = jnp.concatenate([gain_sum[:, i : i + wide] for i in range(0, dout, wide)], 0)
    lane = lax.broadcasted_iota(jnp.int32, (1, wide), 1)
    loss = jnp.sum(loss, axis=0, keepdims=True)
    weights = jnp.sum(weights, axis=0, keepdims=True)
    scalars = jnp.where(lane == 0, loss, jnp.where(lane == 1, weights, 0.0))
    words = [*split_words(gain_sum), *split_words(scalars)]
    left = STAT_ROWS - sum(w.shape[0] for w in words)
    words = jnp.concatenate([*words, jnp.zeros((left, wide), F32)], 0).astype(BF)
    if cw % 128 == 0:
        for q in range(NEAR):
            grad_refs[q][rows:, :] = words
    else:
        for q in range(NEAR):
            grad_refs[0][q, rows:, :] = words


def join(plan, info, ctx, gain, next_hidden, weights):
    n_dp, n_tensor, chunks, _, _ = plan
    _, width, rows = ctx.shape
    dout = gain.shape[1]
    wide = dout // NEAR // chunks
    tall = [rows + STAT_ROWS] + [rows] * (chunks - 1)
    aligned = dout // n_dp // chunks % 128 == 0
    if aligned:
        grads = [shape((n, wide)) for n in tall for _ in range(NEAR)]
    else:
        grads = [shape((NEAR, n, wide)) for n in tall]
    out = pl.pallas_call(
        functools.partial(join_body, plan, [len(w) for w in weights]),
        in_specs=[SM] + [VM] * (3 + sum(len(w) for w in weights)),
        out_specs=[VM] * (1 + len(grads)),
        out_shape=[shape((rows, dout)), *grads],
        scratch_shapes=[
            pltpu.VMEM((n_tensor, rows, width), BF),
            pltpu.VMEM((rows, dout), F32),
            pltpu.VMEM((rows, 128), F32),
            pltpu.VMEM((ROWS, dout), F32),
            pltpu.VMEM((ROWS, dout), F32),
        ],
        compiler_params=params(),
        cost_estimate=pl.CostEstimate(
            flops=2 * rows * dout * width * n_tensor,
            bytes_accessed=2 * dout * (width * n_tensor + 3 * rows),
            transcendentals=rows,
        ),
        name="join",
    )(info, ctx, gain, next_hidden, *[w for held in weights for w in held])
    if aligned:
        return out[0], [out[1 + j * NEAR : 1 + (j + 1) * NEAR] for j in range(chunks)]
    return out[0], [[g[q] for q in range(NEAR)] for g in out[1:]]


def stat_sizes(dout, wide, cw):
    in_block = dout // cw
    return dout // wide, in_block, -(-(2 * in_block + 2) // 16) * 16


def block_words(gains, scalars, tall, cw):
    words = [*split_words(gains), *split_words(scalars)]
    left = tall - sum(w.shape[0] for w in words)
    return jnp.concatenate([*words, jnp.zeros((left, cw), F32)], 0).astype(BF)


def block_sums(words, n):
    words = words.astype(F32)
    return words[:n] + words[n : 2 * n], words[2 * n : 2 * n + 1] + words[2 * n + 1 : 2 * n + 2]


def grad_body(plan, dout, counts, info_ref, *refs):
    n_dp, n_tensor, _, _, xor_far = plan
    keep_ref, send_ref = refs[-2:]
    ctx_refs, at = [], 0
    for n in counts:
        ctx_refs.append(refs[at : at + n])
        at += n
    g_refs = refs[at:-2]
    n_y, n_far, tall, cw = keep_ref.shape
    feats, rows = ctx_refs[0][0].shape[1:]
    wide = n_far * cw
    me = info_ref[0]
    core, y = me % 2, me // 2
    if tall > feats:
        in_piece, in_block, stat_rows = stat_sizes(dout, wide, cw)
        sums = sum(ref[rows:, :].astype(F32) for ref in g_refs)
        gains, scalars = block_sums(sums, in_piece)
        gains = jnp.concatenate([gains[:, b * cw : (b + 1) * cw] for b in range(n_far)], 0)
        words = block_words(gains, scalars[:, :cw], stat_rows, cw)
    for s, ref in ((1, send_ref), (0, keep_ref)):
        for a in range(n_y):
            m = (y ^ a if xor_far else a) * 2 + (core ^ s)
            total = None
            for parts, g in zip(ctx_refs, g_refs):
                c = jnp.concatenate([part[m] for part in parts], 0) if len(parts) > 1 else parts[0][m]
                part = dot(c, g[:rows, :], ((1,), (0,)))
                total = part if total is None else total + part
            total = total.astype(BF)
            for b in range(n_far):
                ref[a, b, :feats, :] = total[:, b * cw : (b + 1) * cw]
                if tall > feats:
                    ref[a, b, feats:, :] = words


def gradient(plan, dout, info, ctxs, grads):
    n_dp, n_tensor, chunks, _, _ = plan
    _, feats, rows = ctxs[0][0].shape
    wide = grads[0].shape[1]
    cw = dout // n_dp // chunks
    tall = feats
    if grads[0].shape[0] > rows:
        tall += stat_sizes(dout, wide, cw)[2]
    block = shape((n_tensor // 2, n_dp // NEAR, tall, cw))
    return pl.pallas_call(
        functools.partial(grad_body, plan, dout, [len(c) for c in ctxs]),
        in_specs=[SM] + [VM] * (NEAR + sum(len(c) for c in ctxs)),
        out_specs=[VM, VM],
        out_shape=[block, block],
        compiler_params=params(),
        cost_estimate=pl.CostEstimate(
            flops=2 * NEAR * n_tensor * rows * feats * wide,
            bytes_accessed=2 * (NEAR * rows * (n_tensor * feats + wide) + n_tensor * feats * wide),
            transcendentals=0,
        ),
        name="gradient",
    )(info, *[part for parts in ctxs for part in parts], *grads)


def merge_body(in_block, feats, keep_ref, got_ref, *out_refs):
    n_y, n_far, tall, cw = keep_ref.shape
    if tall > feats:
        gains, scalars = block_sums(keep_ref[0, 0, feats:, :], in_block)
        more, others = block_sums(got_ref[0, 0, feats:, :], in_block)
        words = block_words(gains + more, scalars + others, tall - feats, cw)
    for i in range(n_y * n_far):
        a, b = divmod(i, n_far)
        total = keep_ref[a, b, :feats, :].astype(F32) + got_ref[a, b, :feats, :].astype(F32)
        ref, at = (out_refs[0], (a, b)) if len(out_refs) == 1 else (out_refs[i], (0, 0))
        ref[(*at, slice(0, feats), slice(None))] = total.astype(BF)
        if tall > feats:
            ref[(*at, slice(feats, tall), slice(None))] = words


def merge(plan, dout, feats, keep, got):
    n_y, n_far, tall, cw = keep.shape
    if plan[4]:
        outs = [shape((1, 1, tall, cw))] * (n_y * n_far)
    else:
        outs = [shape(keep.shape)]
    return pl.pallas_call(
        functools.partial(merge_body, dout // cw, feats),
        in_specs=[VM, VM],
        out_specs=[VM] * len(outs),
        out_shape=outs,
        compiler_params=params(),
        cost_estimate=pl.CostEstimate(flops=keep.size, bytes_accessed=6 * keep.size, transcendentals=0),
        name="merge",
    )(keep, got)


def finish_body(counts, in_piece, n_far, *refs):
    grad_ref, gain_ref, loss_ref = refs[-3:]
    feats = grad_ref.shape[0]
    chunks, at = [], 0
    for n in counts:
        chunks.append(refs[at : at + n])
        at += n
    tall, cw = chunks[0][0].shape[2:]

    def total(blocks, rows):
        parts = [
            r[a, b, rows, :].astype(F32) for r in blocks for a in range(r.shape[0]) for b in range(r.shape[1])
        ]
        return sum(parts[1:], parts[0])

    gains, scalars = block_sums(total(chunks[0], slice(feats, tall)), in_piece * n_far)
    lane = lax.broadcasted_iota(jnp.int32, (1, cw), 1)
    weight = jnp.sum(jnp.where(lane == 1, scalars, 0.0), axis=1, keepdims=True)
    loss_ref[0, 0] = jnp.sum(jnp.where(lane == 0, scalars / weight, 0.0))
    gains = gains / weight
    for r in range(in_piece):
        for b in range(n_far):
            gain_ref[pl.ds(r * n_far + b, 1), :] = gains[b * in_piece + r : b * in_piece + r + 1, :]
    for j, blocks in enumerate(chunks):
        grad_ref[:, j * cw : (j + 1) * cw] = (total(blocks, slice(0, feats)) / weight).astype(BF)


def finish(plan, dout, feats, chunks):
    n_dp = plan[0]
    cw = chunks[0][0].shape[3]
    n_far = n_dp // NEAR
    return pl.pallas_call(
        functools.partial(finish_body, [len(c) for c in chunks], dout // (n_far * cw), n_far),
        in_specs=[VM] * sum(len(c) for c in chunks),
        out_specs=[VM, VM, SM],
        out_shape=[shape((feats, dout // n_dp)), shape((dout // cw, cw), F32), shape((1, 1), F32)],
        compiler_params=params(),
        name="finish",
    )(*[b for c in chunks for b in c])


def swap(x, axis, n, mask):
    return lax.ppermute(x, axis, [(i, i ^ mask) for i in range(n)])


def swap_far(x, n_dp, n_tensor, a, b):
    mask = b * NEAR * n_tensor + a * 2
    return lax.ppermute(x, ("dp", "tensor"), [(i, i ^ mask) for i in range(n_dp * n_tensor)])


def exchange_far(plan, blocks):
    n_dp, n_tensor, _, _, xor_far = plan
    n_far = n_dp // NEAR
    if xor_far:
        return [blocks[0]] + [
            swap_far(block, n_dp, n_tensor, *divmod(i, n_far)) for i, block in enumerate(blocks) if i
        ]
    cores = [[2 * y + c for y in range(n_tensor // 2)] for c in range(2)]
    nears = [[NEAR * f + q for f in range(n_far)] for q in range(NEAR)]
    x = lax.all_to_all(blocks[0], "tensor", 0, 0, tiled=True, axis_index_groups=cores)
    return [lax.all_to_all(x, "dp", 1, 1, tiled=True, axis_index_groups=nears)]


def gather_large(n_dp, n_tensor, _, weight, context):
    ctx = lax.all_to_all(context, "tensor", 0, 0, tiled=True)
    held = {0: weight}
    bit = n_tensor // 2
    while bit:
        held.update({m | bit: swap(w, "tensor", n_tensor, bit) for m, w in list(held.items())})
        bit //= 2
    ctxs = [[ctx]] + [[swap(ctx, "dp", n_dp, q)] for q in range(1, NEAR)]
    return ctx, ctxs, [[held[m]] for m in range(n_tensor)]


def gather_small(n_dp, n_tensor, side, weight, context):
    barrier = lax.optimization_barrier

    def dp(x, mask):
        return swap(x, "dp", n_dp, mask)

    def tensor(x, mask):
        return swap(x, "tensor", n_tensor, mask)

    dout = weight.shape[1]
    cut = dout // 4
    mine = tensor(lax.dynamic_slice_in_dim(weight, side * cut, cut, 1), 2)
    beside = tensor(weight, 1)
    rest = weight[:, 2 * cut :]
    mine, context = barrier((mine, context))
    other, mine_beside = dp(mine, 1), tensor(mine, 1)
    ctx = lax.all_to_all(context, "tensor", 0, 0, tiled=True)
    rest, other, mine_beside, beside, ctx = barrier((rest, other, mine_beside, beside, ctx))
    rest, other_beside = tensor(rest, 2), tensor(other, 1)
    ctx_x, ctx_z = dp(ctx, 1), dp(ctx, 2)
    rest, other_beside, ctx_x, ctx_z = barrier((rest, other_beside, ctx_x, ctx_z))
    half = ctx.shape[1] // 2
    ctxs = [[ctx], [ctx_x], [ctx_z], [dp(ctx_x[:, :half], 2), dp(ctx_z[:, half:], 1)]]
    far = [mine, other, rest]
    return ctx, ctxs, [[weight], [beside], far, [mine_beside, other_beside, tensor(rest, 1)]]


def on_device(
    n_dp,
    n_tensor,
    query_states,
    key_states,
    value_states,
    joining_weight,
    norm_gain,
    next_hidden,
    lengths,
    vote_counts,
):
    _, tokens, width = query_states.shape
    seq = tokens // lengths.shape[0]
    dout = norm_gain.shape[0]
    rows = next_hidden.shape[0]
    chunks = 2 if dout // n_dp >= 256 else 1
    xor_far = (n_tensor // 2) * (n_dp // NEAR) <= 4
    plan = (n_dp, n_tensor, chunks, seq, xor_far)
    me = lax.axis_index("tensor").astype(jnp.int32)
    group = lax.axis_index("dp").astype(jnp.int32)
    info = jnp.stack([me, group, lengths[0], vote_counts[0]])

    attended = attend(info, query_states[0], key_states[0], value_states[0], rows)
    gather = gather_small if xor_far else gather_large
    ctx, ctxs, weights = gather(n_dp, n_tensor, group & 1, joining_weight[0], attended)
    hidden, grads = join(plan, info, ctx, norm_gain[None, :], next_hidden, weights)
    parts = []
    for j in range(chunks):
        near = [grads[j][0]] + [swap(grads[j][q], "dp", n_dp, q) for q in range(1, NEAR)]
        keep, send = gradient(plan, dout, info, ctxs, near)
        blocks = merge(plan, dout, width, keep, swap(send, "tensor", n_tensor, 1))
        parts.append(exchange_far(plan, blocks))
    weight_grad, gain_grad, loss = finish(plan, dout, width, parts)
    return (hidden, weight_grad[None], gain_grad.reshape(dout), loss.reshape(()))


def solution(mesh):
    return jax.shard_map(
        functools.partial(on_device, mesh.shape["dp"], mesh.shape["tensor"]),
        mesh=mesh,
        in_specs=(
            P(None, "dp", "tensor"),
            P(None, "dp", "tensor"),
            P(None, "dp", "tensor"),
            P(None, "tensor", None),
            P(),
            P(("dp", "tensor"), None),
            P("dp"),
            P("dp"),
        ),
        out_specs=(P(("dp", "tensor"), None), P(None, "tensor", "dp"), P(), P()),
        check_vma=False,
    )
```

```python
import functools
import math

import jax
import jax.numpy as jnp
from jax import lax
from jax.experimental import pallas as pl
from jax.experimental.pallas import tpu as pltpu
from jax.sharding import PartitionSpec as P

HD = 128
QB = 128
ROWS = 128
COLS = 256
NEAR = 4
STAT_ROWS = 32

loss_scale = 65536.0
neg_large = -1e30
MIB = 1 << 20
BF = jnp.bfloat16
F32 = jnp.float32


def dot(a, b, dims):
    return lax.dot_general(a, b, (dims, ((), ())), preferred_element_type=F32)


def split_words(x):
    high = x.astype(BF).astype(F32)
    return high, (x - high).astype(BF).astype(F32)


def shape(dims, dtype=BF):
    return jax.ShapeDtypeStruct(dims, dtype)


def params():
    return pltpu.CompilerParams(vmem_limit_bytes=48 * MIB)


VM = pl.BlockSpec(memory_space=pltpu.VMEM)
SM = pl.BlockSpec(memory_space=pltpu.SMEM)


def attend_body(info_ref, q_ref, k_ref, v_ref, o_ref):
    seq = q_ref.shape[0]
    rows = o_ref.shape[2]
    rate = math.log2(math.e) / math.sqrt(HD)
    length = info_ref[2]
    key = lax.broadcasted_iota(jnp.int32, (seq, 1), 0)
    hide = jnp.where(key < length, 0.0, neg_large)
    r = lax.broadcasted_iota(jnp.int32, (QB, QB), 0)
    c = lax.broadcasted_iota(jnp.int32, (QB, QB), 1)
    for h in range(q_ref.shape[1] // HD):
        at = slice(h * HD, (h + 1) * HD)
        q_t, v_t = q_ref[:, at].T, v_ref[:, at].T
        for i in range(seq // QB):
            keys = (i + 1) * QB
            scores = dot(k_ref[:keys, at], q_t[:, i * QB : keys], ((1,), (0,))) + hide[:keys]
            last = jnp.where(r <= c, scores[keys - QB :], neg_large)
            scores = last if i == 0 else jnp.concatenate([scores[: keys - QB], last], 0)
            peak = jnp.max(scores, axis=0, keepdims=True)
            e = jnp.exp2((scores - peak) * rate)
            total = jnp.sum(e, axis=0, keepdims=True)
            out = (dot(v_t[:, :keys], e.astype(BF), ((1,), (0,))) / total).astype(BF)
            for n in range(0, QB, min(rows, QB)):
                block, first = divmod(i * QB + n, rows)
                o_ref[block, at, first : first + min(rows, QB)] = out[:, n : n + rows]


def attend(info, q, k, v, rows):
    seq, width = q.shape
    heads = width // HD
    block = VM
    return pl.pallas_call(
        attend_body,
                in_specs=[SM, block, block, block],
        out_specs=VM,
        out_shape=shape((seq // rows, width, rows)),
        compiler_params=pltpu.CompilerParams(vmem_limit_bytes=60 * MIB),
        cost_estimate=pl.CostEstimate(
            flops=4 * seq * seq * width, bytes_accessed=8 * seq * width, transcendentals=heads * seq * seq
        ),
        name="attend",
    )(info, q, k, v)


def join_body(plan, counts, info_ref, ctx_ref, gain_ref, next_ref, *refs):
    n_dp, n_tensor, chunks, seq, xor_far = plan
    w_refs, at = [], 0
    for n in counts:
        w_refs.append(refs[at : at + n])
        at += n
    hidden_ref, grad_refs = refs[at], refs[at + 1 : -5]
    turned_ref, joined_ref, square_ref, acc_ref, slope_ref = refs[-5:]
    rows, dout = joined_ref.shape
    me, group, length, votes = info_ref[0], info_ref[1], info_ref[2], info_ref[3]
    for m in range(n_tensor):
        turned_ref[m] = ctx_ref[me ^ m].T
    near, far = group % NEAR, group // NEAR
    columns = [(c, 0, c) for c in range(0, dout, COLS)]
    if xor_far:
        cut, spare = w_refs[-1][0].shape[1], w_refs[-1][2].shape[1]
        own, other = near % 2 * cut, (1 - near % 2) * cut
        columns = [(pl.multiple_of(own + c, COLS), 0, c) for c in range(0, cut, COLS)]
        columns += [(pl.multiple_of(other + c, COLS), 1, c) for c in range(0, cut, COLS)]
        columns += [(2 * cut + c, 2, c) for c in range(0, spare, COLS)]
    for step, (start, piece, first) in enumerate(columns):
        to = pl.ds(start, COLS)
        total = None
        for m in range(n_tensor):
            whole = len(w_refs[m]) == 1
            w = w_refs[m][0][:, to] if whole else w_refs[m][piece][:, first : first + COLS]
            part = dot(turned_ref[m], w, ((1,), (0,)))
            total = part if total is None else total + part
        joined_ref[:, to] = total
        sq = total * total
        lanes = sum(sq[:, i : i + 128] for i in range(0, COLS, 128))
        square_ref[...] = lanes if step == 0 else square_ref[...] + lanes
    acc_ref[...] = jnp.zeros_like(acc_ref)
    slice_w = dout // n_dp
    cw = slice_w // chunks
    n_far = n_dp // NEAR

    def body(r, carry):
        loss, weights = carry
        at = pl.ds(pl.multiple_of(r * ROWS, ROWS), ROWS)
        inv = lax.rsqrt(jnp.sum(square_ref[at, :], axis=1, keepdims=True) * (1.0 / dout) + 1e-06)
        pos = (me * rows + r * ROWS) % seq + lax.broadcasted_iota(jnp.int32, (ROWS, 1), 0)
        weight = jnp.where(pos < length - 1, votes.astype(F32), 0.0)
        scaled = weight * (loss_scale * 2.0 / dout)
        miss = jnp.zeros((ROWS, 128), F32)
        lean = jnp.zeros((ROWS, 128), F32)
        for c in range(0, dout, 512):
            cs = slice(c, c + 512)
            normed = joined_ref[at, cs] * inv
            gain = gain_ref[:, cs]
            predicted = normed * gain
            hidden_ref[at, cs] = predicted.astype(BF)
            misfit = predicted - next_ref[at, cs].astype(F32)
            grad = scaled * misfit
            slope = grad * gain
            acc_ref[:, cs] += grad * normed
            slope_ref[:, cs] = slope
            sq = misfit * misfit
            ln = slope * normed
            miss += sum(sq[:, i : i + 128] for i in range(0, 512, 128))
            lean += sum(ln[:, i : i + 128] for i in range(0, 512, 128))
            joined_ref[at, cs] = normed
        lean = jnp.sum(lean, axis=1, keepdims=True) * (1.0 / dout)

        def gradient_at(cs):
            return (inv * (slope_ref[:, cs] - joined_ref[at, cs] * lean)).astype(BF)

        for j in range(chunks):
            for q in range(NEAR):
                for b in range(n_far):
                    to = slice(b * cw, (b + 1) * cw)
                    if cw % 128 == 0:
                        other = (far ^ b if xor_far else b) * NEAR + (near ^ q)
                        start = pl.multiple_of(other * slice_w + j * cw, 128)
                        grad_refs[j * NEAR + q][at, to] = gradient_at(pl.ds(start, cw))
                    else:
                        start = (b * NEAR + q) * slice_w + j * cw
                        grad_refs[j][near ^ q, at, to] = gradient_at(slice(start, start + cw))
        loss = loss + weight * (jnp.sum(miss, axis=1, keepdims=True) * (1.0 / dout))
        return loss, weights + weight

    zero = jnp.zeros((ROWS, 1), F32)
    loss, weights = lax.fori_loop(0, rows // ROWS, body, (zero, zero))
    wide = n_far * cw
    gain_sum = jnp.sum(acc_ref[...], axis=0, keepdims=True)
    gain_sum = jnp.concatenate([gain_sum[:, i : i + wide] for i in range(0, dout, wide)], 0)
    lane = lax.broadcasted_iota(jnp.int32, (1, wide), 1)
    loss = jnp.sum(loss, axis=0, keepdims=True)
    weights = jnp.sum(weights, axis=0, keepdims=True)
    scalars = jnp.where(lane == 0, loss, jnp.where(lane == 1, weights, 0.0))
    words = [*split_words(gain_sum), *split_words(scalars)]
    left = STAT_ROWS - sum(w.shape[0] for w in words)
    words = jnp.concatenate([*words, jnp.zeros((left, wide), F32)], 0).astype(BF)
    if cw % 128 == 0:
        for q in range(NEAR):
            grad_refs[q][rows:, :] = words
    else:
        for q in range(NEAR):
            grad_refs[0][q, rows:, :] = words


def join(plan, info, ctx, gain, next_hidden, weights):
    n_dp, n_tensor, chunks, _, _ = plan
    _, width, rows = ctx.shape
    dout = gain.shape[1]
    wide = dout // NEAR // chunks
    tall = [rows + STAT_ROWS] + [rows] * (chunks - 1)
    aligned = dout // n_dp // chunks % 128 == 0
    if aligned:
        grads = [shape((n, wide)) for n in tall for _ in range(NEAR)]
    else:
        grads = [shape((NEAR, n, wide)) for n in tall]
    out = pl.pallas_call(
        functools.partial(join_body, plan, [len(w) for w in weights]),
        in_specs=[SM] + [VM] * (3 + sum(len(w) for w in weights)),
        out_specs=[VM] * (1 + len(grads)),
        out_shape=[shape((rows, dout)), *grads],
        scratch_shapes=[
            pltpu.VMEM((n_tensor, rows, width), BF),
            pltpu.VMEM((rows, dout), F32),
            pltpu.VMEM((rows, 128), F32),
            pltpu.VMEM((ROWS, dout), F32),
            pltpu.VMEM((ROWS, dout), F32),
        ],
        compiler_params=params(),
        cost_estimate=pl.CostEstimate(
            flops=2 * rows * dout * width * n_tensor,
            bytes_accessed=2 * dout * (width * n_tensor + 3 * rows),
            transcendentals=rows,
        ),
        name="join",
    )(info, ctx, gain, next_hidden, *[w for held in weights for w in held])
    if aligned:
        return out[0], [out[1 + j * NEAR : 1 + (j + 1) * NEAR] for j in range(chunks)]
    return out[0], [[g[q] for q in range(NEAR)] for g in out[1:]]


def stat_sizes(dout, wide, cw):
    in_block = dout // cw
    return dout // wide, in_block, -(-(2 * in_block + 2) // 16) * 16


def block_words(gains, scalars, tall, cw):
    words = [*split_words(gains), *split_words(scalars)]
    left = tall - sum(w.shape[0] for w in words)
    return jnp.concatenate([*words, jnp.zeros((left, cw), F32)], 0).astype(BF)


def block_sums(words, n):
    words = words.astype(F32)
    return words[:n] + words[n : 2 * n], words[2 * n : 2 * n + 1] + words[2 * n + 1 : 2 * n + 2]


def grad_body(plan, dout, counts, s, info_ref, *refs):
    n_dp, n_tensor, _, _, xor_far = plan
    ref = refs[-1]
    ctx_refs, at = [], 0
    for n in counts:
        ctx_refs.append(refs[at : at + n])
        at += n
    g_refs = refs[at:-1]
    n_y, n_far, tall, cw = ref.shape
    feats, rows = ctx_refs[0][0].shape[1:]
    wide = n_far * cw
    me = info_ref[0]
    core, y = me % 2, me // 2
    if tall > feats:
        in_piece, in_block, stat_rows = stat_sizes(dout, wide, cw)
        sums = sum(g[rows:, :].astype(F32) for g in g_refs)
        gains, scalars = block_sums(sums, in_piece)
        gains = jnp.concatenate([gains[:, b * cw : (b + 1) * cw] for b in range(n_far)], 0)
        words = block_words(gains, scalars[:, :cw], stat_rows, cw)
    for a in range(n_y):
        m = (y ^ a if xor_far else a) * 2 + (core ^ s)
        total = None
        for parts, g in zip(ctx_refs, g_refs):
            c = jnp.concatenate([part[m] for part in parts], 0) if len(parts) > 1 else parts[0][m]
            part = dot(c, g[:rows, :], ((1,), (0,)))
            total = part if total is None else total + part
        total = total.astype(BF)
        for b in range(n_far):
            ref[a, b, :feats, :] = total[:, b * cw : (b + 1) * cw]
            if tall > feats:
                ref[a, b, feats:, :] = words


def gradient(plan, dout, info, ctxs, grads, s):
    n_dp, n_tensor, chunks, _, _ = plan
    _, feats, rows = ctxs[0][0].shape
    wide = grads[0].shape[1]
    cw = dout // n_dp // chunks
    tall = feats
    if grads[0].shape[0] > rows:
        tall += stat_sizes(dout, wide, cw)[2]
    block = shape((n_tensor // 2, n_dp // NEAR, tall, cw))
    return pl.pallas_call(
        functools.partial(grad_body, plan, dout, [len(c) for c in ctxs], s),
        in_specs=[SM] + [VM] * (NEAR + sum(len(c) for c in ctxs)),
        out_specs=VM,
        out_shape=block,
        compiler_params=params(),
        cost_estimate=pl.CostEstimate(
            flops=NEAR * n_tensor * rows * feats * wide,
            bytes_accessed=NEAR * rows * (n_tensor * feats + 2 * wide) + n_tensor * feats * wide,
            transcendentals=0,
        ),
        name="gradient",
    )(info, *[part for parts in ctxs for part in parts], *grads)


def merge_body(in_block, feats, keep_ref, got_ref, *out_refs):
    n_y, n_far, tall, cw = keep_ref.shape
    if tall > feats:
        gains, scalars = block_sums(keep_ref[0, 0, feats:, :], in_block)
        more, others = block_sums(got_ref[0, 0, feats:, :], in_block)
        words = block_words(gains + more, scalars + others, tall - feats, cw)
    for i in range(n_y * n_far):
        a, b = divmod(i, n_far)
        total = keep_ref[a, b, :feats, :].astype(F32) + got_ref[a, b, :feats, :].astype(F32)
        ref, at = (out_refs[0], (a, b)) if len(out_refs) == 1 else (out_refs[i], (0, 0))
        ref[(*at, slice(0, feats), slice(None))] = total.astype(BF)
        if tall > feats:
            ref[(*at, slice(feats, tall), slice(None))] = words


def merge(plan, dout, feats, keep, got):
    n_y, n_far, tall, cw = keep.shape
    if plan[4]:
        outs = [shape((1, 1, tall, cw))] * (n_y * n_far)
    else:
        outs = [shape(keep.shape)]
    return pl.pallas_call(
        functools.partial(merge_body, dout // cw, feats),
        in_specs=[VM, VM],
        out_specs=[VM] * len(outs),
        out_shape=outs,
        compiler_params=params(),
        cost_estimate=pl.CostEstimate(flops=keep.size, bytes_accessed=6 * keep.size, transcendentals=0),
        name="merge",
    )(keep, got)


def finish_body(counts, in_piece, n_far, *refs):
    grad_ref, gain_ref, loss_ref = refs[-3:]
    feats = grad_ref.shape[0]
    chunks, at = [], 0
    for n in counts:
        chunks.append(refs[at : at + n])
        at += n
    tall, cw = chunks[0][0].shape[2:]

    def total(blocks, rows):
        parts = [
            r[a, b, rows, :].astype(F32) for r in blocks for a in range(r.shape[0]) for b in range(r.shape[1])
        ]
        return sum(parts[1:], parts[0])

    gains, scalars = block_sums(total(chunks[0], slice(feats, tall)), in_piece * n_far)
    lane = lax.broadcasted_iota(jnp.int32, (1, cw), 1)
    weight = jnp.sum(jnp.where(lane == 1, scalars, 0.0), axis=1, keepdims=True)
    loss_ref[0, 0] = jnp.sum(jnp.where(lane == 0, scalars / weight, 0.0))
    gains = gains / weight
    for r in range(in_piece):
        for b in range(n_far):
            gain_ref[pl.ds(r * n_far + b, 1), :] = gains[b * in_piece + r : b * in_piece + r + 1, :]
    for j, blocks in enumerate(chunks):
        grad_ref[:, j * cw : (j + 1) * cw] = (total(blocks, slice(0, feats)) / weight).astype(BF)


def finish(plan, dout, feats, chunks):
    n_dp = plan[0]
    cw = chunks[0][0].shape[3]
    n_far = n_dp // NEAR
    return pl.pallas_call(
        functools.partial(finish_body, [len(c) for c in chunks], dout // (n_far * cw), n_far),
        in_specs=[VM] * sum(len(c) for c in chunks),
        out_specs=[VM, VM, SM],
        out_shape=[shape((feats, dout // n_dp)), shape((dout // cw, cw), F32), shape((1, 1), F32)],
        compiler_params=params(),
        name="finish",
    )(*[b for c in chunks for b in c])


def swap(x, axis, n, mask):
    return lax.ppermute(x, axis, [(i, i ^ mask) for i in range(n)])


def swap_far(x, n_dp, n_tensor, a, b):
    mask = b * NEAR * n_tensor + a * 2
    return lax.ppermute(x, ("dp", "tensor"), [(i, i ^ mask) for i in range(n_dp * n_tensor)])


def exchange_far(plan, blocks):
    n_dp, n_tensor, _, _, xor_far = plan
    n_far = n_dp // NEAR
    if xor_far:
        return [blocks[0]] + [
            swap_far(block, n_dp, n_tensor, *divmod(i, n_far)) for i, block in enumerate(blocks) if i
        ]
    cores = [[2 * y + c for y in range(n_tensor // 2)] for c in range(2)]
    nears = [[NEAR * f + q for f in range(n_far)] for q in range(NEAR)]
    x = lax.all_to_all(blocks[0], "tensor", 0, 0, tiled=True, axis_index_groups=cores)
    return [lax.all_to_all(x, "dp", 1, 1, tiled=True, axis_index_groups=nears)]


def gather_large(n_dp, n_tensor, _, weight, context):
    ctx = lax.all_to_all(context, "tensor", 0, 0, tiled=True)
    held = {0: weight}
    bit = n_tensor // 2
    while bit:
        held.update({m | bit: swap(w, "tensor", n_tensor, bit) for m, w in list(held.items())})
        bit //= 2
    ctxs = [[ctx]] + [[swap(ctx, "dp", n_dp, q)] for q in range(1, NEAR)]
    return ctx, ctxs, [[held[m]] for m in range(n_tensor)]


def gather_small(n_dp, n_tensor, side, weight, context):
    barrier = lax.optimization_barrier

    def dp(x, mask):
        return swap(x, "dp", n_dp, mask)

    def tensor(x, mask):
        return swap(x, "tensor", n_tensor, mask)

    dout = weight.shape[1]
    cut = dout // 4
    mine = tensor(lax.dynamic_slice_in_dim(weight, side * cut, cut, 1), 2)
    beside = tensor(weight, 1)
    rest = weight[:, 2 * cut :]
    mine, context = barrier((mine, context))
    other, mine_beside = dp(mine, 1), tensor(mine, 1)
    ctx = lax.all_to_all(context, "tensor", 0, 0, tiled=True)
    rest, other, mine_beside, beside, ctx = barrier((rest, other, mine_beside, beside, ctx))
    rest, other_beside = tensor(rest, 2), tensor(other, 1)
    ctx_x, ctx_z = dp(ctx, 1), dp(ctx, 2)
    rest, other_beside, ctx_x, ctx_z = barrier((rest, other_beside, ctx_x, ctx_z))
    half = ctx.shape[1] // 2
    ctxs = [[ctx], [ctx_x], [ctx_z], [dp(ctx_x[:, :half], 2), dp(ctx_z[:, half:], 1)]]
    far = [mine, other, rest]
    return ctx, ctxs, [[weight], [beside], far, [mine_beside, other_beside, tensor(rest, 1)]]


def on_device(
    n_dp,
    n_tensor,
    query_states,
    key_states,
    value_states,
    joining_weight,
    norm_gain,
    next_hidden,
    lengths,
    vote_counts,
):
    _, tokens, width = query_states.shape
    seq = tokens // lengths.shape[0]
    dout = norm_gain.shape[0]
    rows = next_hidden.shape[0]
    chunks = 2 if dout // n_dp >= 256 else 1
    xor_far = (n_tensor // 2) * (n_dp // NEAR) <= 4
    plan = (n_dp, n_tensor, chunks, seq, xor_far)
    me = lax.axis_index("tensor").astype(jnp.int32)
    group = lax.axis_index("dp").astype(jnp.int32)
    info = jnp.stack([me, group, lengths[0], vote_counts[0]])

    attended = attend(info, query_states[0], key_states[0], value_states[0], rows)
    gather = gather_small if xor_far else gather_large
    ctx, ctxs, weights = gather(n_dp, n_tensor, group & 1, joining_weight[0], attended)
    hidden, grads = join(plan, info, ctx, norm_gain[None, :], next_hidden, weights)
    parts = []
    for j in range(chunks):
        near = [grads[j][0]] + [swap(grads[j][q], "dp", n_dp, q) for q in range(1, NEAR)]
        send = gradient(plan, dout, info, ctxs, near, 1)
        keep = gradient(plan, dout, info, ctxs, near, 0)
        blocks = merge(plan, dout, width, keep, swap(send, "tensor", n_tensor, 1))
        parts.append(exchange_far(plan, blocks))
    weight_grad, gain_grad, loss = finish(plan, dout, width, parts)
    return (hidden, weight_grad[None], gain_grad.reshape(dout), loss.reshape(()))


def solution(mesh):
    return jax.shard_map(
        functools.partial(on_device, mesh.shape["dp"], mesh.shape["tensor"]),
        mesh=mesh,
        in_specs=(
            P(None, "dp", "tensor"),
            P(None, "dp", "tensor"),
            P(None, "dp", "tensor"),
            P(None, "tensor", None),
            P(),
            P(("dp", "tensor"), None),
            P("dp"),
            P("dp"),
        ),
        out_specs=(P(("dp", "tensor"), None), P(None, "tensor", "dp"), P(), P()),
        check_vma=False,
    )
```

```python
import functools
import math

import jax
import jax.numpy as jnp
from jax import lax
from jax.experimental import pallas as pl
from jax.experimental.pallas import tpu as pltpu
from jax.sharding import PartitionSpec as P

HD = 128
QB = 128
ROWS = 128
COLS = 256
NEAR = 4
STAT_ROWS = 32

loss_scale = 65536.0
neg_large = -1e30
MIB = 1 << 20
BF = jnp.bfloat16
F32 = jnp.float32


def dot(a, b, dims):
    return lax.dot_general(a, b, (dims, ((), ())), preferred_element_type=F32)


def split_words(x):
    high = x.astype(BF).astype(F32)
    return high, (x - high).astype(BF).astype(F32)


def shape(dims, dtype=BF):
    return jax.ShapeDtypeStruct(dims, dtype)


def params():
    return pltpu.CompilerParams(vmem_limit_bytes=48 * MIB)


VM = pl.BlockSpec(memory_space=pltpu.VMEM)
SM = pl.BlockSpec(memory_space=pltpu.SMEM)


def attend_body(info_ref, q_ref, k_ref, v_ref, o_ref):
    seq = q_ref.shape[0]
    rows = o_ref.shape[2]
    rate = math.log2(math.e) / math.sqrt(HD)
    length = info_ref[2]
    key = lax.broadcasted_iota(jnp.int32, (seq, 1), 0)
    hide = jnp.where(key < length, 0.0, neg_large)
    r = lax.broadcasted_iota(jnp.int32, (QB, QB), 0)
    c = lax.broadcasted_iota(jnp.int32, (QB, QB), 1)
    for h in range(q_ref.shape[1] // HD):
        at = slice(h * HD, (h + 1) * HD)
        q_t, v_t = q_ref[:, at].T, v_ref[:, at].T
        for i in range(seq // QB):
            keys = (i + 1) * QB
            scores = dot(k_ref[:keys, at], q_t[:, i * QB : keys], ((1,), (0,))) + hide[:keys]
            last = jnp.where(r <= c, scores[keys - QB :], neg_large)
            scores = last if i == 0 else jnp.concatenate([scores[: keys - QB], last], 0)
            peak = jnp.max(scores, axis=0, keepdims=True)
            e = jnp.exp2((scores - peak) * rate)
            total = jnp.sum(e, axis=0, keepdims=True)
            out = (dot(v_t[:, :keys], e.astype(BF), ((1,), (0,))) / total).astype(BF)
            for n in range(0, QB, min(rows, QB)):
                block, first = divmod(i * QB + n, rows)
                o_ref[block, at, first : first + min(rows, QB)] = out[:, n : n + rows]


def attend(info, q, k, v, rows):
    seq, width = q.shape
    heads = width // HD
    block = VM
    return pl.pallas_call(
        attend_body,
                in_specs=[SM, block, block, block],
        out_specs=VM,
        out_shape=shape((seq // rows, width, rows)),
        compiler_params=pltpu.CompilerParams(vmem_limit_bytes=60 * MIB),
        cost_estimate=pl.CostEstimate(
            flops=4 * seq * seq * width, bytes_accessed=8 * seq * width, transcendentals=heads * seq * seq
        ),
        name="attend",
    )(info, q, k, v)


def join_body(plan, counts, info_ref, ctx_ref, gain_ref, next_ref, *refs):
    n_dp, n_tensor, chunks, seq, xor_far = plan
    w_refs, at = [], 0
    for n in counts:
        w_refs.append(refs[at : at + n])
        at += n
    hidden_ref, grad_refs = refs[at], refs[at + 1 : -5]
    turned_ref, joined_ref, square_ref, acc_ref, slope_ref = refs[-5:]
    rows, dout = joined_ref.shape
    me, group, length, votes = info_ref[0], info_ref[1], info_ref[2], info_ref[3]
    for m in range(n_tensor):
        turned_ref[m] = ctx_ref[me ^ m].T
    near, far = group % NEAR, group // NEAR
    columns = [(c, 0, c) for c in range(0, dout, COLS)]
    if xor_far:
        cut, spare = w_refs[-1][0].shape[1], w_refs[-1][2].shape[1]
        own, other = near % 2 * cut, (1 - near % 2) * cut
        columns = [(pl.multiple_of(own + c, COLS), 0, c) for c in range(0, cut, COLS)]
        columns += [(pl.multiple_of(other + c, COLS), 1, c) for c in range(0, cut, COLS)]
        columns += [(2 * cut + c, 2, c) for c in range(0, spare, COLS)]
    for step, (start, piece, first) in enumerate(columns):
        to = pl.ds(start, COLS)
        total = None
        for m in range(n_tensor):
            whole = len(w_refs[m]) == 1
            w = w_refs[m][0][:, to] if whole else w_refs[m][piece][:, first : first + COLS]
            part = dot(turned_ref[m], w, ((1,), (0,)))
            total = part if total is None else total + part
        joined_ref[:, to] = total
        sq = total * total
        lanes = sum(sq[:, i : i + 128] for i in range(0, COLS, 128))
        square_ref[...] = lanes if step == 0 else square_ref[...] + lanes
    acc_ref[...] = jnp.zeros_like(acc_ref)
    slice_w = dout // n_dp
    cw = slice_w // chunks
    n_far = n_dp // NEAR

    def body(r, carry):
        loss, weights = carry
        at = pl.ds(pl.multiple_of(r * ROWS, ROWS), ROWS)
        inv = lax.rsqrt(jnp.sum(square_ref[at, :], axis=1, keepdims=True) * (1.0 / dout) + 1e-06)
        pos = (me * rows + r * ROWS) % seq + lax.broadcasted_iota(jnp.int32, (ROWS, 1), 0)
        weight = jnp.where(pos < length - 1, votes.astype(F32), 0.0)
        scaled = weight * (loss_scale * 2.0 / dout)
        miss = jnp.zeros((ROWS, 128), F32)
        lean = jnp.zeros((ROWS, 128), F32)
        for c in range(0, dout, 512):
            cs = slice(c, c + 512)
            normed = joined_ref[at, cs] * inv
            gain = gain_ref[:, cs]
            predicted = normed * gain
            hidden_ref[at, cs] = predicted.astype(BF)
            misfit = predicted - next_ref[at, cs].astype(F32)
            grad = scaled * misfit
            slope = grad * gain
            acc_ref[:, cs] += grad * normed
            slope_ref[:, cs] = slope
            sq = misfit * misfit
            ln = slope * normed
            miss += sum(sq[:, i : i + 128] for i in range(0, 512, 128))
            lean += sum(ln[:, i : i + 128] for i in range(0, 512, 128))
            joined_ref[at, cs] = normed
        lean = jnp.sum(lean, axis=1, keepdims=True) * (1.0 / dout)

        def gradient_at(cs):
            return (inv * (slope_ref[:, cs] - joined_ref[at, cs] * lean)).astype(BF)

        for j in range(chunks):
            for q in range(NEAR):
                for b in range(n_far):
                    to = slice(b * cw, (b + 1) * cw)
                    if cw % 128 == 0:
                        other = (far ^ b if xor_far else b) * NEAR + (near ^ q)
                        start = pl.multiple_of(other * slice_w + j * cw, 128)
                        grad_refs[j * NEAR + q][at, to] = gradient_at(pl.ds(start, cw))
                    else:
                        start = (b * NEAR + q) * slice_w + j * cw
                        grad_refs[j][near ^ q, at, to] = gradient_at(slice(start, start + cw))
        loss = loss + weight * (jnp.sum(miss, axis=1, keepdims=True) * (1.0 / dout))
        return loss, weights + weight

    zero = jnp.zeros((ROWS, 1), F32)
    loss, weights = lax.fori_loop(0, rows // ROWS, body, (zero, zero))
    wide = n_far * cw
    gain_sum = jnp.sum(acc_ref[...], axis=0, keepdims=True)
    gain_sum = jnp.concatenate([gain_sum[:, i : i + wide] for i in range(0, dout, wide)], 0)
    lane = lax.broadcasted_iota(jnp.int32, (1, wide), 1)
    loss = jnp.sum(loss, axis=0, keepdims=True)
    weights = jnp.sum(weights, axis=0, keepdims=True)
    scalars = jnp.where(lane == 0, loss, jnp.where(lane == 1, weights, 0.0))
    words = [*split_words(gain_sum), *split_words(scalars)]
    left = STAT_ROWS - sum(w.shape[0] for w in words)
    words = jnp.concatenate([*words, jnp.zeros((left, wide), F32)], 0).astype(BF)
    if cw % 128 == 0:
        for q in range(NEAR):
            grad_refs[q][rows:, :] = words
    else:
        for q in range(NEAR):
            grad_refs[0][q, rows:, :] = words


def join(plan, info, ctx, gain, next_hidden, weights):
    n_dp, n_tensor, chunks, _, _ = plan
    _, width, rows = ctx.shape
    dout = gain.shape[1]
    wide = dout // NEAR // chunks
    tall = [rows + STAT_ROWS] + [rows] * (chunks - 1)
    aligned = dout // n_dp // chunks % 128 == 0
    if aligned:
        grads = [shape((n, wide)) for n in tall for _ in range(NEAR)]
    else:
        grads = [shape((NEAR, n, wide)) for n in tall]
    out = pl.pallas_call(
        functools.partial(join_body, plan, [len(w) for w in weights]),
        in_specs=[SM] + [VM] * (3 + sum(len(w) for w in weights)),
        out_specs=[VM] * (1 + len(grads)),
        out_shape=[shape((rows, dout)), *grads],
        scratch_shapes=[
            pltpu.VMEM((n_tensor, rows, width), BF),
            pltpu.VMEM((rows, dout), F32),
            pltpu.VMEM((rows, 128), F32),
            pltpu.VMEM((ROWS, dout), F32),
            pltpu.VMEM((ROWS, dout), F32),
        ],
        compiler_params=params(),
        cost_estimate=pl.CostEstimate(
            flops=2 * rows * dout * width * n_tensor,
            bytes_accessed=2 * dout * (width * n_tensor + 3 * rows),
            transcendentals=rows,
        ),
        name="join",
    )(info, ctx, gain, next_hidden, *[w for held in weights for w in held])
    if aligned:
        return out[0], [out[1 + j * NEAR : 1 + (j + 1) * NEAR] for j in range(chunks)]
    return out[0], [[g[q] for q in range(NEAR)] for g in out[1:]]


def stat_sizes(dout, wide, cw):
    in_block = dout // cw
    return dout // wide, in_block, -(-(2 * in_block + 2) // 16) * 16


def block_words(gains, scalars, tall, cw):
    words = [*split_words(gains), *split_words(scalars)]
    left = tall - sum(w.shape[0] for w in words)
    return jnp.concatenate([*words, jnp.zeros((left, cw), F32)], 0).astype(BF)


def block_sums(words, n):
    words = words.astype(F32)
    return words[:n] + words[n : 2 * n], words[2 * n : 2 * n + 1] + words[2 * n + 1 : 2 * n + 2]


def grad_body(plan, dout, counts, info_ref, *refs):
    n_dp, n_tensor, _, _, xor_far = plan
    keep_ref, send_ref = refs[-2:]
    ctx_refs, at = [], 0
    for n in counts:
        ctx_refs.append(refs[at : at + n])
        at += n
    g_refs = refs[at:-2]
    n_y, n_far, tall, cw = keep_ref.shape
    feats, rows = ctx_refs[0][0].shape[1:]
    wide = n_far * cw
    me = info_ref[0]
    core, y = me % 2, me // 2
    if tall > feats:
        in_piece, in_block, stat_rows = stat_sizes(dout, wide, cw)
        sums = sum(ref[rows:, :].astype(F32) for ref in g_refs)
        gains, scalars = block_sums(sums, in_piece)
        gains = jnp.concatenate([gains[:, b * cw : (b + 1) * cw] for b in range(n_far)], 0)
        words = block_words(gains, scalars[:, :cw], stat_rows, cw)
    for s, ref in ((1, send_ref), (0, keep_ref)):
        for a in range(n_y):
            m = (y ^ a if xor_far else a) * 2 + (core ^ s)
            total = None
            for parts, g in zip(ctx_refs, g_refs):
                c = jnp.concatenate([part[m] for part in parts], 0) if len(parts) > 1 else parts[0][m]
                part = dot(c, g[:rows, :], ((1,), (0,)))
                total = part if total is None else total + part
            total = total.astype(BF)
            for b in range(n_far):
                ref[a, b, :feats, :] = total[:, b * cw : (b + 1) * cw]
                if tall > feats:
                    ref[a, b, feats:, :] = words


def gradient(plan, dout, info, ctxs, grads):
    n_dp, n_tensor, chunks, _, _ = plan
    _, feats, rows = ctxs[0][0].shape
    wide = grads[0].shape[1]
    cw = dout // n_dp // chunks
    tall = feats
    if grads[0].shape[0] > rows:
        tall += stat_sizes(dout, wide, cw)[2]
    block = shape((n_tensor // 2, n_dp // NEAR, tall, cw))
    return pl.pallas_call(
        functools.partial(grad_body, plan, dout, [len(c) for c in ctxs]),
        in_specs=[SM] + [VM] * (NEAR + sum(len(c) for c in ctxs)),
        out_specs=[VM, VM],
        out_shape=[block, block],
        compiler_params=params(),
        cost_estimate=pl.CostEstimate(
            flops=2 * NEAR * n_tensor * rows * feats * wide,
            bytes_accessed=2 * (NEAR * rows * (n_tensor * feats + wide) + n_tensor * feats * wide),
            transcendentals=0,
        ),
        name="gradient",
    )(info, *[part for parts in ctxs for part in parts], *grads)


def merge_body(in_block, feats, keep_ref, got_ref, *out_refs):
    n_y, n_far, tall, cw = keep_ref.shape
    if tall > feats:
        gains, scalars = block_sums(keep_ref[0, 0, feats:, :], in_block)
        more, others = block_sums(got_ref[0, 0, feats:, :], in_block)
        words = block_words(gains + more, scalars + others, tall - feats, cw)
    each = out_refs[0].shape[0] * out_refs[0].shape[1]
    for i in range(n_y * n_far):
        a, b = divmod(i, n_far)
        total = keep_ref[a, b, :feats, :].astype(F32) + got_ref[a, b, :feats, :].astype(F32)
        ref, at = out_refs[i // each], divmod(i % each, out_refs[0].shape[1])
        ref[(*at, slice(0, feats), slice(None))] = total.astype(BF)
        if tall > feats:
            ref[(*at, slice(feats, tall), slice(None))] = words


def merge(dims, dout, feats, keep, got):
    n_y, n_far, tall, cw = keep.shape
    outs = [shape((*dims, tall, cw))] * (n_y * n_far // math.prod(dims))
    return pl.pallas_call(
        functools.partial(merge_body, dout // cw, feats),
        in_specs=[VM, VM],
        out_specs=[VM] * len(outs),
        out_shape=outs,
        compiler_params=params(),
        cost_estimate=pl.CostEstimate(flops=keep.size, bytes_accessed=6 * keep.size, transcendentals=0),
        name="merge",
    )(keep, got)


def finish_body(counts, in_piece, n_far, *refs):
    grad_ref, gain_ref, loss_ref = refs[-3:]
    feats = grad_ref.shape[0]
    chunks, at = [], 0
    for n in counts:
        chunks.append(refs[at : at + n])
        at += n
    tall, cw = chunks[0][0].shape[2:]

    def total(blocks, rows):
        parts = [
            r[a, b, rows, :].astype(F32) for r in blocks for a in range(r.shape[0]) for b in range(r.shape[1])
        ]
        return sum(parts[1:], parts[0])

    gains, scalars = block_sums(total(chunks[0], slice(feats, tall)), in_piece * n_far)
    lane = lax.broadcasted_iota(jnp.int32, (1, cw), 1)
    weight = jnp.sum(jnp.where(lane == 1, scalars, 0.0), axis=1, keepdims=True)
    loss_ref[0, 0] = jnp.sum(jnp.where(lane == 0, scalars / weight, 0.0))
    gains = gains / weight
    for r in range(in_piece):
        for b in range(n_far):
            gain_ref[pl.ds(r * n_far + b, 1), :] = gains[b * in_piece + r : b * in_piece + r + 1, :]
    for j, blocks in enumerate(chunks):
        grad_ref[:, j * cw : (j + 1) * cw] = (total(blocks, slice(0, feats)) / weight).astype(BF)


def finish(plan, dout, feats, chunks):
    n_dp = plan[0]
    cw = chunks[0][0].shape[3]
    n_far = n_dp // NEAR
    return pl.pallas_call(
        functools.partial(finish_body, [len(c) for c in chunks], dout // (n_far * cw), n_far),
        in_specs=[VM] * sum(len(c) for c in chunks),
        out_specs=[VM, VM, SM],
        out_shape=[shape((feats, dout // n_dp)), shape((dout // cw, cw), F32), shape((1, 1), F32)],
        compiler_params=params(),
        name="finish",
    )(*[b for c in chunks for b in c])


def swap(x, axis, n, mask):
    return lax.ppermute(x, axis, [(i, i ^ mask) for i in range(n)])


def swap_far(x, n_dp, n_tensor, a, b):
    mask = b * NEAR * n_tensor + a * 2
    return lax.ppermute(x, ("dp", "tensor"), [(i, i ^ mask) for i in range(n_dp * n_tensor)])


def exchange_far(plan, two_steps, dout, feats, keep, got):
    n_dp, n_tensor, _, _, pairwise = plan
    n_y, n_far = n_tensor // 2, n_dp // NEAR
    if not pairwise:
        groups = [
            [(NEAR * f + q) * n_tensor + 2 * y + c for y in range(n_y) for f in range(n_far)]
            for q in range(NEAR)
            for c in range(2)
        ]
        (x,) = merge((n_y, n_far), dout, feats, keep, got)
        x = x.reshape(n_y * n_far, *x.shape[2:])
        x = lax.all_to_all(x, ("dp", "tensor"), 0, 0, tiled=True, axis_index_groups=groups)
        return [x.reshape(keep.shape)]

    def far(x, a, b):
        return swap_far(x, n_dp, n_tensor, a, b)

    if two_steps:
        own, across = merge((1, 2), dout, feats, keep, got)
        own, beyond = merge((1, 1), dout, feats, own, far(across, 1, 0))
        return [own, far(beyond, 0, 1)]
    blocks = merge((1, 1), dout, feats, keep, got)
    return [blocks[0], far(blocks[1], 0, 1), far(blocks[2], 1, 0), far(blocks[3], 1, 1)]


def gather_large(n_dp, n_tensor, _, weight, context):
    ctx = lax.all_to_all(context, "tensor", 0, 0, tiled=True)
    held = {0: weight}
    bit = n_tensor // 2
    while bit:
        held.update({m | bit: swap(w, "tensor", n_tensor, bit) for m, w in list(held.items())})
        bit //= 2
    ctxs = [[ctx]] + [[swap(ctx, "dp", n_dp, q)] for q in range(1, NEAR)]
    return ctx, ctxs, [[held[m]] for m in range(n_tensor)]


def gather_small(n_dp, n_tensor, side, weight, context):
    barrier = lax.optimization_barrier

    def dp(x, mask):
        return swap(x, "dp", n_dp, mask)

    def tensor(x, mask):
        return swap(x, "tensor", n_tensor, mask)

    dout = weight.shape[1]
    cut = dout // 4
    mine = tensor(lax.dynamic_slice_in_dim(weight, side * cut, cut, 1), 2)
    beside = tensor(weight, 1)
    rest = weight[:, 2 * cut :]
    mine, context = barrier((mine, context))
    other, mine_beside = dp(mine, 1), tensor(mine, 1)
    ctx = lax.all_to_all(context, "tensor", 0, 0, tiled=True)
    rest, other, mine_beside, beside, ctx = barrier((rest, other, mine_beside, beside, ctx))
    rest, other_beside = tensor(rest, 2), tensor(other, 1)
    ctx_x, ctx_z = dp(ctx, 1), dp(ctx, 2)
    rest, other_beside, ctx_x, ctx_z = barrier((rest, other_beside, ctx_x, ctx_z))
    half = ctx.shape[1] // 2
    ctxs = [[ctx], [ctx_x], [ctx_z], [dp(ctx_x[:, :half], 2), dp(ctx_z[:, half:], 1)]]
    far = [mine, other, rest]
    return ctx, ctxs, [[weight], [beside], far, [mine_beside, other_beside, tensor(rest, 1)]]


def on_device(
    n_dp,
    n_tensor,
    query_states,
    key_states,
    value_states,
    joining_weight,
    norm_gain,
    next_hidden,
    lengths,
    vote_counts,
):
    _, tokens, width = query_states.shape
    seq = tokens // lengths.shape[0]
    dout = norm_gain.shape[0]
    rows = next_hidden.shape[0]
    chunks = 2 if dout // n_dp >= 256 else 1
    xor_far = (n_tensor, n_dp // NEAR) == (4, 2)
    plan = (n_dp, n_tensor, chunks, seq, xor_far)
    me = lax.axis_index("tensor").astype(jnp.int32)
    group = lax.axis_index("dp").astype(jnp.int32)
    info = jnp.stack([me, group, lengths[0], vote_counts[0]])

    attended = attend(info, query_states[0], key_states[0], value_states[0], rows)
    gather = gather_small if xor_far else gather_large
    ctx, ctxs, weights = gather(n_dp, n_tensor, group & 1, joining_weight[0], attended)
    hidden, grads = join(plan, info, ctx, norm_gain[None, :], next_hidden, weights)
    parts = []
    for j in range(chunks):
        near = [grads[j][0]] + [swap(grads[j][q], "dp", n_dp, q) for q in range(1, NEAR)]
        keep, send = gradient(plan, dout, info, ctxs, near)
        got = swap(send, "tensor", n_tensor, 1)
        parts.append(exchange_far(plan, j == chunks - 1, dout, width, keep, got))
    weight_grad, gain_grad, loss = finish(plan, dout, width, parts)
    return (hidden, weight_grad[None], gain_grad.reshape(dout), loss.reshape(()))


def solution(mesh):
    return jax.shard_map(
        functools.partial(on_device, mesh.shape["dp"], mesh.shape["tensor"]),
        mesh=mesh,
        in_specs=(
            P(None, "dp", "tensor"),
            P(None, "dp", "tensor"),
            P(None, "dp", "tensor"),
            P(None, "tensor", None),
            P(),
            P(("dp", "tensor"), None),
            P("dp"),
            P("dp"),
        ),
        out_specs=(P(("dp", "tensor"), None), P(None, "tensor", "dp"), P(), P()),
        check_vma=False,
    )
```

```python
import functools
import math

import jax
import jax.numpy as jnp
from jax import lax
from jax.experimental import pallas as pl
from jax.experimental.pallas import tpu as pltpu
from jax.sharding import PartitionSpec as P

HD = 128
QB = 128
ROWS = 128
COLS = 256
NEAR = 4
STAT_ROWS = 32

loss_scale = 65536.0
neg_large = -1e30
MIB = 1 << 20
BF = jnp.bfloat16
F32 = jnp.float32


def dot(a, b, dims):
    return lax.dot_general(a, b, (dims, ((), ())), preferred_element_type=F32)


def split_words(x):
    high = x.astype(BF).astype(F32)
    return high, (x - high).astype(BF).astype(F32)


def shape(dims, dtype=BF):
    return jax.ShapeDtypeStruct(dims, dtype)


def params():
    return pltpu.CompilerParams(vmem_limit_bytes=32 * MIB)


VM = pl.BlockSpec(memory_space=pltpu.VMEM)
SM = pl.BlockSpec(memory_space=pltpu.SMEM)


def attend_body(info_ref, q_ref, k_ref, v_ref, o_ref):
    seq = q_ref.shape[0]
    rows = o_ref.shape[2]
    rate = math.log2(math.e) / math.sqrt(HD)
    length = info_ref[2]
    key = lax.broadcasted_iota(jnp.int32, (seq, 1), 0)
    hide = jnp.where(key < length, 0.0, neg_large)
    r = lax.broadcasted_iota(jnp.int32, (QB, QB), 0)
    c = lax.broadcasted_iota(jnp.int32, (QB, QB), 1)
    for h in range(q_ref.shape[1] // HD):
        at = slice(h * HD, (h + 1) * HD)
        q_t, v_t = q_ref[:, at].T, v_ref[:, at].T
        for i in range(seq // QB):
            keys = (i + 1) * QB
            scores = dot(k_ref[:keys, at], q_t[:, i * QB : keys], ((1,), (0,))) + hide[:keys]
            last = jnp.where(r <= c, scores[keys - QB :], neg_large)
            scores = last if i == 0 else jnp.concatenate([scores[: keys - QB], last], 0)
            peak = jnp.max(scores, axis=0, keepdims=True)
            e = jnp.exp2((scores - peak) * rate)
            total = jnp.sum(e, axis=0, keepdims=True)
            out = (dot(v_t[:, :keys], e.astype(BF), ((1,), (0,))) / total).astype(BF)
            for n in range(0, QB, min(rows, QB)):
                block, first = divmod(i * QB + n, rows)
                o_ref[block, at, first : first + min(rows, QB)] = out[:, n : n + rows]


def attend(info, q, k, v, rows):
    seq, width = q.shape
    heads = width // HD
    block = VM
    return pl.pallas_call(
        attend_body,
                in_specs=[SM, block, block, block],
        out_specs=VM,
        out_shape=shape((seq // rows, width, rows)),
        compiler_params=pltpu.CompilerParams(vmem_limit_bytes=60 * MIB),
        cost_estimate=pl.CostEstimate(
            flops=4 * seq * seq * width, bytes_accessed=8 * seq * width, transcendentals=heads * seq * seq
        ),
        name="attend",
    )(info, q, k, v)


def mix_body(n_tensor, counts, info_ref, ctx_ref, *refs):
    w_refs, at = [], 0
    for n in counts:
        w_refs.append(refs[at : at + n])
        at += n
    part_ref, square_ref, turned_ref = refs[at:]
    dout = part_ref.shape[1]
    me, side = info_ref[0], info_ref[1] % 2
    for m in range(n_tensor):
        turned_ref[m] = ctx_ref[me ^ m].T
    columns = [(c, 0, c) for c in range(0, dout, COLS)]
    if max(counts) > 1:
        cut = w_refs[-1][0].shape[1]
        columns = [(pl.multiple_of(side * cut + c, COLS), 0, c) for c in range(0, cut, COLS)]
        columns += [(pl.multiple_of((1 - side) * cut + c, COLS), 1, c) for c in range(0, cut, COLS)]
        columns += [(c, None, c) for c in range(2 * cut, dout, COLS)]
    for step, (start, piece, first) in enumerate(columns):
        to = pl.ds(start, COLS)
        total = None
        for m in range(n_tensor):
            whole = len(w_refs[m]) == 1
            if not whole and piece is None:
                continue
            w = w_refs[m][0][:, to] if whole else w_refs[m][piece][:, first : first + COLS]
            part = dot(turned_ref[m], w, ((1,), (0,)))
            total = part if total is None else total + part
        part_ref[:, to] = total
        if piece is not None:
            sq = total * total
            lanes = sum(sq[:, i : i + 128] for i in range(0, COLS, 128))
            square_ref[...] = lanes if step == 0 else square_ref[...] + lanes


def mix(info, ctx, weights):
    n_tensor, width, rows = ctx.shape
    dout = weights[0][0].shape[1]
    counts = [len(w) for w in weights]
    return pl.pallas_call(
        functools.partial(mix_body, n_tensor, counts),
        in_specs=[SM] + [VM] * (1 + sum(counts)),
        out_specs=[VM] * 3,
        out_shape=[shape((rows, dout), F32), shape((rows, 128), F32), shape((n_tensor, rows, width))],
        compiler_params=params(),
        cost_estimate=pl.CostEstimate(
            flops=2 * rows * dout * width * n_tensor,
            bytes_accessed=2 * dout * (width * n_tensor + 2 * rows),
            transcendentals=0,
        ),
        name="mix",
    )(info, ctx, *[w for held in weights for w in held])


def join_body(plan, n_late, info_ref, part_ref, early_ref, turned_ref, gain_ref, next_ref, *refs):
    n_dp, n_tensor, chunks, seq, xor_far = plan
    late_refs, hidden_ref, grad_refs = refs[:n_late], refs[n_late], refs[n_late + 1 : -4]
    joined_ref, square_ref, acc_ref, slope_ref = refs[-4:]
    rows, dout = joined_ref.shape
    step = acc_ref.shape[0]
    me, group, length, votes = info_ref[0], info_ref[1], info_ref[2], info_ref[3]
    near, far = group % NEAR, group // NEAR
    square_ref[...] = early_ref[...]
    ready = dout - late_refs[0].shape[1] if n_late else dout
    for c in range(ready, dout, COLS):
        total = part_ref[:, c : c + COLS]
        for m, ref in enumerate(late_refs, n_tensor - n_late):
            total += dot(turned_ref[m], ref[:, c - ready : c - ready + COLS], ((1,), (0,)))
        joined_ref[:, c : c + COLS] = total
        sq = total * total
        square_ref[...] += sum(sq[:, i : i + 128] for i in range(0, COLS, 128))
    acc_ref[...] = jnp.zeros_like(acc_ref)
    slice_w = dout // n_dp
    cw = slice_w // chunks
    n_far = n_dp // NEAR

    def body(r, carry):
        loss, weights = carry
        at = pl.ds(pl.multiple_of(r * step, step), step)
        inv = lax.rsqrt(jnp.sum(square_ref[at, :], axis=1, keepdims=True) * (1.0 / dout) + 1e-06)
        pos = (me * rows + r * step) % seq + lax.broadcasted_iota(jnp.int32, (step, 1), 0)
        weight = jnp.where(pos < length - 1, votes.astype(F32), 0.0)
        scaled = weight * (loss_scale * 2.0 / dout)
        miss = jnp.zeros((step, 128), F32)
        lean = jnp.zeros((step, 128), F32)
        for c in range(0, dout, 512):
            cs = slice(c, c + 512)
            normed = (part_ref if c < ready else joined_ref)[at, cs] * inv
            gain = gain_ref[:, cs]
            predicted = normed * gain
            hidden_ref[at, cs] = predicted.astype(BF)
            misfit = predicted - next_ref[at, cs].astype(F32)
            grad = scaled * misfit
            slope = grad * gain
            acc_ref[:, cs] += grad * normed
            slope_ref[:, cs] = slope
            sq = misfit * misfit
            ln = slope * normed
            miss += sum(sq[:, i : i + 128] for i in range(0, 512, 128))
            lean += sum(ln[:, i : i + 128] for i in range(0, 512, 128))
            joined_ref[at, cs] = normed
        lean = jnp.sum(lean, axis=1, keepdims=True) * (1.0 / dout)

        def gradient_at(cs):
            return (inv * (slope_ref[:, cs] - joined_ref[at, cs] * lean)).astype(BF)

        for j in range(chunks):
            for q in range(NEAR):
                for b in range(n_far):
                    to = slice(b * cw, (b + 1) * cw)
                    if cw % 128 == 0:
                        other = (far ^ b if xor_far else b) * NEAR + (near ^ q)
                        start = pl.multiple_of(other * slice_w + j * cw, 128)
                        grad_refs[j * NEAR + q][at, to] = gradient_at(pl.ds(start, cw))
                    else:
                        start = (b * NEAR + q) * slice_w + j * cw
                        grad_refs[j][near ^ q, at, to] = gradient_at(slice(start, start + cw))
        loss = loss + weight * (jnp.sum(miss, axis=1, keepdims=True) * (1.0 / dout))
        return loss, weights + weight

    zero = jnp.zeros((step, 1), F32)
    loss, weights = lax.fori_loop(0, rows // step, body, (zero, zero))
    wide = n_far * cw
    gain_sum = jnp.sum(acc_ref[...], axis=0, keepdims=True)
    gain_sum = jnp.concatenate([gain_sum[:, i : i + wide] for i in range(0, dout, wide)], 0)
    lane = lax.broadcasted_iota(jnp.int32, (1, wide), 1)
    loss = jnp.sum(loss, axis=0, keepdims=True)
    weights = jnp.sum(weights, axis=0, keepdims=True)
    scalars = jnp.where(lane == 0, loss, jnp.where(lane == 1, weights, 0.0))
    words = [*split_words(gain_sum), *split_words(scalars)]
    left = STAT_ROWS - sum(w.shape[0] for w in words)
    words = jnp.concatenate([*words, jnp.zeros((left, wide), F32)], 0).astype(BF)
    if cw % 128 == 0:
        for q in range(NEAR):
            grad_refs[q][rows:, :] = words
    else:
        for q in range(NEAR):
            grad_refs[0][q, rows:, :] = words


def join(plan, info, early, gain, next_hidden, late):
    n_dp, n_tensor, chunks, _, _ = plan
    _, rows, width = early[2].shape
    step = min(ROWS, rows)
    dout = gain.shape[1]
    wide = dout // NEAR // chunks
    tall = [rows + STAT_ROWS] + [rows] * (chunks - 1)
    aligned = dout // n_dp // chunks % 128 == 0
    if aligned:
        grads = [shape((n, wide)) for n in tall for _ in range(NEAR)]
    else:
        grads = [shape((NEAR, n, wide)) for n in tall]
    out = pl.pallas_call(
        functools.partial(join_body, plan, len(late)),
        in_specs=[SM] + [VM] * (5 + len(late)),
        out_specs=[VM] * (1 + len(grads)),
        out_shape=[shape((rows, dout)), *grads],
        scratch_shapes=[
            pltpu.VMEM((rows, dout), F32),
            pltpu.VMEM((rows, 128), F32),
            pltpu.VMEM((step, dout), F32),
            pltpu.VMEM((step, dout), F32),
        ],
        compiler_params=params(),
        cost_estimate=pl.CostEstimate(
            flops=rows * dout * width,
            bytes_accessed=2 * dout * (width + 5 * rows),
            transcendentals=rows,
        ),
        name="join",
    )(info, *early, gain, next_hidden, *late)
    if aligned:
        return out[0], [out[1 + j * NEAR : 1 + (j + 1) * NEAR] for j in range(chunks)]
    return out[0], [[g[q] for q in range(NEAR)] for g in out[1:]]


def stat_sizes(dout, wide, cw):
    in_block = dout // cw
    return dout // wide, in_block, -(-(2 * in_block + 2) // 16) * 16


def block_words(gains, scalars, tall, cw):
    words = [*split_words(gains), *split_words(scalars)]
    left = tall - sum(w.shape[0] for w in words)
    return jnp.concatenate([*words, jnp.zeros((left, cw), F32)], 0).astype(BF)


def block_sums(words, n):
    words = words.astype(F32)
    return words[:n] + words[n : 2 * n], words[2 * n : 2 * n + 1] + words[2 * n + 1 : 2 * n + 2]


def grad_body(plan, dout, counts, info_ref, *refs):
    n_dp, n_tensor, _, _, xor_far = plan
    keep_ref, send_ref = refs[-2:]
    ctx_refs, at = [], 0
    for n in counts:
        ctx_refs.append(refs[at : at + n])
        at += n
    g_refs = refs[at:-2]
    n_y, n_far, tall, cw = keep_ref.shape
    feats, rows = ctx_refs[0][0].shape[1:]
    wide = n_far * cw
    me = info_ref[0]
    core, y = me % 2, me // 2
    if tall > feats:
        in_piece, in_block, stat_rows = stat_sizes(dout, wide, cw)
        sums = sum(ref[rows:, :].astype(F32) for ref in g_refs)
        gains, scalars = block_sums(sums, in_piece)
        gains = jnp.concatenate([gains[:, b * cw : (b + 1) * cw] for b in range(n_far)], 0)
        words = block_words(gains, scalars[:, :cw], stat_rows, cw)
    for s, ref in ((1, send_ref), (0, keep_ref)):
        for a in range(n_y):
            m = (y ^ a if xor_far else a) * 2 + (core ^ s)
            total = None
            for parts, g in zip(ctx_refs, g_refs):
                c = jnp.concatenate([part[m] for part in parts], 0) if len(parts) > 1 else parts[0][m]
                part = dot(c, g[:rows, :], ((1,), (0,)))
                total = part if total is None else total + part
            total = total.astype(BF)
            for b in range(n_far):
                ref[a, b, :feats, :] = total[:, b * cw : (b + 1) * cw]
                if tall > feats:
                    ref[a, b, feats:, :] = words


def gradient(plan, dout, info, ctxs, grads):
    n_dp, n_tensor, chunks, _, _ = plan
    _, feats, rows = ctxs[0][0].shape
    wide = grads[0].shape[1]
    cw = dout // n_dp // chunks
    tall = feats
    if grads[0].shape[0] > rows:
        tall += stat_sizes(dout, wide, cw)[2]
    block = shape((n_tensor // 2, n_dp // NEAR, tall, cw))
    return pl.pallas_call(
        functools.partial(grad_body, plan, dout, [len(c) for c in ctxs]),
        in_specs=[SM] + [VM] * (NEAR + sum(len(c) for c in ctxs)),
        out_specs=[VM, VM],
        out_shape=[block, block],
        compiler_params=params(),
        cost_estimate=pl.CostEstimate(
            flops=2 * NEAR * n_tensor * rows * feats * wide,
            bytes_accessed=2 * (NEAR * rows * (n_tensor * feats + wide) + n_tensor * feats * wide),
            transcendentals=0,
        ),
        name="gradient",
    )(info, *[part for parts in ctxs for part in parts], *grads)


def merge_body(in_block, feats, keep_ref, got_ref, *out_refs):
    n_y, n_far, tall, cw = keep_ref.shape
    if tall > feats:
        gains, scalars = block_sums(keep_ref[0, 0, feats:, :], in_block)
        more, others = block_sums(got_ref[0, 0, feats:, :], in_block)
        words = block_words(gains + more, scalars + others, tall - feats, cw)
    each = out_refs[0].shape[0] * out_refs[0].shape[1]
    for i in range(n_y * n_far):
        a, b = divmod(i, n_far)
        total = keep_ref[a, b, :feats, :].astype(F32) + got_ref[a, b, :feats, :].astype(F32)
        ref, at = out_refs[i // each], divmod(i % each, out_refs[0].shape[1])
        ref[(*at, slice(0, feats), slice(None))] = total.astype(BF)
        if tall > feats:
            ref[(*at, slice(feats, tall), slice(None))] = words


def merge(dims, dout, feats, keep, got):
    n_y, n_far, tall, cw = keep.shape
    outs = [shape((*dims, tall, cw))] * (n_y * n_far // math.prod(dims))
    return pl.pallas_call(
        functools.partial(merge_body, dout // cw, feats),
        in_specs=[VM, VM],
        out_specs=[VM] * len(outs),
        out_shape=outs,
        compiler_params=params(),
        cost_estimate=pl.CostEstimate(flops=keep.size, bytes_accessed=6 * keep.size, transcendentals=0),
        name="merge",
    )(keep, got)


def finish_body(counts, in_piece, n_far, *refs):
    grad_ref, gain_ref, loss_ref = refs[-3:]
    feats = grad_ref.shape[0]
    chunks, at = [], 0
    for n in counts:
        chunks.append(refs[at : at + n])
        at += n
    tall, cw = chunks[0][0].shape[2:]

    def total(blocks, rows):
        parts = [
            r[a, b, rows, :].astype(F32) for r in blocks for a in range(r.shape[0]) for b in range(r.shape[1])
        ]
        return sum(parts[1:], parts[0])

    gains, scalars = block_sums(total(chunks[0], slice(feats, tall)), in_piece * n_far)
    lane = lax.broadcasted_iota(jnp.int32, (1, cw), 1)
    weight = jnp.sum(jnp.where(lane == 1, scalars, 0.0), axis=1, keepdims=True)
    loss_ref[0, 0] = jnp.sum(jnp.where(lane == 0, scalars / weight, 0.0))
    gains = gains / weight
    for r in range(in_piece):
        for b in range(n_far):
            gain_ref[pl.ds(r * n_far + b, 1), :] = gains[b * in_piece + r : b * in_piece + r + 1, :]
    for j, blocks in enumerate(chunks):
        grad_ref[:, j * cw : (j + 1) * cw] = (total(blocks, slice(0, feats)) / weight).astype(BF)


def finish(plan, dout, feats, chunks):
    n_dp = plan[0]
    cw = chunks[0][0].shape[3]
    n_far = n_dp // NEAR
    return pl.pallas_call(
        functools.partial(finish_body, [len(c) for c in chunks], dout // (n_far * cw), n_far),
        in_specs=[VM] * sum(len(c) for c in chunks),
        out_specs=[VM, VM, SM],
        out_shape=[shape((feats, dout // n_dp)), shape((dout // cw, cw), F32), shape((1, 1), F32)],
        compiler_params=params(),
        name="finish",
    )(*[b for c in chunks for b in c])


def swap(x, axis, n, mask):
    return lax.ppermute(x, axis, [(i, i ^ mask) for i in range(n)])


def swap_far(x, n_dp, n_tensor, a, b):
    mask = b * NEAR * n_tensor + a * 2
    return lax.ppermute(x, ("dp", "tensor"), [(i, i ^ mask) for i in range(n_dp * n_tensor)])


def exchange_far(plan, two_steps, dout, feats, keep, got):
    n_dp, n_tensor, _, _, pairwise = plan
    n_y, n_far = n_tensor // 2, n_dp // NEAR
    if not pairwise:
        groups = [
            [(NEAR * f + q) * n_tensor + 2 * y + c for y in range(n_y) for f in range(n_far)]
            for q in range(NEAR)
            for c in range(2)
        ]
        (x,) = merge((n_y, n_far), dout, feats, keep, got)
        x = x.reshape(n_y * n_far, *x.shape[2:])
        x = lax.all_to_all(x, ("dp", "tensor"), 0, 0, tiled=True, axis_index_groups=groups)
        return [x.reshape(keep.shape)]

    def far(x, a, b):
        return swap_far(x, n_dp, n_tensor, a, b)

    if two_steps:
        own, across = merge((1, 2), dout, feats, keep, got)
        own, beyond = merge((1, 1), dout, feats, own, far(across, 1, 0))
        return [own, far(beyond, 0, 1)]
    blocks = merge((1, 1), dout, feats, keep, got)
    return [blocks[0], far(blocks[1], 0, 1), far(blocks[2], 1, 0), far(blocks[3], 1, 1)]


def gather_large(n_dp, n_tensor, _, info, weight, context):
    ctx = lax.all_to_all(context, "tensor", 0, 0, tiled=True)
    held = {0: weight}
    bit = n_tensor // 2
    while bit:
        held.update({m | bit: swap(w, "tensor", n_tensor, bit) for m, w in list(held.items())})
        bit //= 2
    ctxs = [[ctx]] + [[swap(ctx, "dp", n_dp, q)] for q in range(1, NEAR)]
    return ctxs, mix(info, ctx, [[held[m]] for m in range(n_tensor)]), []


def gather_small(n_dp, n_tensor, side, info, weight, context):
    barrier = lax.optimization_barrier

    def dp(x, mask):
        return swap(x, "dp", n_dp, mask)

    def tensor(x, mask):
        return swap(x, "tensor", n_tensor, mask)

    dout = weight.shape[1]
    cut = dout // 4
    mine = tensor(lax.dynamic_slice_in_dim(weight, side * cut, cut, 1), 2)
    beside = tensor(weight, 1)
    rest = weight[:, 2 * cut :]
    mine, context = barrier((mine, context))
    other, mine_beside = dp(mine, 1), tensor(mine, 1)
    ctx = lax.all_to_all(context, "tensor", 0, 0, tiled=True)
    rest, other, mine_beside, beside, ctx = barrier((rest, other, mine_beside, beside, ctx))
    rest, other_beside = tensor(rest, 2), tensor(other, 1)
    ctx_x, ctx_z = dp(ctx, 1), dp(ctx, 2)
    early = mix(info, ctx, [[weight], [beside], [mine, other], [mine_beside, other_beside]])
    rest, early, ctx_x, ctx_z = barrier((rest, early, ctx_x, ctx_z))
    half = ctx.shape[1] // 2
    ctxs = [[ctx], [ctx_x], [ctx_z], [dp(ctx_x[:, :half], 2), dp(ctx_z[:, half:], 1)]]
    return ctxs, early, [rest, tensor(rest, 1)]


def on_device(
    n_dp,
    n_tensor,
    query_states,
    key_states,
    value_states,
    joining_weight,
    norm_gain,
    next_hidden,
    lengths,
    vote_counts,
):
    _, tokens, width = query_states.shape
    seq = tokens // lengths.shape[0]
    dout = norm_gain.shape[0]
    rows = next_hidden.shape[0]
    chunks = 2 if dout // n_dp >= 256 else 1
    xor_far = (n_tensor, n_dp // NEAR) == (4, 2)
    plan = (n_dp, n_tensor, chunks, seq, xor_far)
    me = lax.axis_index("tensor").astype(jnp.int32)
    group = lax.axis_index("dp").astype(jnp.int32)
    info = jnp.stack([me, group, lengths[0], vote_counts[0]])

    attended = attend(info, query_states[0], key_states[0], value_states[0], rows)
    gather = gather_small if xor_far else gather_large
    ctxs, early, late = gather(n_dp, n_tensor, group & 1, info, joining_weight[0], attended)
    hidden, grads = join(plan, info, early, norm_gain[None, :], next_hidden, late)
    parts = []
    for j in range(chunks):
        near = [grads[j][0]] + [swap(grads[j][q], "dp", n_dp, q) for q in range(1, NEAR)]
        keep, send = gradient(plan, dout, info, ctxs, near)
        got = swap(send, "tensor", n_tensor, 1)
        parts.append(exchange_far(plan, j == chunks - 1, dout, width, keep, got))
    weight_grad, gain_grad, loss = finish(plan, dout, width, parts)
    return (hidden, weight_grad[None], gain_grad.reshape(dout), loss.reshape(()))


def solution(mesh):
    return jax.shard_map(
        functools.partial(on_device, mesh.shape["dp"], mesh.shape["tensor"]),
        mesh=mesh,
        in_specs=(
            P(None, "dp", "tensor"),
            P(None, "dp", "tensor"),
            P(None, "dp", "tensor"),
            P(None, "tensor", None),
            P(),
            P(("dp", "tensor"), None),
            P("dp"),
            P("dp"),
        ),
        out_specs=(P(("dp", "tensor"), None), P(None, "tensor", "dp"), P(), P()),
        check_vma=False,
    )
```

```python
import functools
import math

import jax
import jax.numpy as jnp
from jax import lax
from jax.experimental import pallas as pl
from jax.experimental.pallas import tpu as pltpu
from jax.sharding import PartitionSpec as P

HD = 128
QB = 128
ROWS = 128
COLS = 256
NEAR = 4
STAT_ROWS = 32

loss_scale = 65536.0
neg_large = -1e30
MIB = 1 << 20
BF = jnp.bfloat16
F32 = jnp.float32


def dot(a, b, dims):
    return lax.dot_general(a, b, (dims, ((), ())), preferred_element_type=F32)


def split_words(x):
    high = x.astype(BF).astype(F32)
    return high, (x - high).astype(BF).astype(F32)


def shape(dims, dtype=BF):
    return jax.ShapeDtypeStruct(dims, dtype)


def params():
    return pltpu.CompilerParams(vmem_limit_bytes=32 * MIB)


VM = pl.BlockSpec(memory_space=pltpu.VMEM)
SM = pl.BlockSpec(memory_space=pltpu.SMEM)


def attend_body(len_ref, me_ref, q_ref, k_ref, v_ref, *out_refs):
    seq = q_ref.shape[0]
    o_ref = out_refs[-1]
    rows = o_ref.shape[2]
    rate = math.log2(math.e) / math.sqrt(HD)
    length = len_ref[0]
    key = lax.broadcasted_iota(jnp.int32, (seq, 1), 0)
    hide = jnp.where(key < length, 0.0, neg_large)
    r = lax.broadcasted_iota(jnp.int32, (QB, QB), 0)
    c = lax.broadcasted_iota(jnp.int32, (QB, QB), 1)
    for h in range(q_ref.shape[1] // HD):
        at = slice(h * HD, (h + 1) * HD)
        q_t, v_t = q_ref[:, at].T, v_ref[:, at].T
        for i in range(seq // QB):
            keys = (i + 1) * QB
            scores = dot(k_ref[:keys, at], q_t[:, i * QB : keys], ((1,), (0,))) + hide[:keys]
            last = jnp.where(r <= c, scores[keys - QB :], neg_large)
            scores = last if i == 0 else jnp.concatenate([scores[: keys - QB], last], 0)
            peak = jnp.max(scores, axis=0, keepdims=True)
            e = jnp.exp2((scores - peak) * rate)
            total = jnp.sum(e, axis=0, keepdims=True)
            out = (dot(v_t[:, :keys], e.astype(BF), ((1,), (0,))) / total).astype(BF)
            for n in range(0, QB, min(rows, QB)):
                block, first = divmod(i * QB + n, rows)
                o_ref[block, at, first : first + min(rows, QB)] = out[:, n : n + rows]
    for m, ref in enumerate(out_refs[:-1]):
        ref[...] = o_ref[me_ref[0] ^ m]


def attend(lengths, me, q, k, v, rows, split):
    seq, width = q.shape
    heads = width // HD
    blocks = seq // rows
    return pl.pallas_call(
        attend_body,
        in_specs=[SM, SM, VM, VM, VM],
        out_specs=[VM] * (blocks if split else 1),
        out_shape=[shape((width, rows))] * blocks if split else [shape((blocks, width, rows))],
        scratch_shapes=[pltpu.VMEM((blocks, width, rows), BF)] if split else [],
        compiler_params=pltpu.CompilerParams(vmem_limit_bytes=60 * MIB),
        cost_estimate=pl.CostEstimate(
            flops=4 * seq * seq * width, bytes_accessed=8 * seq * width, transcendentals=heads * seq * seq
        ),
        name="attend",
    )(lengths, me, q, k, v)


def mix_body(n_tensor, counts, split, info_ref, ctx_ref, *refs):
    w_refs, at = [], 0
    for n in counts:
        w_refs.append(refs[at : at + n])
        at += n
    part_ref, square_ref, turned_ref = refs[at:]
    dout = part_ref.shape[1]
    me, side = info_ref[0], info_ref[1] % 2
    for m in range(n_tensor):
        turned_ref[m] = ctx_ref[m if split else me ^ m].T
    columns = [(c, 0, c) for c in range(0, dout, COLS)]
    if max(counts) > 1:
        cut = w_refs[-1][0].shape[1]
        columns = [(pl.multiple_of(side * cut + c, COLS), 0, c) for c in range(0, cut, COLS)]
        columns += [(pl.multiple_of((1 - side) * cut + c, COLS), 1, c) for c in range(0, cut, COLS)]
        columns += [(c, None, c) for c in range(2 * cut, dout, COLS)]
    for step, (start, piece, first) in enumerate(columns):
        to = pl.ds(start, COLS)
        total = None
        for m in range(n_tensor):
            whole = len(w_refs[m]) == 1
            if not whole and piece is None:
                continue
            w = w_refs[m][0][:, to] if whole else w_refs[m][piece][:, first : first + COLS]
            part = dot(turned_ref[m], w, ((1,), (0,)))
            total = part if total is None else total + part
        part_ref[:, to] = total
        if piece is not None:
            sq = total * total
            lanes = sum(sq[:, i : i + 128] for i in range(0, COLS, 128))
            square_ref[...] = lanes if step == 0 else square_ref[...] + lanes


def mix(info, ctx, weights, split):
    n_tensor, width, rows = ctx.shape
    dout = weights[0][0].shape[1]
    counts = [len(w) for w in weights]
    return pl.pallas_call(
        functools.partial(mix_body, n_tensor, counts, split),
        in_specs=[SM] + [VM] * (1 + sum(counts)),
        out_specs=[VM] * 3,
        out_shape=[shape((rows, dout), F32), shape((rows, 128), F32), shape((n_tensor, rows, width))],
        compiler_params=params(),
        cost_estimate=pl.CostEstimate(
            flops=2 * rows * dout * width * n_tensor,
            bytes_accessed=2 * dout * (width * n_tensor + 2 * rows),
            transcendentals=0,
        ),
        name="mix",
    )(info, ctx, *[w for held in weights for w in held])


def join_body(plan, n_late, info_ref, part_ref, early_ref, turned_ref, gain_ref, next_ref, *refs):
    n_dp, n_tensor, chunks, seq, xor_far = plan
    late_refs, hidden_ref, grad_refs = refs[:n_late], refs[n_late], refs[n_late + 1 : -4]
    joined_ref, square_ref, acc_ref, slope_ref = refs[-4:]
    rows, dout = joined_ref.shape
    step = acc_ref.shape[0]
    me, group, length, votes = info_ref[0], info_ref[1], info_ref[2], info_ref[3]
    near, far = group % NEAR, group // NEAR
    square_ref[...] = early_ref[...]
    ready = dout - late_refs[0].shape[1] if n_late else dout
    for c in range(ready, dout, COLS):
        total = part_ref[:, c : c + COLS]
        for m, ref in enumerate(late_refs, n_tensor - n_late):
            total += dot(turned_ref[m], ref[:, c - ready : c - ready + COLS], ((1,), (0,)))
        joined_ref[:, c : c + COLS] = total
        sq = total * total
        square_ref[...] += sum(sq[:, i : i + 128] for i in range(0, COLS, 128))
    acc_ref[...] = jnp.zeros_like(acc_ref)
    slice_w = dout // n_dp
    cw = slice_w // chunks
    n_far = n_dp // NEAR

    def body(r, carry):
        loss, weights = carry
        at = pl.ds(pl.multiple_of(r * step, step), step)
        inv = lax.rsqrt(jnp.sum(square_ref[at, :], axis=1, keepdims=True) * (1.0 / dout) + 1e-06)
        pos = (me * rows + r * step) % seq + lax.broadcasted_iota(jnp.int32, (step, 1), 0)
        weight = jnp.where(pos < length - 1, votes.astype(F32), 0.0)
        scaled = weight * (loss_scale * 2.0 / dout)
        miss = jnp.zeros((step, 128), F32)
        lean = jnp.zeros((step, 128), F32)
        for c in range(0, dout, 512):
            cs = slice(c, c + 512)
            normed = (part_ref if c < ready else joined_ref)[at, cs] * inv
            gain = gain_ref[:, cs]
            predicted = normed * gain
            hidden_ref[at, cs] = predicted.astype(BF)
            misfit = predicted - next_ref[at, cs].astype(F32)
            grad = scaled * misfit
            slope = grad * gain
            acc_ref[:, cs] += grad * normed
            slope_ref[:, cs] = slope
            sq = misfit * misfit
            ln = slope * normed
            miss += sum(sq[:, i : i + 128] for i in range(0, 512, 128))
            lean += sum(ln[:, i : i + 128] for i in range(0, 512, 128))
            joined_ref[at, cs] = normed
        lean = jnp.sum(lean, axis=1, keepdims=True) * (1.0 / dout)

        def gradient_at(cs):
            return (inv * (slope_ref[:, cs] - joined_ref[at, cs] * lean)).astype(BF)

        for j in range(chunks):
            for q in range(NEAR):
                for b in range(n_far):
                    to = slice(b * cw, (b + 1) * cw)
                    if cw % 128 == 0:
                        other = (far ^ b if xor_far else b) * NEAR + (near ^ q)
                        start = pl.multiple_of(other * slice_w + j * cw, 128)
                        grad_refs[j * NEAR + q][at, to] = gradient_at(pl.ds(start, cw))
                    else:
                        start = (b * NEAR + q) * slice_w + j * cw
                        grad_refs[j][near ^ q, at, to] = gradient_at(slice(start, start + cw))
        loss = loss + weight * (jnp.sum(miss, axis=1, keepdims=True) * (1.0 / dout))
        return loss, weights + weight

    zero = jnp.zeros((step, 1), F32)
    loss, weights = lax.fori_loop(0, rows // step, body, (zero, zero))
    wide = n_far * cw
    gain_sum = jnp.sum(acc_ref[...], axis=0, keepdims=True)
    gain_sum = jnp.concatenate([gain_sum[:, i : i + wide] for i in range(0, dout, wide)], 0)
    lane = lax.broadcasted_iota(jnp.int32, (1, wide), 1)
    loss = jnp.sum(loss, axis=0, keepdims=True)
    weights = jnp.sum(weights, axis=0, keepdims=True)
    scalars = jnp.where(lane == 0, loss, jnp.where(lane == 1, weights, 0.0))
    words = [*split_words(gain_sum), *split_words(scalars)]
    left = STAT_ROWS - sum(w.shape[0] for w in words)
    words = jnp.concatenate([*words, jnp.zeros((left, wide), F32)], 0).astype(BF)
    if cw % 128 == 0:
        for q in range(NEAR):
            grad_refs[q][rows:, :] = words
    else:
        for q in range(NEAR):
            grad_refs[0][q, rows:, :] = words


def join(plan, info, early, gain, next_hidden, late):
    n_dp, n_tensor, chunks, _, _ = plan
    _, rows, width = early[2].shape
    step = min(ROWS, rows)
    dout = gain.shape[1]
    wide = dout // NEAR // chunks
    tall = [rows + STAT_ROWS] + [rows] * (chunks - 1)
    aligned = dout // n_dp // chunks % 128 == 0
    if aligned:
        grads = [shape((n, wide)) for n in tall for _ in range(NEAR)]
    else:
        grads = [shape((NEAR, n, wide)) for n in tall]
    out = pl.pallas_call(
        functools.partial(join_body, plan, len(late)),
        in_specs=[SM] + [VM] * (5 + len(late)),
        out_specs=[VM] * (1 + len(grads)),
        out_shape=[shape((rows, dout)), *grads],
        scratch_shapes=[
            pltpu.VMEM((rows, dout), F32),
            pltpu.VMEM((rows, 128), F32),
            pltpu.VMEM((step, dout), F32),
            pltpu.VMEM((step, dout), F32),
        ],
        compiler_params=params(),
        cost_estimate=pl.CostEstimate(
            flops=rows * dout * width,
            bytes_accessed=2 * dout * (width + 5 * rows),
            transcendentals=rows,
        ),
        name="join",
    )(info, *early, gain, next_hidden, *late)
    if aligned:
        return out[0], [out[1 + j * NEAR : 1 + (j + 1) * NEAR] for j in range(chunks)]
    return out[0], [[g[q] for q in range(NEAR)] for g in out[1:]]


def stat_sizes(dout, wide, cw):
    in_block = dout // cw
    return dout // wide, in_block, -(-(2 * in_block + 2) // 16) * 16


def block_words(gains, scalars, tall, cw):
    words = [*split_words(gains), *split_words(scalars)]
    left = tall - sum(w.shape[0] for w in words)
    return jnp.concatenate([*words, jnp.zeros((left, cw), F32)], 0).astype(BF)


def block_sums(words, n):
    words = words.astype(F32)
    return words[:n] + words[n : 2 * n], words[2 * n : 2 * n + 1] + words[2 * n + 1 : 2 * n + 2]


def grad_body(plan, dout, counts, info_ref, *refs):
    n_dp, n_tensor, _, _, xor_far = plan
    keep_ref, send_ref = refs[-2:]
    ctx_refs, at = [], 0
    for n in counts:
        ctx_refs.append(refs[at : at + n])
        at += n
    g_refs = refs[at:-2]
    n_y, n_far, tall, cw = keep_ref.shape
    feats, rows = ctx_refs[0][0].shape[1:]
    wide = n_far * cw
    me = info_ref[0]
    core = me % 2
    if tall > feats:
        in_piece, in_block, stat_rows = stat_sizes(dout, wide, cw)
        sums = sum(ref[rows:, :].astype(F32) for ref in g_refs)
        gains, scalars = block_sums(sums, in_piece)
        gains = jnp.concatenate([gains[:, b * cw : (b + 1) * cw] for b in range(n_far)], 0)
        words = block_words(gains, scalars[:, :cw], stat_rows, cw)
    for s, ref in ((1, send_ref), (0, keep_ref)):
        for a in range(n_y):
            m = a * 2 + (s if xor_far else core ^ s)
            total = None
            for parts, g in zip(ctx_refs, g_refs):
                c = jnp.concatenate([part[m] for part in parts], 0) if len(parts) > 1 else parts[0][m]
                part = dot(c, g[:rows, :], ((1,), (0,)))
                total = part if total is None else total + part
            total = total.astype(BF)
            for b in range(n_far):
                ref[a, b, :feats, :] = total[:, b * cw : (b + 1) * cw]
                if tall > feats:
                    ref[a, b, feats:, :] = words


def gradient(plan, dout, info, ctxs, grads):
    n_dp, n_tensor, chunks, _, _ = plan
    _, feats, rows = ctxs[0][0].shape
    wide = grads[0].shape[1]
    cw = dout // n_dp // chunks
    tall = feats
    if grads[0].shape[0] > rows:
        tall += stat_sizes(dout, wide, cw)[2]
    block = shape((n_tensor // 2, n_dp // NEAR, tall, cw))
    return pl.pallas_call(
        functools.partial(grad_body, plan, dout, [len(c) for c in ctxs]),
        in_specs=[SM] + [VM] * (NEAR + sum(len(c) for c in ctxs)),
        out_specs=[VM, VM],
        out_shape=[block, block],
        compiler_params=params(),
        cost_estimate=pl.CostEstimate(
            flops=2 * NEAR * n_tensor * rows * feats * wide,
            bytes_accessed=2 * (NEAR * rows * (n_tensor * feats + wide) + n_tensor * feats * wide),
            transcendentals=0,
        ),
        name="gradient",
    )(info, *[part for parts in ctxs for part in parts], *grads)


def merge_body(in_block, feats, keep_ref, got_ref, *out_refs):
    n_y, n_far, tall, cw = keep_ref.shape
    if tall > feats:
        gains, scalars = block_sums(keep_ref[0, 0, feats:, :], in_block)
        more, others = block_sums(got_ref[0, 0, feats:, :], in_block)
        words = block_words(gains + more, scalars + others, tall - feats, cw)
    each = out_refs[0].shape[0] * out_refs[0].shape[1]
    for i in range(n_y * n_far):
        a, b = divmod(i, n_far)
        total = keep_ref[a, b, :feats, :].astype(F32) + got_ref[a, b, :feats, :].astype(F32)
        ref, at = out_refs[i // each], divmod(i % each, out_refs[0].shape[1])
        ref[(*at, slice(0, feats), slice(None))] = total.astype(BF)
        if tall > feats:
            ref[(*at, slice(feats, tall), slice(None))] = words


def merge(dims, dout, feats, keep, got):
    n_y, n_far, tall, cw = keep.shape
    outs = [shape((*dims, tall, cw))] * (n_y * n_far // math.prod(dims))
    return pl.pallas_call(
        functools.partial(merge_body, dout // cw, feats),
        in_specs=[VM, VM],
        out_specs=[VM] * len(outs),
        out_shape=outs,
        compiler_params=params(),
        cost_estimate=pl.CostEstimate(flops=keep.size, bytes_accessed=6 * keep.size, transcendentals=0),
        name="merge",
    )(keep, got)


def finish_body(counts, in_piece, n_far, *refs):
    grad_ref, gain_ref, loss_ref = refs[-3:]
    feats = grad_ref.shape[0]
    chunks, at = [], 0
    for n in counts:
        chunks.append(refs[at : at + n])
        at += n
    tall, cw = chunks[0][0].shape[2:]

    def total(blocks, rows):
        parts = [
            r[a, b, rows, :].astype(F32) for r in blocks for a in range(r.shape[0]) for b in range(r.shape[1])
        ]
        return sum(parts[1:], parts[0])

    gains, scalars = block_sums(total(chunks[0], slice(feats, tall)), in_piece * n_far)
    lane = lax.broadcasted_iota(jnp.int32, (1, cw), 1)
    weight = jnp.sum(jnp.where(lane == 1, scalars, 0.0), axis=1, keepdims=True)
    loss_ref[0, 0] = jnp.sum(jnp.where(lane == 0, scalars / weight, 0.0))
    gains = gains / weight
    for r in range(in_piece):
        for b in range(n_far):
            gain_ref[pl.ds(r * n_far + b, 1), :] = gains[b * in_piece + r : b * in_piece + r + 1, :]
    for j, blocks in enumerate(chunks):
        grad_ref[:, j * cw : (j + 1) * cw] = (total(blocks, slice(0, feats)) / weight).astype(BF)


def finish(plan, dout, feats, chunks):
    n_dp = plan[0]
    cw = chunks[0][0].shape[3]
    n_far = n_dp // NEAR
    return pl.pallas_call(
        functools.partial(finish_body, [len(c) for c in chunks], dout // (n_far * cw), n_far),
        in_specs=[VM] * sum(len(c) for c in chunks),
        out_specs=[VM, VM, SM],
        out_shape=[shape((feats, dout // n_dp)), shape((dout // cw, cw), F32), shape((1, 1), F32)],
        compiler_params=params(),
        name="finish",
    )(*[b for c in chunks for b in c])


def swap(x, axis, n, mask):
    return lax.ppermute(x, axis, [(i, i ^ mask) for i in range(n)])


def swap_far(x, n_dp, n_tensor, a, b):
    mask = b * NEAR * n_tensor + a * 2
    return lax.ppermute(x, ("dp", "tensor"), [(i, i ^ mask) for i in range(n_dp * n_tensor)])


def exchange_far(plan, two_steps, dout, feats, keep, got):
    n_dp, n_tensor, _, _, pairwise = plan
    n_y, n_far = n_tensor // 2, n_dp // NEAR
    if not pairwise:
        groups = [
            [(NEAR * f + q) * n_tensor + 2 * y + c for y in range(n_y) for f in range(n_far)]
            for q in range(NEAR)
            for c in range(2)
        ]
        (x,) = merge((n_y, n_far), dout, feats, keep, got)
        x = x.reshape(n_y * n_far, *x.shape[2:])
        x = lax.all_to_all(x, ("dp", "tensor"), 0, 0, tiled=True, axis_index_groups=groups)
        return [x.reshape(keep.shape)]

    def far(x, a, b):
        return swap_far(x, n_dp, n_tensor, a, b)

    if two_steps:
        own, across = merge((1, 2), dout, feats, keep, got)
        own, beyond = merge((1, 1), dout, feats, own, far(across, 1, 0))
        return [own, far(beyond, 0, 1)]
    blocks = merge((1, 1), dout, feats, keep, got)
    return [blocks[0], far(blocks[1], 0, 1), far(blocks[2], 1, 0), far(blocks[3], 1, 1)]


def gather_large(n_dp, n_tensor, _, info, weight, context):
    ctx = lax.all_to_all(context[0], "tensor", 0, 0, tiled=True)
    held = {0: weight}
    bit = n_tensor // 2
    while bit:
        held.update({m | bit: swap(w, "tensor", n_tensor, bit) for m, w in list(held.items())})
        bit //= 2
    ctxs = [[ctx]] + [[swap(ctx, "dp", n_dp, q)] for q in range(1, NEAR)]
    return ctxs, mix(info, ctx, [[held[m]] for m in range(n_tensor)], False), []


def gather_small(n_dp, n_tensor, side, info, weight, context):
    barrier = lax.optimization_barrier

    def dp(x, mask):
        return swap(x, "dp", n_dp, mask)

    def tensor(x, mask):
        return swap(x, "tensor", n_tensor, mask)

    dout = weight.shape[1]
    cut = dout // 4
    mine = tensor(lax.dynamic_slice_in_dim(weight, side * cut, cut, 1), 2)
    beside = tensor(weight, 1)
    rest = weight[:, 2 * cut :]
    mine, beside, context = barrier((mine, beside, context))
    ctx = jnp.stack([context[0]] + [tensor(context[m], m) for m in range(1, n_tensor)])
    other, mine_beside = dp(mine, 1), tensor(mine, 1)
    rest, other, mine_beside, ctx = barrier((rest, other, mine_beside, ctx))
    rest, other_beside = tensor(rest, 2), tensor(other, 1)
    ctx_x, ctx_z = dp(ctx, 1), dp(ctx, 2)
    early = mix(info, ctx, [[weight], [beside], [mine, other], [mine_beside, other_beside]], True)
    rest, early, ctx_x, ctx_z = barrier((rest, early, ctx_x, ctx_z))
    half = ctx.shape[1] // 2
    ctxs = [[ctx], [ctx_x], [ctx_z], [dp(ctx_x[:, :half], 2), dp(ctx_z[:, half:], 1)]]
    return ctxs, early, [rest, tensor(rest, 1)]


def on_device(
    n_dp,
    n_tensor,
    query_states,
    key_states,
    value_states,
    joining_weight,
    norm_gain,
    next_hidden,
    lengths,
    vote_counts,
):
    _, tokens, width = query_states.shape
    seq = tokens // lengths.shape[0]
    dout = norm_gain.shape[0]
    rows = next_hidden.shape[0]
    chunks = 2 if dout // n_dp >= 256 else 1
    xor_far = (n_tensor, n_dp // NEAR) == (4, 2)
    plan = (n_dp, n_tensor, chunks, seq, xor_far)
    me = lax.axis_index("tensor").astype(jnp.int32)
    group = lax.axis_index("dp").astype(jnp.int32)
    info = jnp.stack([me, group, lengths[0], vote_counts[0]])

    attended = attend(lengths, me.reshape(1), query_states[0], key_states[0], value_states[0], rows, xor_far)
    gather = gather_small if xor_far else gather_large
    ctxs, early, late = gather(n_dp, n_tensor, group & 1, info, joining_weight[0], attended)
    hidden, grads = join(plan, info, early, norm_gain[None, :], next_hidden, late)
    parts = []
    for j in range(chunks):
        near = [grads[j][0]] + [swap(grads[j][q], "dp", n_dp, q) for q in range(1, NEAR)]
        keep, send = gradient(plan, dout, info, ctxs, near)
        got = swap(send, "tensor", n_tensor, 1)
        parts.append(exchange_far(plan, j == chunks - 1, dout, width, keep, got))
    weight_grad, gain_grad, loss = finish(plan, dout, width, parts)
    return (hidden, weight_grad[None], gain_grad.reshape(dout), loss.reshape(()))


def solution(mesh):
    return jax.shard_map(
        functools.partial(on_device, mesh.shape["dp"], mesh.shape["tensor"]),
        mesh=mesh,
        in_specs=(
            P(None, "dp", "tensor"),
            P(None, "dp", "tensor"),
            P(None, "dp", "tensor"),
            P(None, "tensor", None),
            P(),
            P(("dp", "tensor"), None),
            P("dp"),
            P("dp"),
        ),
        out_specs=(P(("dp", "tensor"), None), P(None, "tensor", "dp"), P(), P()),
        check_vma=False,
    )
```

```python
import functools
import math

import jax
import jax.numpy as jnp
from jax import lax
from jax.experimental import pallas as pl
from jax.experimental.pallas import tpu as pltpu
from jax.sharding import PartitionSpec as P

HD = 128
QB = 128
ROWS = 128
COLS = 256
NEAR = 4
STAT_ROWS = 32

loss_scale = 65536.0
neg_large = -1e30
MIB = 1 << 20
BF = jnp.bfloat16
F32 = jnp.float32


def dot(a, b, dims):
    return lax.dot_general(a, b, (dims, ((), ())), preferred_element_type=F32)


def split_words(x):
    high = x.astype(BF).astype(F32)
    return high, (x - high).astype(BF).astype(F32)


def shape(dims, dtype=BF):
    return jax.ShapeDtypeStruct(dims, dtype)


def params():
    return pltpu.CompilerParams(vmem_limit_bytes=32 * MIB)


VM = pl.BlockSpec(memory_space=pltpu.VMEM)
SM = pl.BlockSpec(memory_space=pltpu.SMEM)


def attend_body(len_ref, me_ref, q_ref, k_ref, v_ref, *out_refs):
    seq = q_ref.shape[0]
    o_ref = out_refs[-1]
    rows = o_ref.shape[2]
    rate = math.log2(math.e) / math.sqrt(HD)
    length = len_ref[0]
    key = lax.broadcasted_iota(jnp.int32, (seq, 1), 0)
    hide = jnp.where(key < length, 0.0, neg_large)
    r = lax.broadcasted_iota(jnp.int32, (QB, QB), 0)
    c = lax.broadcasted_iota(jnp.int32, (QB, QB), 1)
    for h in range(q_ref.shape[1] // HD):
        at = slice(h * HD, (h + 1) * HD)
        q_t, v_t = q_ref[:, at].T, v_ref[:, at].T
        for i in range(seq // QB):
            keys = (i + 1) * QB
            scores = dot(k_ref[:keys, at], q_t[:, i * QB : keys], ((1,), (0,))) + hide[:keys]
            last = jnp.where(r <= c, scores[keys - QB :], neg_large)
            scores = last if i == 0 else jnp.concatenate([scores[: keys - QB], last], 0)
            peak = jnp.max(scores, axis=0, keepdims=True)
            e = jnp.exp2((scores - peak) * rate)
            total = jnp.sum(e, axis=0, keepdims=True)
            out = (dot(v_t[:, :keys], e.astype(BF), ((1,), (0,))) / total).astype(BF)
            for n in range(0, QB, min(rows, QB)):
                block, first = divmod(i * QB + n, rows)
                o_ref[block, at, first : first + min(rows, QB)] = out[:, n : n + rows]
    for m, ref in enumerate(out_refs[:-1]):
        ref[...] = o_ref[me_ref[0] ^ m]


def attend(lengths, me, q, k, v, rows, split):
    seq, width = q.shape
    heads = width // HD
    blocks = seq // rows
    return pl.pallas_call(
        attend_body,
        in_specs=[SM, SM, VM, VM, VM],
        out_specs=[VM] * (blocks if split else 1),
        out_shape=[shape((width, rows))] * blocks if split else [shape((blocks, width, rows))],
        scratch_shapes=[pltpu.VMEM((blocks, width, rows), BF)] if split else [],
        compiler_params=pltpu.CompilerParams(vmem_limit_bytes=60 * MIB),
        cost_estimate=pl.CostEstimate(
            flops=4 * seq * seq * width, bytes_accessed=8 * seq * width, transcendentals=heads * seq * seq
        ),
        name="attend",
    )(lengths, me, q, k, v)


def mix_body(n_tensor, counts, split, info_ref, ctx_ref, *refs):
    w_refs, at = [], 0
    for n in counts:
        w_refs.append(refs[at : at + n])
        at += n
    part_ref, square_ref, turned_ref = refs[at:]
    dout = part_ref.shape[1]
    me, side = info_ref[0], info_ref[1] % 2
    for m in range(n_tensor):
        turned_ref[m] = ctx_ref[m if split else me ^ m].T
    columns = [(c, 0, c) for c in range(0, dout, COLS)]
    if max(counts) > 1:
        cut = w_refs[-1][0].shape[1]
        columns = [(pl.multiple_of(side * cut + c, COLS), 0, c) for c in range(0, cut, COLS)]
        columns += [(pl.multiple_of((1 - side) * cut + c, COLS), 1, c) for c in range(0, cut, COLS)]
        columns += [(c, None, c) for c in range(2 * cut, dout, COLS)]
    for step, (start, piece, first) in enumerate(columns):
        to = pl.ds(start, COLS)
        total = None
        for m in range(n_tensor):
            whole = len(w_refs[m]) == 1
            if not whole and piece is None:
                continue
            w = w_refs[m][0][:, to] if whole else w_refs[m][piece][:, first : first + COLS]
            part = dot(turned_ref[m], w, ((1,), (0,)))
            total = part if total is None else total + part
        part_ref[:, to] = total
        if piece is not None:
            sq = total * total
            lanes = sum(sq[:, i : i + 128] for i in range(0, COLS, 128))
            square_ref[...] = lanes if step == 0 else square_ref[...] + lanes


def mix(info, ctx, weights, split):
    n_tensor, width, rows = ctx.shape
    dout = weights[0][0].shape[1]
    counts = [len(w) for w in weights]
    return pl.pallas_call(
        functools.partial(mix_body, n_tensor, counts, split),
        in_specs=[SM] + [VM] * (1 + sum(counts)),
        out_specs=[VM] * 3,
        out_shape=[shape((rows, dout), F32), shape((rows, 128), F32), shape((n_tensor, rows, width))],
        compiler_params=params(),
        cost_estimate=pl.CostEstimate(
            flops=2 * rows * dout * width * n_tensor,
            bytes_accessed=2 * dout * (width * n_tensor + 2 * rows),
            transcendentals=0,
        ),
        name="mix",
    )(info, ctx, *[w for held in weights for w in held])


def join_body(plan, n_late, info_ref, part_ref, early_ref, turned_ref, gain_ref, next_ref, *refs):
    n_dp, n_tensor, chunks, seq, xor_far = plan
    late_refs, hidden_ref, grad_refs = refs[:n_late], refs[n_late], refs[n_late + 1 : -4]
    joined_ref, square_ref, acc_ref, slope_ref = refs[-4:]
    rows, dout = joined_ref.shape
    step = acc_ref.shape[0]
    me, group, length, votes = info_ref[0], info_ref[1], info_ref[2], info_ref[3]
    near, far = group % NEAR, group // NEAR
    square_ref[...] = early_ref[...]
    ready = dout - late_refs[0].shape[1] if n_late else dout
    for c in range(ready, dout, COLS):
        total = part_ref[:, c : c + COLS]
        for m, ref in enumerate(late_refs, n_tensor - n_late):
            total += dot(turned_ref[m], ref[:, c - ready : c - ready + COLS], ((1,), (0,)))
        joined_ref[:, c : c + COLS] = total
        sq = total * total
        square_ref[...] += sum(sq[:, i : i + 128] for i in range(0, COLS, 128))
    acc_ref[...] = jnp.zeros_like(acc_ref)
    slice_w = dout // n_dp
    cw = slice_w // chunks
    n_far = n_dp // NEAR

    def body(r, carry):
        loss, weights = carry
        at = pl.ds(pl.multiple_of(r * step, step), step)
        inv = lax.rsqrt(jnp.sum(square_ref[at, :], axis=1, keepdims=True) * (1.0 / dout) + 1e-06)
        pos = (me * rows + r * step) % seq + lax.broadcasted_iota(jnp.int32, (step, 1), 0)
        weight = jnp.where(pos < length - 1, votes.astype(F32), 0.0)
        scaled = weight * (loss_scale * 2.0 / dout)
        miss = jnp.zeros((step, 128), F32)
        lean = jnp.zeros((step, 128), F32)
        for c in range(0, dout, 512):
            cs = slice(c, c + 512)
            normed = (part_ref if c < ready else joined_ref)[at, cs] * inv
            gain = gain_ref[:, cs]
            predicted = normed * gain
            hidden_ref[at, cs] = predicted.astype(BF)
            misfit = predicted - next_ref[at, cs].astype(F32)
            grad = scaled * misfit
            slope = grad * gain
            acc_ref[:, cs] += grad * normed
            slope_ref[:, cs] = slope
            sq = misfit * misfit
            ln = slope * normed
            miss += sum(sq[:, i : i + 128] for i in range(0, 512, 128))
            lean += sum(ln[:, i : i + 128] for i in range(0, 512, 128))
            joined_ref[at, cs] = normed
        lean = jnp.sum(lean, axis=1, keepdims=True) * (1.0 / dout)

        def gradient_at(cs):
            return (inv * (slope_ref[:, cs] - joined_ref[at, cs] * lean)).astype(BF)

        for j in range(chunks):
            for q in range(NEAR):
                for b in range(n_far):
                    to = slice(b * cw, (b + 1) * cw)
                    if cw % 128 == 0:
                        other = (far ^ b if xor_far else b) * NEAR + (near ^ q)
                        start = pl.multiple_of(other * slice_w + j * cw, 128)
                        grad_refs[j * NEAR + q][at, to] = gradient_at(pl.ds(start, cw))
                    else:
                        start = (b * NEAR + q) * slice_w + j * cw
                        grad_refs[j][near ^ q, at, to] = gradient_at(slice(start, start + cw))
        loss = loss + weight * (jnp.sum(miss, axis=1, keepdims=True) * (1.0 / dout))
        return loss, weights + weight

    zero = jnp.zeros((step, 1), F32)
    loss, weights = lax.fori_loop(0, rows // step, body, (zero, zero))
    wide = n_far * cw
    gain_sum = jnp.sum(acc_ref[...], axis=0, keepdims=True)
    gain_sum = jnp.concatenate([gain_sum[:, i : i + wide] for i in range(0, dout, wide)], 0)
    lane = lax.broadcasted_iota(jnp.int32, (1, wide), 1)
    loss = jnp.sum(loss, axis=0, keepdims=True)
    weights = jnp.sum(weights, axis=0, keepdims=True)
    scalars = jnp.where(lane == 0, loss, jnp.where(lane == 1, weights, 0.0))
    words = [*split_words(gain_sum), *split_words(scalars)]
    left = STAT_ROWS - sum(w.shape[0] for w in words)
    words = jnp.concatenate([*words, jnp.zeros((left, wide), F32)], 0).astype(BF)
    if cw % 128 == 0:
        for q in range(NEAR):
            grad_refs[q][rows:, :] = words
    else:
        for q in range(NEAR):
            grad_refs[0][q, rows:, :] = words


def join(plan, info, early, gain, next_hidden, late):
    n_dp, n_tensor, chunks, _, _ = plan
    _, rows, width = early[2].shape
    step = min(ROWS, rows)
    dout = gain.shape[1]
    wide = dout // NEAR // chunks
    tall = [rows + STAT_ROWS] + [rows] * (chunks - 1)
    aligned = dout // n_dp // chunks % 128 == 0
    if aligned:
        grads = [shape((n, wide)) for n in tall for _ in range(NEAR)]
    else:
        grads = [shape((NEAR, n, wide)) for n in tall]
    out = pl.pallas_call(
        functools.partial(join_body, plan, len(late)),
        in_specs=[SM] + [VM] * (5 + len(late)),
        out_specs=[VM] * (1 + len(grads)),
        out_shape=[shape((rows, dout)), *grads],
        scratch_shapes=[
            pltpu.VMEM((rows, dout), F32),
            pltpu.VMEM((rows, 128), F32),
            pltpu.VMEM((step, dout), F32),
            pltpu.VMEM((step, dout), F32),
        ],
        compiler_params=params(),
        cost_estimate=pl.CostEstimate(
            flops=rows * dout * width,
            bytes_accessed=2 * dout * (width + 5 * rows),
            transcendentals=rows,
        ),
        name="join",
    )(info, *early, gain, next_hidden, *late)
    if aligned:
        return out[0], [out[1 + j * NEAR : 1 + (j + 1) * NEAR] for j in range(chunks)]
    return out[0], [[g[q] for q in range(NEAR)] for g in out[1:]]


def stat_sizes(dout, wide, cw):
    in_block = dout // cw
    return dout // wide, in_block, -(-(2 * in_block + 2) // 16) * 16


def block_words(gains, scalars, tall, cw):
    words = [*split_words(gains), *split_words(scalars)]
    left = tall - sum(w.shape[0] for w in words)
    return jnp.concatenate([*words, jnp.zeros((left, cw), F32)], 0).astype(BF)


def block_sums(words, n):
    words = words.astype(F32)
    return words[:n] + words[n : 2 * n], words[2 * n : 2 * n + 1] + words[2 * n + 1 : 2 * n + 2]


def grad_body(plan, dout, counts, info_ref, *refs):
    n_dp, n_tensor, _, _, xor_far = plan
    keep_ref, send_ref = refs[-2:]
    ctx_refs, at = [], 0
    for n in counts:
        ctx_refs.append(refs[at : at + n])
        at += n
    g_refs = refs[at:-2]
    n_y, n_far, tall, cw = keep_ref.shape
    feats, rows = ctx_refs[0][0].shape[1:]
    wide = n_far * cw
    me = info_ref[0]
    core = me % 2
    if tall > feats:
        in_piece, in_block, stat_rows = stat_sizes(dout, wide, cw)
        sums = sum(ref[rows:, :].astype(F32) for ref in g_refs)
        gains, scalars = block_sums(sums, in_piece)
        gains = jnp.concatenate([gains[:, b * cw : (b + 1) * cw] for b in range(n_far)], 0)
        words = block_words(gains, scalars[:, :cw], stat_rows, cw)
    for s, ref in ((1, send_ref), (0, keep_ref)):
        for a in range(n_y):
            m = a * 2 + (s if xor_far else core ^ s)
            total = None
            for parts, g in zip(ctx_refs, g_refs):
                c = jnp.concatenate([part[m] for part in parts], 0) if len(parts) > 1 else parts[0][m]
                part = dot(c, g[:rows, :], ((1,), (0,)))
                total = part if total is None else total + part
            total = total.astype(BF)
            for b in range(n_far):
                ref[a, b, :feats, :] = total[:, b * cw : (b + 1) * cw]
                if tall > feats:
                    ref[a, b, feats:, :] = words


def gradient(plan, dout, info, ctxs, grads):
    n_dp, n_tensor, chunks, _, _ = plan
    _, feats, rows = ctxs[0][0].shape
    wide = grads[0].shape[1]
    cw = dout // n_dp // chunks
    tall = feats
    if grads[0].shape[0] > rows:
        tall += stat_sizes(dout, wide, cw)[2]
    block = shape((n_tensor // 2, n_dp // NEAR, tall, cw))
    return pl.pallas_call(
        functools.partial(grad_body, plan, dout, [len(c) for c in ctxs]),
        in_specs=[SM] + [VM] * (NEAR + sum(len(c) for c in ctxs)),
        out_specs=[VM, VM],
        out_shape=[block, block],
        compiler_params=params(),
        cost_estimate=pl.CostEstimate(
            flops=2 * NEAR * n_tensor * rows * feats * wide,
            bytes_accessed=2 * (NEAR * rows * (n_tensor * feats + wide) + n_tensor * feats * wide),
            transcendentals=0,
        ),
        name="gradient",
    )(info, *[part for parts in ctxs for part in parts], *grads)


def merge_body(in_block, feats, keep_ref, got_ref, *out_refs):
    n_y, n_far, tall, cw = keep_ref.shape
    if tall > feats:
        gains, scalars = block_sums(keep_ref[0, 0, feats:, :], in_block)
        more, others = block_sums(got_ref[0, 0, feats:, :], in_block)
        words = block_words(gains + more, scalars + others, tall - feats, cw)
    each = out_refs[0].shape[0] * out_refs[0].shape[1]
    for i in range(n_y * n_far):
        a, b = divmod(i, n_far)
        total = keep_ref[a, b, :feats, :].astype(F32) + got_ref[a, b, :feats, :].astype(F32)
        ref, at = out_refs[i // each], divmod(i % each, out_refs[0].shape[1])
        ref[(*at, slice(0, feats), slice(None))] = total.astype(BF)
        if tall > feats:
            ref[(*at, slice(feats, tall), slice(None))] = words


def merge(dims, dout, feats, keep, got):
    n_y, n_far, tall, cw = keep.shape
    outs = [shape((*dims, tall, cw))] * (n_y * n_far // math.prod(dims))
    return pl.pallas_call(
        functools.partial(merge_body, dout // cw, feats),
        in_specs=[VM, VM],
        out_specs=[VM] * len(outs),
        out_shape=outs,
        compiler_params=params(),
        cost_estimate=pl.CostEstimate(flops=keep.size, bytes_accessed=6 * keep.size, transcendentals=0),
        name="merge",
    )(keep, got)


def finish_body(counts, in_piece, n_far, *refs):
    grad_ref, gain_ref, loss_ref = refs[-3:]
    feats = grad_ref.shape[0]
    chunks, at = [], 0
    for n in counts:
        chunks.append(refs[at : at + n])
        at += n
    tall, cw = chunks[0][0].shape[2:]

    def total(blocks, rows):
        parts = [
            r[a, b, rows, :].astype(F32) for r in blocks for a in range(r.shape[0]) for b in range(r.shape[1])
        ]
        return sum(parts[1:], parts[0])

    gains, scalars = block_sums(total(chunks[0], slice(feats, tall)), in_piece * n_far)
    lane = lax.broadcasted_iota(jnp.int32, (1, cw), 1)
    weight = jnp.sum(jnp.where(lane == 1, scalars, 0.0), axis=1, keepdims=True)
    loss_ref[0, 0] = jnp.sum(jnp.where(lane == 0, scalars / weight, 0.0))
    gains = gains / weight
    for r in range(in_piece):
        for b in range(n_far):
            gain_ref[pl.ds(r * n_far + b, 1), :] = gains[b * in_piece + r : b * in_piece + r + 1, :]
    for j, blocks in enumerate(chunks):
        grad_ref[:, j * cw : (j + 1) * cw] = (total(blocks, slice(0, feats)) / weight).astype(BF)


def finish(plan, dout, feats, chunks):
    n_dp = plan[0]
    cw = chunks[0][0].shape[3]
    n_far = n_dp // NEAR
    return pl.pallas_call(
        functools.partial(finish_body, [len(c) for c in chunks], dout // (n_far * cw), n_far),
        in_specs=[VM] * sum(len(c) for c in chunks),
        out_specs=[VM, VM, SM],
        out_shape=[shape((feats, dout // n_dp)), shape((dout // cw, cw), F32), shape((1, 1), F32)],
        compiler_params=params(),
        name="finish",
    )(*[b for c in chunks for b in c])


def swap(x, axis, n, mask):
    return lax.ppermute(x, axis, [(i, i ^ mask) for i in range(n)])


def swap_far(x, n_dp, n_tensor, a, b):
    mask = b * NEAR * n_tensor + a * 2
    return lax.ppermute(x, ("dp", "tensor"), [(i, i ^ mask) for i in range(n_dp * n_tensor)])


def exchange_far(plan, two_steps, dout, feats, keep, got):
    n_dp, n_tensor, _, _, pairwise = plan
    n_y, n_far = n_tensor // 2, n_dp // NEAR
    if not pairwise:
        groups = [
            [(NEAR * f + q) * n_tensor + 2 * y + c for y in range(n_y) for f in range(n_far)]
            for q in range(NEAR)
            for c in range(2)
        ]
        (x,) = merge((n_y, n_far), dout, feats, keep, got)
        x = x.reshape(n_y * n_far, *x.shape[2:])
        x = lax.all_to_all(x, ("dp", "tensor"), 0, 0, tiled=True, axis_index_groups=groups)
        return [x.reshape(keep.shape)]

    def far(x, a, b):
        return swap_far(x, n_dp, n_tensor, a, b)

    if two_steps:
        own, across = merge((1, 2), dout, feats, keep, got)
        own, beyond = merge((1, 1), dout, feats, own, far(across, 1, 0))
        return [own, far(beyond, 0, 1)]
    blocks = merge((1, 1), dout, feats, keep, got)
    return [blocks[0], far(blocks[1], 0, 1), far(blocks[2], 1, 0), far(blocks[3], 1, 1)]


def gather_large(n_dp, n_tensor, _, info, weight, context):
    ctx = lax.all_to_all(context[0], "tensor", 0, 0, tiled=True)
    held = {0: weight}
    bit = n_tensor // 2
    while bit:
        held.update({m | bit: swap(w, "tensor", n_tensor, bit) for m, w in list(held.items())})
        bit //= 2
    ctxs = [[ctx]] + [[swap(ctx, "dp", n_dp, q)] for q in range(1, NEAR)]
    return ctxs, mix(info, ctx, [[held[m]] for m in range(n_tensor)], False), []


def gather_small(n_dp, n_tensor, side, info, weight, context):
    barrier = lax.optimization_barrier

    def dp(x, mask):
        return swap(x, "dp", n_dp, mask)

    def tensor(x, mask):
        return swap(x, "tensor", n_tensor, mask)

    dout = weight.shape[1]
    cut = dout // 4
    mine = tensor(lax.dynamic_slice_in_dim(weight, side * cut, cut, 1), 2)
    beside = tensor(weight, 1)
    rest = weight[:, 2 * cut :]
    mine, beside, context = barrier((mine, beside, context))
    ctx = jnp.stack([context[0]] + [tensor(context[m], m) for m in range(1, n_tensor)])
    other, mine_beside = dp(mine, 1), tensor(mine, 1)
    rest, other, mine_beside, ctx = barrier((rest, other, mine_beside, ctx))
    rest, other_beside = tensor(rest, 2), tensor(other, 1)
    ctx_x, ctx_z = dp(ctx, 1), dp(ctx, 2)
    early = mix(info, ctx, [[weight], [beside], [mine, other], [mine_beside, other_beside]], True)
    rest, early = barrier((rest, early))
    late = [rest, tensor(rest, 1)]
    late, ctx_x, ctx_z = barrier((late, ctx_x, ctx_z))
    half = ctx.shape[1] // 2
    ctxs = [[ctx], [ctx_x], [ctx_z], [dp(ctx_x[:, :half], 2), dp(ctx_z[:, half:], 1)]]
    return ctxs, early, late


def on_device(
    n_dp,
    n_tensor,
    query_states,
    key_states,
    value_states,
    joining_weight,
    norm_gain,
    next_hidden,
    lengths,
    vote_counts,
):
    _, tokens, width = query_states.shape
    seq = tokens // lengths.shape[0]
    dout = norm_gain.shape[0]
    rows = next_hidden.shape[0]
    chunks = 2 if dout // n_dp >= 256 else 1
    xor_far = (n_tensor, n_dp // NEAR) == (4, 2)
    plan = (n_dp, n_tensor, chunks, seq, xor_far)
    me = lax.axis_index("tensor").astype(jnp.int32)
    group = lax.axis_index("dp").astype(jnp.int32)
    info = jnp.stack([me, group, lengths[0], vote_counts[0]])

    attended = attend(lengths, me.reshape(1), query_states[0], key_states[0], value_states[0], rows, xor_far)
    gather = gather_small if xor_far else gather_large
    ctxs, early, late = gather(n_dp, n_tensor, group & 1, info, joining_weight[0], attended)
    hidden, grads = join(plan, info, early, norm_gain[None, :], next_hidden, late)
    parts = []
    for j in range(chunks):
        near = [grads[j][0]] + [swap(grads[j][q], "dp", n_dp, q) for q in range(1, NEAR)]
        keep, send = gradient(plan, dout, info, ctxs, near)
        got = swap(send, "tensor", n_tensor, 1)
        parts.append(exchange_far(plan, j == chunks - 1, dout, width, keep, got))
    weight_grad, gain_grad, loss = finish(plan, dout, width, parts)
    return (hidden, weight_grad[None], gain_grad.reshape(dout), loss.reshape(()))


def solution(mesh):
    return jax.shard_map(
        functools.partial(on_device, mesh.shape["dp"], mesh.shape["tensor"]),
        mesh=mesh,
        in_specs=(
            P(None, "dp", "tensor"),
            P(None, "dp", "tensor"),
            P(None, "dp", "tensor"),
            P(None, "tensor", None),
            P(),
            P(("dp", "tensor"), None),
            P("dp"),
            P("dp"),
        ),
        out_specs=(P(("dp", "tensor"), None), P(None, "tensor", "dp"), P(), P()),
        check_vma=False,
    )
```

```python
import functools
import math

import jax
import jax.numpy as jnp
from jax import lax
from jax.experimental import pallas as pl
from jax.experimental.pallas import tpu as pltpu
from jax.sharding import PartitionSpec as P

HD = 128
QB = 128
ROWS = 128
COLS = 256
NEAR = 4
STAT_ROWS = 32

loss_scale = 65536.0
neg_large = -1e30
MIB = 1 << 20
BF = jnp.bfloat16
F32 = jnp.float32


def dot(a, b, dims):
    return lax.dot_general(a, b, (dims, ((), ())), preferred_element_type=F32)


def split_words(x):
    high = x.astype(BF).astype(F32)
    return high, (x - high).astype(BF).astype(F32)


def shape(dims, dtype=BF):
    return jax.ShapeDtypeStruct(dims, dtype)


def params():
    return pltpu.CompilerParams(vmem_limit_bytes=32 * MIB)


VM = pl.BlockSpec(memory_space=pltpu.VMEM)
SM = pl.BlockSpec(memory_space=pltpu.SMEM)


def attend_body(n_out, len_ref, me_ref, q_hbm, k_hbm, v_hbm, *refs):
    out_refs, (q_ref, k_ref, v_ref, sems) = refs[:n_out], refs[n_out : n_out + 4]
    o_ref = refs[-1] if n_out > 1 else out_refs[0]
    seq = q_ref.shape[0]
    rows = o_ref.shape[2]

    def copies(h):
        at = slice(h * HD, (h + 1) * HD)
        pairs = ((q_hbm, q_ref), (k_hbm, k_ref), (v_hbm, v_ref))
        return [pltpu.make_async_copy(a.at[:, at], b.at[:, at], sems.at[h, i]) for i, (a, b) in enumerate(pairs)]

    loads = [copies(h) for h in range(q_ref.shape[1] // HD)]
    for load in loads:
        for copy in load:
            copy.start()
    rate = math.log2(math.e) / math.sqrt(HD)
    length = len_ref[0]
    key = lax.broadcasted_iota(jnp.int32, (seq, 1), 0)
    hide = jnp.where(key < length, 0.0, neg_large)
    r = lax.broadcasted_iota(jnp.int32, (QB, QB), 0)
    c = lax.broadcasted_iota(jnp.int32, (QB, QB), 1)
    for h in range(q_ref.shape[1] // HD):
        at = slice(h * HD, (h + 1) * HD)
        for copy in loads[h]:
            copy.wait()
        q_t, v_t = q_ref[:, at].T, v_ref[:, at].T
        for i in range(seq // QB):
            keys = (i + 1) * QB
            scores = dot(k_ref[:keys, at], q_t[:, i * QB : keys], ((1,), (0,))) + hide[:keys]
            last = jnp.where(r <= c, scores[keys - QB :], neg_large)
            scores = last if i == 0 else jnp.concatenate([scores[: keys - QB], last], 0)
            peak = jnp.max(scores, axis=0, keepdims=True)
            e = jnp.exp2((scores - peak) * rate)
            total = jnp.sum(e, axis=0, keepdims=True)
            out = (dot(v_t[:, :keys], e.astype(BF), ((1,), (0,))) / total).astype(BF)
            for n in range(0, QB, min(rows, QB)):
                block, first = divmod(i * QB + n, rows)
                o_ref[block, at, first : first + min(rows, QB)] = out[:, n : n + rows]
    for m, ref in enumerate(out_refs if n_out > 1 else []):
        ref[...] = o_ref[me_ref[0] ^ m]


def attend(lengths, me, q, k, v, rows, split):
    seq, width = q.shape
    heads = width // HD
    blocks = seq // rows
    hbm = pl.BlockSpec(memory_space=pl.ANY)
    return pl.pallas_call(
        functools.partial(attend_body, blocks if split else 1),
        in_specs=[SM, SM, hbm, hbm, hbm],
        out_specs=[VM] * (blocks if split else 1),
        out_shape=[shape((width, rows))] * blocks if split else [shape((blocks, width, rows))],
        scratch_shapes=[pltpu.VMEM((seq, width), BF)] * 3
        + [pltpu.SemaphoreType.DMA((heads, 3))]
        + ([pltpu.VMEM((blocks, width, rows), BF)] if split else []),
        compiler_params=pltpu.CompilerParams(vmem_limit_bytes=60 * MIB),
        cost_estimate=pl.CostEstimate(
            flops=4 * seq * seq * width, bytes_accessed=8 * seq * width, transcendentals=heads * seq * seq
        ),
        name="attend",
    )(lengths, me, q, k, v)


def stack_body(*refs):
    for i, ref in enumerate(refs[:-1]):
        refs[-1][i] = ref[...]


def stack(arrays):
    return pl.pallas_call(
        stack_body,
        in_specs=[VM] * len(arrays),
        out_specs=VM,
        out_shape=shape((len(arrays), *arrays[0].shape)),
        compiler_params=params(),
        cost_estimate=pl.CostEstimate(
            flops=0, bytes_accessed=4 * len(arrays) * arrays[0].size, transcendentals=0
        ),
        name="stack",
    )(*arrays)


def mix_body(n_tensor, counts, split, info_ref, ctx_ref, *refs):
    w_refs, at = [], 0
    for n in counts:
        w_refs.append(refs[at : at + n])
        at += n
    part_ref, square_ref, turned_ref = refs[at:]
    dout = part_ref.shape[1]
    me, side = info_ref[0], info_ref[1] % 2
    for m in range(n_tensor):
        turned_ref[m] = ctx_ref[m if split else me ^ m].T
    columns = [(c, 0, c) for c in range(0, dout, COLS)]
    if max(counts) > 1:
        cut = w_refs[-1][0].shape[1]
        columns = [(pl.multiple_of(side * cut + c, COLS), 0, c) for c in range(0, cut, COLS)]
        columns += [(pl.multiple_of((1 - side) * cut + c, COLS), 1, c) for c in range(0, cut, COLS)]
        columns += [(c, None, c) for c in range(2 * cut, dout, COLS)]
    for step, (start, piece, first) in enumerate(columns):
        to = pl.ds(start, COLS)
        total = None
        for m in range(n_tensor):
            whole = len(w_refs[m]) == 1
            if not whole and piece is None:
                continue
            w = w_refs[m][0][:, to] if whole else w_refs[m][piece][:, first : first + COLS]
            part = dot(turned_ref[m], w, ((1,), (0,)))
            total = part if total is None else total + part
        part_ref[:, to] = total
        if piece is not None:
            sq = total * total
            lanes = sum(sq[:, i : i + 128] for i in range(0, COLS, 128))
            square_ref[...] = lanes if step == 0 else square_ref[...] + lanes


def mix(info, ctx, weights, split):
    n_tensor, width, rows = ctx.shape
    dout = weights[0][0].shape[1]
    counts = [len(w) for w in weights]
    return pl.pallas_call(
        functools.partial(mix_body, n_tensor, counts, split),
        in_specs=[SM] + [VM] * (1 + sum(counts)),
        out_specs=[VM] * 3,
        out_shape=[shape((rows, dout), F32), shape((rows, 128), F32), shape((n_tensor, rows, width))],
        compiler_params=params(),
        cost_estimate=pl.CostEstimate(
            flops=2 * rows * dout * width * n_tensor,
            bytes_accessed=2 * dout * (width * n_tensor + 2 * rows),
            transcendentals=0,
        ),
        name="mix",
    )(info, ctx, *[w for held in weights for w in held])


def join_body(plan, n_late, info_ref, part_ref, early_ref, turned_ref, gain_ref, next_ref, *refs):
    n_dp, n_tensor, chunks, seq, xor_far = plan
    late_refs, hidden_ref, grad_refs = refs[:n_late], refs[n_late], refs[n_late + 1 : -4]
    joined_ref, square_ref, acc_ref, slope_ref = refs[-4:]
    rows, dout = joined_ref.shape
    step = acc_ref.shape[0]
    me, group, length, votes = info_ref[0], info_ref[1], info_ref[2], info_ref[3]
    near, far = group % NEAR, group // NEAR
    square_ref[...] = early_ref[...]
    ready = dout - late_refs[0].shape[1] if n_late else dout
    for c in range(ready, dout, COLS):
        total = part_ref[:, c : c + COLS]
        for m, ref in enumerate(late_refs, n_tensor - n_late):
            total += dot(turned_ref[m], ref[:, c - ready : c - ready + COLS], ((1,), (0,)))
        joined_ref[:, c : c + COLS] = total
        sq = total * total
        square_ref[...] += sum(sq[:, i : i + 128] for i in range(0, COLS, 128))
    acc_ref[...] = jnp.zeros_like(acc_ref)
    slice_w = dout // n_dp
    cw = slice_w // chunks
    n_far = n_dp // NEAR

    def body(r, carry):
        loss, weights = carry
        at = pl.ds(pl.multiple_of(r * step, step), step)
        inv = lax.rsqrt(jnp.sum(square_ref[at, :], axis=1, keepdims=True) * (1.0 / dout) + 1e-06)
        pos = (me * rows + r * step) % seq + lax.broadcasted_iota(jnp.int32, (step, 1), 0)
        weight = jnp.where(pos < length - 1, votes.astype(F32), 0.0)
        scaled = weight * (loss_scale * 2.0 / dout)
        miss = jnp.zeros((step, 128), F32)
        lean = jnp.zeros((step, 128), F32)
        for c in range(0, dout, 512):
            cs = slice(c, c + 512)
            normed = (part_ref if c < ready else joined_ref)[at, cs] * inv
            gain = gain_ref[:, cs]
            predicted = normed * gain
            hidden_ref[at, cs] = predicted.astype(BF)
            misfit = predicted - next_ref[at, cs].astype(F32)
            grad = scaled * misfit
            slope = grad * gain
            acc_ref[:, cs] += grad * normed
            slope_ref[:, cs] = slope
            sq = misfit * misfit
            ln = slope * normed
            miss += sum(sq[:, i : i + 128] for i in range(0, 512, 128))
            lean += sum(ln[:, i : i + 128] for i in range(0, 512, 128))
            joined_ref[at, cs] = normed
        lean = jnp.sum(lean, axis=1, keepdims=True) * (1.0 / dout)

        def gradient_at(cs):
            return (inv * (slope_ref[:, cs] - joined_ref[at, cs] * lean)).astype(BF)

        for j in range(chunks):
            for q in range(NEAR):
                for b in range(n_far):
                    to = slice(b * cw, (b + 1) * cw)
                    if cw % 128 == 0:
                        other = (far ^ b if xor_far else b) * NEAR + (near ^ q)
                        start = pl.multiple_of(other * slice_w + j * cw, 128)
                        grad_refs[j * NEAR + q][at, to] = gradient_at(pl.ds(start, cw))
                    else:
                        start = (b * NEAR + q) * slice_w + j * cw
                        grad_refs[j][near ^ q, at, to] = gradient_at(slice(start, start + cw))
        loss = loss + weight * (jnp.sum(miss, axis=1, keepdims=True) * (1.0 / dout))
        return loss, weights + weight

    zero = jnp.zeros((step, 1), F32)
    loss, weights = lax.fori_loop(0, rows // step, body, (zero, zero))
    wide = n_far * cw
    gain_sum = jnp.sum(acc_ref[...], axis=0, keepdims=True)
    gain_sum = jnp.concatenate([gain_sum[:, i : i + wide] for i in range(0, dout, wide)], 0)
    lane = lax.broadcasted_iota(jnp.int32, (1, wide), 1)
    loss = jnp.sum(loss, axis=0, keepdims=True)
    weights = jnp.sum(weights, axis=0, keepdims=True)
    scalars = jnp.where(lane == 0, loss, jnp.where(lane == 1, weights, 0.0))
    words = [*split_words(gain_sum), *split_words(scalars)]
    left = STAT_ROWS - sum(w.shape[0] for w in words)
    words = jnp.concatenate([*words, jnp.zeros((left, wide), F32)], 0).astype(BF)
    if cw % 128 == 0:
        for q in range(NEAR):
            grad_refs[q][rows:, :] = words
    else:
        for q in range(NEAR):
            grad_refs[0][q, rows:, :] = words


def join(plan, info, early, gain, next_hidden, late):
    n_dp, n_tensor, chunks, _, _ = plan
    _, rows, width = early[2].shape
    step = min(ROWS, rows)
    dout = gain.shape[1]
    wide = dout // NEAR // chunks
    tall = [rows + STAT_ROWS] + [rows] * (chunks - 1)
    aligned = dout // n_dp // chunks % 128 == 0
    if aligned:
        grads = [shape((n, wide)) for n in tall for _ in range(NEAR)]
    else:
        grads = [shape((NEAR, n, wide)) for n in tall]
    out = pl.pallas_call(
        functools.partial(join_body, plan, len(late)),
        in_specs=[SM] + [VM] * (5 + len(late)),
        out_specs=[VM] * (1 + len(grads)),
        out_shape=[shape((rows, dout)), *grads],
        scratch_shapes=[
            pltpu.VMEM((rows, dout), F32),
            pltpu.VMEM((rows, 128), F32),
            pltpu.VMEM((step, dout), F32),
            pltpu.VMEM((step, dout), F32),
        ],
        compiler_params=params(),
        cost_estimate=pl.CostEstimate(
            flops=rows * dout * width,
            bytes_accessed=2 * dout * (width + 5 * rows),
            transcendentals=rows,
        ),
        name="join",
    )(info, *early, gain, next_hidden, *late)
    if aligned:
        return out[0], [out[1 + j * NEAR : 1 + (j + 1) * NEAR] for j in range(chunks)]
    return out[0], [[g[q] for q in range(NEAR)] for g in out[1:]]


def stat_sizes(dout, wide, cw):
    in_block = dout // cw
    return dout // wide, in_block, -(-(2 * in_block + 2) // 16) * 16


def block_words(gains, scalars, tall, cw):
    words = [*split_words(gains), *split_words(scalars)]
    left = tall - sum(w.shape[0] for w in words)
    return jnp.concatenate([*words, jnp.zeros((left, cw), F32)], 0).astype(BF)


def block_sums(words, n):
    words = words.astype(F32)
    return words[:n] + words[n : 2 * n], words[2 * n : 2 * n + 1] + words[2 * n + 1 : 2 * n + 2]


def grad_body(plan, dout, counts, info_ref, *refs):
    n_dp, n_tensor, _, _, xor_far = plan
    keep_ref, send_ref = refs[-2:]
    ctx_refs, at = [], 0
    for n in counts:
        ctx_refs.append(refs[at : at + n])
        at += n
    g_refs = refs[at:-2]
    n_y, n_far, tall, cw = keep_ref.shape
    feats, rows = ctx_refs[0][0].shape[1:]
    wide = n_far * cw
    me = info_ref[0]
    core = me % 2
    if tall > feats:
        in_piece, in_block, stat_rows = stat_sizes(dout, wide, cw)
        sums = sum(ref[rows:, :].astype(F32) for ref in g_refs)
        gains, scalars = block_sums(sums, in_piece)
        gains = jnp.concatenate([gains[:, b * cw : (b + 1) * cw] for b in range(n_far)], 0)
        words = block_words(gains, scalars[:, :cw], stat_rows, cw)
    for s, ref in ((1, send_ref), (0, keep_ref)):
        for a in range(n_y):
            m = a * 2 + (s if xor_far else core ^ s)
            total = None
            for parts, g in zip(ctx_refs, g_refs):
                c = jnp.concatenate([part[m] for part in parts], 0) if len(parts) > 1 else parts[0][m]
                part = dot(c, g[:rows, :], ((1,), (0,)))
                total = part if total is None else total + part
            total = total.astype(BF)
            for b in range(n_far):
                ref[a, b, :feats, :] = total[:, b * cw : (b + 1) * cw]
                if tall > feats:
                    ref[a, b, feats:, :] = words


def gradient(plan, dout, info, ctxs, grads):
    n_dp, n_tensor, chunks, _, _ = plan
    _, feats, rows = ctxs[0][0].shape
    wide = grads[0].shape[1]
    cw = dout // n_dp // chunks
    tall = feats
    if grads[0].shape[0] > rows:
        tall += stat_sizes(dout, wide, cw)[2]
    block = shape((n_tensor // 2, n_dp // NEAR, tall, cw))
    return pl.pallas_call(
        functools.partial(grad_body, plan, dout, [len(c) for c in ctxs]),
        in_specs=[SM] + [VM] * (NEAR + sum(len(c) for c in ctxs)),
        out_specs=[VM, VM],
        out_shape=[block, block],
        compiler_params=params(),
        cost_estimate=pl.CostEstimate(
            flops=2 * NEAR * n_tensor * rows * feats * wide,
            bytes_accessed=2 * (NEAR * rows * (n_tensor * feats + wide) + n_tensor * feats * wide),
            transcendentals=0,
        ),
        name="gradient",
    )(info, *[part for parts in ctxs for part in parts], *grads)


def merge_body(in_block, feats, keep_ref, got_ref, *out_refs):
    n_y, n_far, tall, cw = keep_ref.shape
    if tall > feats:
        gains, scalars = block_sums(keep_ref[0, 0, feats:, :], in_block)
        more, others = block_sums(got_ref[0, 0, feats:, :], in_block)
        words = block_words(gains + more, scalars + others, tall - feats, cw)
    each = out_refs[0].shape[0] * out_refs[0].shape[1]
    for i in range(n_y * n_far):
        a, b = divmod(i, n_far)
        total = keep_ref[a, b, :feats, :].astype(F32) + got_ref[a, b, :feats, :].astype(F32)
        ref, at = out_refs[i // each], divmod(i % each, out_refs[0].shape[1])
        ref[(*at, slice(0, feats), slice(None))] = total.astype(BF)
        if tall > feats:
            ref[(*at, slice(feats, tall), slice(None))] = words


def merge(dims, dout, feats, keep, got):
    n_y, n_far, tall, cw = keep.shape
    outs = [shape((*dims, tall, cw))] * (n_y * n_far // math.prod(dims))
    return pl.pallas_call(
        functools.partial(merge_body, dout // cw, feats),
        in_specs=[VM, VM],
        out_specs=[VM] * len(outs),
        out_shape=outs,
        compiler_params=params(),
        cost_estimate=pl.CostEstimate(flops=keep.size, bytes_accessed=6 * keep.size, transcendentals=0),
        name="merge",
    )(keep, got)


def finish_body(counts, in_piece, n_far, *refs):
    grad_ref, gain_ref, loss_ref = refs[-3:]
    feats = grad_ref.shape[0]
    chunks, at = [], 0
    for n in counts:
        chunks.append(refs[at : at + n])
        at += n
    tall, cw = chunks[0][0].shape[2:]

    def total(blocks, rows):
        parts = [
            r[a, b, rows, :].astype(F32) for r in blocks for a in range(r.shape[0]) for b in range(r.shape[1])
        ]
        return sum(parts[1:], parts[0])

    gains, scalars = block_sums(total(chunks[0], slice(feats, tall)), in_piece * n_far)
    lane = lax.broadcasted_iota(jnp.int32, (1, cw), 1)
    weight = jnp.sum(jnp.where(lane == 1, scalars, 0.0), axis=1, keepdims=True)
    loss_ref[0, 0] = jnp.sum(jnp.where(lane == 0, scalars / weight, 0.0))
    gains = gains / weight
    for r in range(in_piece):
        for b in range(n_far):
            gain_ref[pl.ds(r * n_far + b, 1), :] = gains[b * in_piece + r : b * in_piece + r + 1, :]
    for j, blocks in enumerate(chunks):
        grad_ref[:, j * cw : (j + 1) * cw] = (total(blocks, slice(0, feats)) / weight).astype(BF)


def finish(plan, dout, feats, chunks):
    n_dp = plan[0]
    cw = chunks[0][0].shape[3]
    n_far = n_dp // NEAR
    return pl.pallas_call(
        functools.partial(finish_body, [len(c) for c in chunks], dout // (n_far * cw), n_far),
        in_specs=[VM] * sum(len(c) for c in chunks),
        out_specs=[VM, VM, SM],
        out_shape=[shape((feats, dout // n_dp)), shape((dout // cw, cw), F32), shape((1, 1), F32)],
        compiler_params=params(),
        name="finish",
    )(*[b for c in chunks for b in c])


def swap(x, axis, n, mask):
    return lax.ppermute(x, axis, [(i, i ^ mask) for i in range(n)])


def swap_far(x, n_dp, n_tensor, a, b):
    mask = b * NEAR * n_tensor + a * 2
    return lax.ppermute(x, ("dp", "tensor"), [(i, i ^ mask) for i in range(n_dp * n_tensor)])


def exchange_far(plan, two_steps, dout, feats, keep, got):
    n_dp, n_tensor, _, _, pairwise = plan
    n_y, n_far = n_tensor // 2, n_dp // NEAR
    if not pairwise:
        groups = [
            [(NEAR * f + q) * n_tensor + 2 * y + c for y in range(n_y) for f in range(n_far)]
            for q in range(NEAR)
            for c in range(2)
        ]
        (x,) = merge((n_y, n_far), dout, feats, keep, got)
        x = x.reshape(n_y * n_far, *x.shape[2:])
        x = lax.all_to_all(x, ("dp", "tensor"), 0, 0, tiled=True, axis_index_groups=groups)
        return [x.reshape(keep.shape)]

    def far(x, a, b):
        return swap_far(x, n_dp, n_tensor, a, b)

    if two_steps:
        own, across = merge((1, 2), dout, feats, keep, got)
        own, beyond = merge((1, 1), dout, feats, own, far(across, 1, 0))
        return [own, far(beyond, 0, 1)]
    blocks = merge((1, 1), dout, feats, keep, got)
    return [blocks[0], far(blocks[1], 0, 1), far(blocks[2], 1, 0), far(blocks[3], 1, 1)]


def gather_large(n_dp, n_tensor, _, info, weight, context):
    ctx = lax.all_to_all(context[0], "tensor", 0, 0, tiled=True)
    held = {0: weight}
    bit = n_tensor // 2
    while bit:
        held.update({m | bit: swap(w, "tensor", n_tensor, bit) for m, w in list(held.items())})
        bit //= 2
    ctxs = [[ctx]] + [[swap(ctx, "dp", n_dp, q)] for q in range(1, NEAR)]
    return ctxs, mix(info, ctx, [[held[m]] for m in range(n_tensor)], False), []


def gather_small(n_dp, n_tensor, side, info, weight, context):
    barrier = lax.optimization_barrier

    def dp(x, mask):
        return swap(x, "dp", n_dp, mask)

    def tensor(x, mask):
        return swap(x, "tensor", n_tensor, mask)

    dout = weight.shape[1]
    cut = dout // 4
    mine = tensor(lax.dynamic_slice_in_dim(weight, side * cut, cut, 1), 2)
    beside = tensor(weight, 1)
    rest = weight[:, 2 * cut :]
    mine, beside, context = barrier((mine, beside, context))
    ctx = stack([context[0]] + [tensor(context[m], m) for m in range(1, n_tensor)])
    other, mine_beside = dp(mine, 1), tensor(mine, 1)
    rest, other, mine_beside, ctx = barrier((rest, other, mine_beside, ctx))
    rest, other_beside = tensor(rest, 2), tensor(other, 1)
    ctx_x, ctx_z = dp(ctx, 1), dp(ctx, 2)
    early = mix(info, ctx, [[weight], [beside], [mine, other], [mine_beside, other_beside]], True)
    rest, early, ctx_x, ctx_z = barrier((rest, early, ctx_x, ctx_z))
    half = ctx.shape[1] // 2
    ctxs = [[ctx], [ctx_x], [ctx_z], [dp(ctx_x[:, :half], 2), dp(ctx_z[:, half:], 1)]]
    return ctxs, early, [rest, tensor(rest, 1)]


def on_device(
    n_dp,
    n_tensor,
    query_states,
    key_states,
    value_states,
    joining_weight,
    norm_gain,
    next_hidden,
    lengths,
    vote_counts,
):
    _, tokens, width = query_states.shape
    seq = tokens // lengths.shape[0]
    dout = norm_gain.shape[0]
    rows = next_hidden.shape[0]
    chunks = 2 if dout // n_dp >= 256 else 1
    xor_far = (n_tensor, n_dp // NEAR) == (4, 2)
    plan = (n_dp, n_tensor, chunks, seq, xor_far)
    me = lax.axis_index("tensor").astype(jnp.int32)
    group = lax.axis_index("dp").astype(jnp.int32)
    info = jnp.stack([me, group, lengths[0], vote_counts[0]])

    attended = attend(lengths, me.reshape(1), query_states[0], key_states[0], value_states[0], rows, xor_far)
    gather = gather_small if xor_far else gather_large
    ctxs, early, late = gather(n_dp, n_tensor, group & 1, info, joining_weight[0], attended)
    hidden, grads = join(plan, info, early, norm_gain[None, :], next_hidden, late)
    parts = []
    for j in range(chunks):
        near = [grads[j][0]] + [swap(grads[j][q], "dp", n_dp, q) for q in range(1, NEAR)]
        keep, send = gradient(plan, dout, info, ctxs, near)
        got = swap(send, "tensor", n_tensor, 1)
        parts.append(exchange_far(plan, j == chunks - 1, dout, width, keep, got))
    weight_grad, gain_grad, loss = finish(plan, dout, width, parts)
    return (hidden, weight_grad[None], gain_grad.reshape(dout), loss.reshape(()))


def solution(mesh):
    return jax.shard_map(
        functools.partial(on_device, mesh.shape["dp"], mesh.shape["tensor"]),
        mesh=mesh,
        in_specs=(
            P(None, "dp", "tensor"),
            P(None, "dp", "tensor"),
            P(None, "dp", "tensor"),
            P(None, "tensor", None),
            P(),
            P(("dp", "tensor"), None),
            P("dp"),
            P("dp"),
        ),
        out_specs=(P(("dp", "tensor"), None), P(None, "tensor", "dp"), P(), P()),
        check_vma=False,
    )
```

```python
import functools
import math

import jax
import jax.numpy as jnp
from jax import lax
from jax.experimental import pallas as pl
from jax.experimental.pallas import tpu as pltpu
from jax.sharding import PartitionSpec as P

HD = 128
QB = 128
ROWS = 128
COLS = 256
NEAR = 4
STAT_ROWS = 32

loss_scale = 65536.0
neg_large = -1e30
MIB = 1 << 20
BF = jnp.bfloat16
F32 = jnp.float32


def dot(a, b, dims):
    return lax.dot_general(a, b, (dims, ((), ())), preferred_element_type=F32)


def split_words(x):
    high = x.astype(BF).astype(F32)
    return high, (x - high).astype(BF).astype(F32)


def shape(dims, dtype=BF):
    return jax.ShapeDtypeStruct(dims, dtype)


def params():
    return pltpu.CompilerParams(vmem_limit_bytes=32 * MIB)


VM = pl.BlockSpec(memory_space=pltpu.VMEM)
SM = pl.BlockSpec(memory_space=pltpu.SMEM)


def attend_body(len_ref, me_ref, q_ref, k_ref, v_ref, *out_refs):
    seq = q_ref.shape[0]
    o_ref = out_refs[-1]
    rows = o_ref.shape[2]
    rate = math.log2(math.e) / math.sqrt(HD)
    length = len_ref[0]
    key = lax.broadcasted_iota(jnp.int32, (seq, 1), 0)
    hide = jnp.where(key < length, 0.0, neg_large)
    r = lax.broadcasted_iota(jnp.int32, (QB, QB), 0)
    c = lax.broadcasted_iota(jnp.int32, (QB, QB), 1)
    for h in range(q_ref.shape[1] // HD):
        at = slice(h * HD, (h + 1) * HD)
        q_t, v_t = q_ref[:, at].T, v_ref[:, at].T
        for i in range(seq // QB):
            keys = (i + 1) * QB
            scores = dot(k_ref[:keys, at], q_t[:, i * QB : keys], ((1,), (0,))) + hide[:keys]
            last = jnp.where(r <= c, scores[keys - QB :], neg_large)
            scores = last if i == 0 else jnp.concatenate([scores[: keys - QB], last], 0)
            peak = jnp.max(scores, axis=0, keepdims=True)
            e = jnp.exp2((scores - peak) * rate)
            total = jnp.sum(e, axis=0, keepdims=True)
            out = (dot(v_t[:, :keys], e.astype(BF), ((1,), (0,))) / total).astype(BF)
            for n in range(0, QB, min(rows, QB)):
                block, first = divmod(i * QB + n, rows)
                o_ref[block, at, first : first + min(rows, QB)] = out[:, n : n + rows]
    for m, ref in enumerate(out_refs[:-1]):
        ref[...] = o_ref[me_ref[0] ^ m]


def attend(lengths, me, q, k, v, rows, split):
    seq, width = q.shape
    heads = width // HD
    blocks = seq // rows
    return pl.pallas_call(
        attend_body,
        in_specs=[SM, SM, VM, VM, VM],
        out_specs=[VM] * (blocks if split else 1),
        out_shape=[shape((width, rows))] * blocks if split else [shape((blocks, width, rows))],
        scratch_shapes=[pltpu.VMEM((blocks, width, rows), BF)] if split else [],
        compiler_params=pltpu.CompilerParams(vmem_limit_bytes=60 * MIB),
        cost_estimate=pl.CostEstimate(
            flops=4 * seq * seq * width, bytes_accessed=8 * seq * width, transcendentals=heads * seq * seq
        ),
        name="attend",
    )(lengths, me, q, k, v)


def mix_body(n_tensor, counts, split, info_ref, ctx_ref, *refs):
    w_refs, at = [], 0
    for n in counts:
        w_refs.append(refs[at : at + n])
        at += n
    part_ref, square_ref, turned_ref = refs[at:]
    dout = part_ref.shape[1]
    me, side = info_ref[0], info_ref[1] % 2
    for m in range(n_tensor):
        turned_ref[m] = ctx_ref[m if split else me ^ m].T
    columns = [(c, 0, c) for c in range(0, dout, COLS)]
    if max(counts) > 1:
        cut = w_refs[-1][0].shape[1]
        columns = [(pl.multiple_of(side * cut + c, COLS), 0, c) for c in range(0, cut, COLS)]
        columns += [(pl.multiple_of((1 - side) * cut + c, COLS), 1, c) for c in range(0, cut, COLS)]
        columns += [(c, None, c) for c in range(2 * cut, dout, COLS)]
    for step, (start, piece, first) in enumerate(columns):
        to = pl.ds(start, COLS)
        total = None
        for m in range(n_tensor):
            whole = len(w_refs[m]) == 1
            if not whole and piece is None:
                continue
            w = w_refs[m][0][:, to] if whole else w_refs[m][piece][:, first : first + COLS]
            part = dot(turned_ref[m], w, ((1,), (0,)))
            total = part if total is None else total + part
        part_ref[:, to] = total
        if piece is not None:
            sq = total * total
            lanes = sum(sq[:, i : i + 128] for i in range(0, COLS, 128))
            square_ref[...] = lanes if step == 0 else square_ref[...] + lanes


def mix(info, ctx, weights, split):
    n_tensor, width, rows = ctx.shape
    dout = weights[0][0].shape[1]
    counts = [len(w) for w in weights]
    return pl.pallas_call(
        functools.partial(mix_body, n_tensor, counts, split),
        in_specs=[SM] + [VM] * (1 + sum(counts)),
        out_specs=[VM] * 3,
        out_shape=[shape((rows, dout), F32), shape((rows, 128), F32), shape((n_tensor, rows, width))],
        compiler_params=params(),
        cost_estimate=pl.CostEstimate(
            flops=2 * rows * dout * width * n_tensor,
            bytes_accessed=2 * dout * (width * n_tensor + 2 * rows),
            transcendentals=0,
        ),
        name="mix",
    )(info, ctx, *[w for held in weights for w in held])


def join_body(plan, n_late, info_ref, part_ref, early_ref, turned_ref, gain_ref, next_ref, *refs):
    n_dp, n_tensor, chunks, seq, xor_far = plan
    late_refs, hidden_ref, grad_refs = refs[:n_late], refs[n_late], refs[n_late + 1 : -4]
    joined_ref, square_ref, acc_ref, slope_ref = refs[-4:]
    rows, dout = joined_ref.shape
    step = acc_ref.shape[0]
    me, group, length, votes = info_ref[0], info_ref[1], info_ref[2], info_ref[3]
    near, far = group % NEAR, group // NEAR
    square_ref[...] = early_ref[...]
    ready = dout - late_refs[0].shape[1] if n_late else dout
    for c in range(ready, dout, COLS):
        total = part_ref[:, c : c + COLS]
        for m, ref in enumerate(late_refs, n_tensor - n_late):
            total += dot(turned_ref[m], ref[:, c - ready : c - ready + COLS], ((1,), (0,)))
        joined_ref[:, c : c + COLS] = total
        sq = total * total
        square_ref[...] += sum(sq[:, i : i + 128] for i in range(0, COLS, 128))
    acc_ref[...] = jnp.zeros_like(acc_ref)
    slice_w = dout // n_dp
    cw = slice_w // chunks
    n_far = n_dp // NEAR

    def body(r, carry):
        loss, weights = carry
        at = pl.ds(pl.multiple_of(r * step, step), step)
        inv = lax.rsqrt(jnp.sum(square_ref[at, :], axis=1, keepdims=True) * (1.0 / dout) + 1e-06)
        pos = (me * rows + r * step) % seq + lax.broadcasted_iota(jnp.int32, (step, 1), 0)
        weight = jnp.where(pos < length - 1, votes.astype(F32), 0.0)
        scaled = weight * (loss_scale * 2.0 / dout)
        miss = jnp.zeros((step, 128), F32)
        lean = jnp.zeros((step, 128), F32)
        for c in range(0, dout, 512):
            cs = slice(c, c + 512)
            normed = (part_ref if c < ready else joined_ref)[at, cs] * inv
            gain = gain_ref[:, cs]
            predicted = normed * gain
            hidden_ref[at, cs] = predicted.astype(BF)
            misfit = predicted - next_ref[at, cs].astype(F32)
            grad = scaled * misfit
            slope = grad * gain
            acc_ref[:, cs] += grad * normed
            slope_ref[:, cs] = slope
            sq = misfit * misfit
            ln = slope * normed
            miss += sum(sq[:, i : i + 128] for i in range(0, 512, 128))
            lean += sum(ln[:, i : i + 128] for i in range(0, 512, 128))
            joined_ref[at, cs] = normed
        lean = jnp.sum(lean, axis=1, keepdims=True) * (1.0 / dout)

        def gradient_at(cs):
            return (inv * (slope_ref[:, cs] - joined_ref[at, cs] * lean)).astype(BF)

        for j in range(chunks):
            for q in range(NEAR):
                for b in range(n_far):
                    to = slice(b * cw, (b + 1) * cw)
                    if cw % 128 == 0:
                        other = (far ^ b if xor_far else b) * NEAR + (near ^ q)
                        start = pl.multiple_of(other * slice_w + j * cw, 128)
                        grad_refs[j * NEAR + q][at, to] = gradient_at(pl.ds(start, cw))
                    else:
                        start = (b * NEAR + q) * slice_w + j * cw
                        grad_refs[j][near ^ q, at, to] = gradient_at(slice(start, start + cw))
        loss = loss + weight * (jnp.sum(miss, axis=1, keepdims=True) * (1.0 / dout))
        return loss, weights + weight

    zero = jnp.zeros((step, 1), F32)
    loss, weights = lax.fori_loop(0, rows // step, body, (zero, zero))
    wide = n_far * cw
    gain_sum = jnp.sum(acc_ref[...], axis=0, keepdims=True)
    gain_sum = jnp.concatenate([gain_sum[:, i : i + wide] for i in range(0, dout, wide)], 0)
    lane = lax.broadcasted_iota(jnp.int32, (1, wide), 1)
    loss = jnp.sum(loss, axis=0, keepdims=True)
    weights = jnp.sum(weights, axis=0, keepdims=True)
    scalars = jnp.where(lane == 0, loss, jnp.where(lane == 1, weights, 0.0))
    words = [*split_words(gain_sum), *split_words(scalars)]
    left = STAT_ROWS - sum(w.shape[0] for w in words)
    words = jnp.concatenate([*words, jnp.zeros((left, wide), F32)], 0).astype(BF)
    if cw % 128 == 0:
        for q in range(NEAR):
            grad_refs[q][rows:, :] = words
    else:
        for q in range(NEAR):
            grad_refs[0][q, rows:, :] = words


def join(plan, info, early, gain, next_hidden, late):
    n_dp, n_tensor, chunks, _, _ = plan
    _, rows, width = early[2].shape
    step = min(ROWS, rows)
    dout = gain.shape[1]
    wide = dout // NEAR // chunks
    tall = [rows + STAT_ROWS] + [rows] * (chunks - 1)
    aligned = dout // n_dp // chunks % 128 == 0
    if aligned:
        grads = [shape((n, wide)) for n in tall for _ in range(NEAR)]
    else:
        grads = [shape((NEAR, n, wide)) for n in tall]
    out = pl.pallas_call(
        functools.partial(join_body, plan, len(late)),
        in_specs=[SM] + [VM] * (5 + len(late)),
        out_specs=[VM] * (1 + len(grads)),
        out_shape=[shape((rows, dout)), *grads],
        scratch_shapes=[
            pltpu.VMEM((rows, dout), F32),
            pltpu.VMEM((rows, 128), F32),
            pltpu.VMEM((step, dout), F32),
            pltpu.VMEM((step, dout), F32),
        ],
        compiler_params=params(),
        cost_estimate=pl.CostEstimate(
            flops=rows * dout * width,
            bytes_accessed=2 * dout * (width + 5 * rows),
            transcendentals=rows,
        ),
        name="join",
    )(info, *early, gain, next_hidden, *late)
    if aligned:
        return out[0], [out[1 + j * NEAR : 1 + (j + 1) * NEAR] for j in range(chunks)]
    return out[0], [[g[q] for q in range(NEAR)] for g in out[1:]]


def stat_sizes(dout, wide, cw):
    in_block = dout // cw
    return dout // wide, in_block, -(-(2 * in_block + 2) // 16) * 16


def block_words(gains, scalars, tall, cw):
    words = [*split_words(gains), *split_words(scalars)]
    left = tall - sum(w.shape[0] for w in words)
    return jnp.concatenate([*words, jnp.zeros((left, cw), F32)], 0).astype(BF)


def block_sums(words, n):
    words = words.astype(F32)
    return words[:n] + words[n : 2 * n], words[2 * n : 2 * n + 1] + words[2 * n + 1 : 2 * n + 2]


def grad_body(plan, dout, counts, info_ref, *refs):
    n_dp, n_tensor, _, _, xor_far = plan
    keep_ref, send_ref = refs[-2:]
    ctx_refs, at = [], 0
    for n in counts:
        ctx_refs.append(refs[at : at + n])
        at += n
    g_refs = refs[at:-2]
    n_y, n_far, tall, cw = keep_ref.shape
    feats, rows = ctx_refs[0][0].shape[1:]
    wide = n_far * cw
    me = info_ref[0]
    core = me % 2
    if tall > feats:
        in_piece, in_block, stat_rows = stat_sizes(dout, wide, cw)
        sums = sum(ref[rows:, :].astype(F32) for ref in g_refs)
        gains, scalars = block_sums(sums, in_piece)
        gains = jnp.concatenate([gains[:, b * cw : (b + 1) * cw] for b in range(n_far)], 0)
        words = block_words(gains, scalars[:, :cw], stat_rows, cw)
    for s, ref in ((1, send_ref), (0, keep_ref)):
        for a in range(n_y):
            m = a * 2 + (s if xor_far else core ^ s)
            total = None
            for parts, g in zip(ctx_refs, g_refs):
                c = jnp.concatenate([part[m] for part in parts], 0) if len(parts) > 1 else parts[0][m]
                part = dot(c, g[:rows, :], ((1,), (0,)))
                total = part if total is None else total + part
            total = total.astype(BF)
            for b in range(n_far):
                ref[a, b, :feats, :] = total[:, b * cw : (b + 1) * cw]
                if tall > feats:
                    ref[a, b, feats:, :] = words


def gradient(plan, dout, info, ctxs, grads):
    n_dp, n_tensor, chunks, _, _ = plan
    _, feats, rows = ctxs[0][0].shape
    wide = grads[0].shape[1]
    cw = dout // n_dp // chunks
    tall = feats
    if grads[0].shape[0] > rows:
        tall += stat_sizes(dout, wide, cw)[2]
    block = shape((n_tensor // 2, n_dp // NEAR, tall, cw))
    return pl.pallas_call(
        functools.partial(grad_body, plan, dout, [len(c) for c in ctxs]),
        in_specs=[SM] + [VM] * (NEAR + sum(len(c) for c in ctxs)),
        out_specs=[VM, VM],
        out_shape=[block, block],
        compiler_params=params(),
        cost_estimate=pl.CostEstimate(
            flops=2 * NEAR * n_tensor * rows * feats * wide,
            bytes_accessed=2 * (NEAR * rows * (n_tensor * feats + wide) + n_tensor * feats * wide),
            transcendentals=0,
        ),
        name="gradient",
    )(info, *[part for parts in ctxs for part in parts], *grads)


def merge_body(in_block, feats, keep_ref, got_ref, *out_refs):
    n_y, n_far, tall, cw = keep_ref.shape
    if tall > feats:
        gains, scalars = block_sums(keep_ref[0, 0, feats:, :], in_block)
        more, others = block_sums(got_ref[0, 0, feats:, :], in_block)
        words = block_words(gains + more, scalars + others, tall - feats, cw)
    each = out_refs[0].shape[0] * out_refs[0].shape[1]
    for i in range(n_y * n_far):
        a, b = divmod(i, n_far)
        total = keep_ref[a, b, :feats, :].astype(F32) + got_ref[a, b, :feats, :].astype(F32)
        ref, at = out_refs[i // each], divmod(i % each, out_refs[0].shape[1])
        ref[(*at, slice(0, feats), slice(None))] = total.astype(BF)
        if tall > feats:
            ref[(*at, slice(feats, tall), slice(None))] = words


def merge(dims, dout, feats, keep, got):
    n_y, n_far, tall, cw = keep.shape
    outs = [shape((*dims, tall, cw))] * (n_y * n_far // math.prod(dims))
    return pl.pallas_call(
        functools.partial(merge_body, dout // cw, feats),
        in_specs=[VM, VM],
        out_specs=[VM] * len(outs),
        out_shape=outs,
        compiler_params=params(),
        cost_estimate=pl.CostEstimate(flops=keep.size, bytes_accessed=6 * keep.size, transcendentals=0),
        name="merge",
    )(keep, got)


def finish_body(counts, in_piece, n_far, *refs):
    grad_ref, gain_ref, loss_ref = refs[-3:]
    feats = grad_ref.shape[0]
    chunks, at = [], 0
    for n in counts:
        chunks.append(refs[at : at + n])
        at += n
    tall, cw = chunks[0][0].shape[2:]

    def total(blocks, rows):
        parts = [
            r[a, b, rows, :].astype(F32) for r in blocks for a in range(r.shape[0]) for b in range(r.shape[1])
        ]
        return sum(parts[1:], parts[0])

    gains, scalars = block_sums(total(chunks[0], slice(feats, tall)), in_piece * n_far)
    lane = lax.broadcasted_iota(jnp.int32, (1, cw), 1)
    weight = jnp.sum(jnp.where(lane == 1, scalars, 0.0), axis=1, keepdims=True)
    loss_ref[0, 0] = jnp.sum(jnp.where(lane == 0, scalars / weight, 0.0))
    gains = gains / weight
    for r in range(in_piece):
        for b in range(n_far):
            gain_ref[pl.ds(r * n_far + b, 1), :] = gains[b * in_piece + r : b * in_piece + r + 1, :]
    for j, blocks in enumerate(chunks):
        grad_ref[:, j * cw : (j + 1) * cw] = (total(blocks, slice(0, feats)) / weight).astype(BF)


def finish(plan, dout, feats, chunks):
    n_dp = plan[0]
    cw = chunks[0][0].shape[3]
    n_far = n_dp // NEAR
    return pl.pallas_call(
        functools.partial(finish_body, [len(c) for c in chunks], dout // (n_far * cw), n_far),
        in_specs=[VM] * sum(len(c) for c in chunks),
        out_specs=[VM, VM, SM],
        out_shape=[shape((feats, dout // n_dp)), shape((dout // cw, cw), F32), shape((1, 1), F32)],
        compiler_params=params(),
        name="finish",
    )(*[b for c in chunks for b in c])


def swap(x, axis, n, mask):
    return lax.ppermute(x, axis, [(i, i ^ mask) for i in range(n)])


def swap_far(x, n_dp, n_tensor, a, b):
    mask = b * NEAR * n_tensor + a * 2
    return lax.ppermute(x, ("dp", "tensor"), [(i, i ^ mask) for i in range(n_dp * n_tensor)])


def exchange_far(plan, two_steps, dout, feats, keep, got):
    n_dp, n_tensor, _, _, pairwise = plan
    n_y, n_far = n_tensor // 2, n_dp // NEAR
    if not pairwise:
        groups = [
            [(NEAR * f + q) * n_tensor + 2 * y + c for y in range(n_y) for f in range(n_far)]
            for q in range(NEAR)
            for c in range(2)
        ]
        (x,) = merge((n_y, n_far), dout, feats, keep, got)
        x = x.reshape(n_y * n_far, *x.shape[2:])
        x = lax.all_to_all(x, ("dp", "tensor"), 0, 0, tiled=True, axis_index_groups=groups)
        return [x.reshape(keep.shape)]

    def far(x, a, b):
        return swap_far(x, n_dp, n_tensor, a, b)

    if two_steps:
        own, across = merge((1, 2), dout, feats, keep, got)
        own, beyond = merge((1, 1), dout, feats, own, far(across, 1, 0))
        return [own, far(beyond, 0, 1)]
    blocks = merge((1, 1), dout, feats, keep, got)
    return [blocks[0], far(blocks[1], 0, 1), far(blocks[2], 1, 0), far(blocks[3], 1, 1)]


def gather_large(n_dp, n_tensor, _, info, weight, context):
    ctx = lax.all_to_all(context[0], "tensor", 0, 0, tiled=True)
    held = {0: weight}
    bit = n_tensor // 2
    while bit:
        held.update({m | bit: swap(w, "tensor", n_tensor, bit) for m, w in list(held.items())})
        bit //= 2
    ctxs = [[ctx]] + [[swap(ctx, "dp", n_dp, q)] for q in range(1, NEAR)]
    return ctxs, mix(info, ctx, [[held[m]] for m in range(n_tensor)], False), []


def gather_small(n_dp, n_tensor, side, info, weight, context):
    barrier = lax.optimization_barrier

    def dp(x, mask):
        return swap(x, "dp", n_dp, mask)

    def tensor(x, mask):
        return swap(x, "tensor", n_tensor, mask)

    dout = weight.shape[1]
    cut = dout // 4
    mine = tensor(lax.dynamic_slice_in_dim(weight, side * cut, cut, 1), 2)
    rest = weight[:, 2 * cut :]
    mine, context = barrier((mine, context))
    ctx = jnp.stack([context[0]] + [tensor(context[m], m) for m in range(1, n_tensor)])
    other, mine_beside = dp(mine, 1), tensor(mine, 1)
    rest, other, mine_beside, ctx, own = barrier((rest, other, mine_beside, ctx, weight))
    rest, other_beside, beside = tensor(rest, 2), tensor(other, 1), tensor(own, 1)
    ctx_x, ctx_z = dp(ctx, 1), dp(ctx, 2)
    early = mix(info, ctx, [[weight], [beside], [mine, other], [mine_beside, other_beside]], True)
    rest, early, ctx_x, ctx_z = barrier((rest, early, ctx_x, ctx_z))
    half = ctx.shape[1] // 2
    ctxs = [[ctx], [ctx_x], [ctx_z], [dp(ctx_x[:, :half], 2), dp(ctx_z[:, half:], 1)]]
    return ctxs, early, [rest, tensor(rest, 1)]


def on_device(
    n_dp,
    n_tensor,
    query_states,
    key_states,
    value_states,
    joining_weight,
    norm_gain,
    next_hidden,
    lengths,
    vote_counts,
):
    _, tokens, width = query_states.shape
    seq = tokens // lengths.shape[0]
    dout = norm_gain.shape[0]
    rows = next_hidden.shape[0]
    chunks = 2 if dout // n_dp >= 256 else 1
    xor_far = (n_tensor, n_dp // NEAR) == (4, 2)
    plan = (n_dp, n_tensor, chunks, seq, xor_far)
    me = lax.axis_index("tensor").astype(jnp.int32)
    group = lax.axis_index("dp").astype(jnp.int32)
    info = jnp.stack([me, group, lengths[0], vote_counts[0]])

    attended = attend(lengths, me.reshape(1), query_states[0], key_states[0], value_states[0], rows, xor_far)
    gather = gather_small if xor_far else gather_large
    ctxs, early, late = gather(n_dp, n_tensor, group & 1, info, joining_weight[0], attended)
    hidden, grads = join(plan, info, early, norm_gain[None, :], next_hidden, late)
    parts = []
    for j in range(chunks):
        near = [grads[j][0]] + [swap(grads[j][q], "dp", n_dp, q) for q in range(1, NEAR)]
        keep, send = gradient(plan, dout, info, ctxs, near)
        got = swap(send, "tensor", n_tensor, 1)
        parts.append(exchange_far(plan, True, dout, width, keep, got))
    weight_grad, gain_grad, loss = finish(plan, dout, width, parts)
    return (hidden, weight_grad[None], gain_grad.reshape(dout), loss.reshape(()))


def solution(mesh):
    return jax.shard_map(
        functools.partial(on_device, mesh.shape["dp"], mesh.shape["tensor"]),
        mesh=mesh,
        in_specs=(
            P(None, "dp", "tensor"),
            P(None, "dp", "tensor"),
            P(None, "dp", "tensor"),
            P(None, "tensor", None),
            P(),
            P(("dp", "tensor"), None),
            P("dp"),
            P("dp"),
        ),
        out_specs=(P(("dp", "tensor"), None), P(None, "tensor", "dp"), P(), P()),
        check_vma=False,
    )
```

```python
import functools
import math

import jax
import jax.numpy as jnp
from jax import lax
from jax.experimental import pallas as pl
from jax.experimental.pallas import tpu as pltpu
from jax.sharding import PartitionSpec as P

HD = 128
QB = 128
ROWS = 256
COLS = 256
NEAR = 4
SHORTEST = 256
STAT_ROWS = 32

loss_scale = 65536.0
neg_large = -1e30
MIB = 1 << 20
BF = jnp.bfloat16
F32 = jnp.float32


def dot(a, b, dims):
    return lax.dot_general(a, b, (dims, ((), ())), preferred_element_type=F32)


def split_words(x):
    high = x.astype(BF).astype(F32)
    return high, (x - high).astype(BF).astype(F32)


def shape(dims, dtype=BF):
    return jax.ShapeDtypeStruct(dims, dtype)


def params():
    return pltpu.CompilerParams(vmem_limit_bytes=32 * MIB)


VM = pl.BlockSpec(memory_space=pltpu.VMEM)
SM = pl.BlockSpec(memory_space=pltpu.SMEM)


def attend_body(len_ref, me_ref, q_ref, k_ref, v_ref, *out_refs):
    seq = q_ref.shape[0]
    o_ref = out_refs[-1]
    rows = o_ref.shape[2]
    rate = math.log2(math.e) / math.sqrt(HD)
    length = len_ref[0]
    key = lax.broadcasted_iota(jnp.int32, (seq, 1), 0)
    hide = jnp.where(key < length, 0.0, neg_large)
    r = lax.broadcasted_iota(jnp.int32, (QB, QB), 0)
    c = lax.broadcasted_iota(jnp.int32, (QB, QB), 1)
    for h in range(q_ref.shape[1] // HD):
        at = slice(h * HD, (h + 1) * HD)
        q_t, v_t = q_ref[:, at].T, v_ref[:, at].T
        for i in range(seq // QB):
            keys = (i + 1) * QB
            scores = dot(k_ref[:keys, at], q_t[:, i * QB : keys], ((1,), (0,)))
            if keys > SHORTEST:
                scores = jnp.concatenate([scores[:SHORTEST], scores[SHORTEST:] + hide[SHORTEST:keys]], 0)
            last = jnp.where(r <= c, scores[keys - QB :], neg_large)
            scores = last if i == 0 else jnp.concatenate([scores[: keys - QB], last], 0)
            peak = jnp.max(scores, axis=0, keepdims=True)
            e = jnp.exp2((scores - peak) * rate)
            total = jnp.sum(e, axis=0, keepdims=True)
            out = (dot(v_t[:, :keys], e.astype(BF), ((1,), (0,))) / total).astype(BF)
            for n in range(0, QB, min(rows, QB)):
                block, first = divmod(i * QB + n, rows)
                o_ref[block, at, first : first + min(rows, QB)] = out[:, n : n + rows]
    for m, ref in enumerate(out_refs[:-1]):
        ref[...] = o_ref[me_ref[0] ^ m]


def attend(lengths, me, q, k, v, rows, split):
    seq, width = q.shape
    heads = width // HD
    blocks = seq // rows
    return pl.pallas_call(
        attend_body,
        in_specs=[SM, SM, VM, VM, VM],
        out_specs=[VM] * (blocks if split else 1),
        out_shape=[shape((width, rows))] * blocks if split else [shape((blocks, width, rows))],
        scratch_shapes=[pltpu.VMEM((blocks, width, rows), BF)] if split else [],
        compiler_params=pltpu.CompilerParams(vmem_limit_bytes=60 * MIB),
        cost_estimate=pl.CostEstimate(
            flops=4 * seq * seq * width, bytes_accessed=8 * seq * width, transcendentals=heads * seq * seq
        ),
        name="attend",
    )(lengths, me, q, k, v)


def mix_body(n_tensor, counts, split, info_ref, ctx_ref, *refs):
    w_refs, at = [], 0
    for n in counts:
        w_refs.append(refs[at : at + n])
        at += n
    part_ref, square_ref, turned_ref = refs[at:]
    dout = part_ref.shape[1]
    me, side = info_ref[0], info_ref[1] % 2
    for m in range(n_tensor):
        turned_ref[m] = ctx_ref[m if split else me ^ m].T
    columns = [(c, 0, c) for c in range(0, dout, COLS)]
    if max(counts) > 1:
        cut = w_refs[-1][0].shape[1]
        columns = [(pl.multiple_of(side * cut + c, COLS), 0, c) for c in range(0, cut, COLS)]
        columns += [(pl.multiple_of((1 - side) * cut + c, COLS), 1, c) for c in range(0, cut, COLS)]
        columns += [(c, None, c) for c in range(2 * cut, dout, COLS)]
    for step, (start, piece, first) in enumerate(columns):
        to = pl.ds(start, COLS)
        total = None
        for m in range(n_tensor):
            whole = len(w_refs[m]) == 1
            if not whole and piece is None:
                continue
            w = w_refs[m][0][:, to] if whole else w_refs[m][piece][:, first : first + COLS]
            part = dot(turned_ref[m], w, ((1,), (0,)))
            total = part if total is None else total + part
        part_ref[:, to] = total
        if piece is not None:
            sq = total * total
            lanes = sum(sq[:, i : i + 128] for i in range(0, COLS, 128))
            square_ref[...] = lanes if step == 0 else square_ref[...] + lanes


def mix(info, ctx, weights, split):
    n_tensor, width, rows = ctx.shape
    dout = weights[0][0].shape[1]
    counts = [len(w) for w in weights]
    return pl.pallas_call(
        functools.partial(mix_body, n_tensor, counts, split),
        in_specs=[SM] + [VM] * (1 + sum(counts)),
        out_specs=[VM] * 3,
        out_shape=[shape((rows, dout), F32), shape((rows, 128), F32), shape((n_tensor, rows, width))],
        compiler_params=params(),
        cost_estimate=pl.CostEstimate(
            flops=2 * rows * dout * width * n_tensor,
            bytes_accessed=2 * dout * (width * n_tensor + 2 * rows),
            transcendentals=0,
        ),
        name="mix",
    )(info, ctx, *[w for held in weights for w in held])


def join_body(plan, n_late, info_ref, part_ref, early_ref, turned_ref, gain_ref, next_ref, *refs):
    n_dp, n_tensor, chunks, seq, xor_far = plan
    late_refs, hidden_ref, grad_refs = refs[:n_late], refs[n_late], refs[n_late + 1 : -4]
    joined_ref, square_ref, acc_ref, slope_ref = refs[-4:]
    rows, dout = joined_ref.shape
    step = acc_ref.shape[0]
    me, group, length, votes = info_ref[0], info_ref[1], info_ref[2], info_ref[3]
    near, far = group % NEAR, group // NEAR
    square_ref[...] = early_ref[...]
    ready = dout - late_refs[0].shape[1] if n_late else dout
    for c in range(ready, dout, COLS):
        total = part_ref[:, c : c + COLS]
        for m, ref in enumerate(late_refs, n_tensor - n_late):
            total += dot(turned_ref[m], ref[:, c - ready : c - ready + COLS], ((1,), (0,)))
        joined_ref[:, c : c + COLS] = total
        sq = total * total
        square_ref[...] += sum(sq[:, i : i + 128] for i in range(0, COLS, 128))
    acc_ref[...] = jnp.zeros_like(acc_ref)
    slice_w = dout // n_dp
    cw = slice_w // chunks
    n_far = n_dp // NEAR

    def body(r, carry):
        loss, weights = carry
        at = pl.ds(pl.multiple_of(r * step, step), step)
        inv = lax.rsqrt(jnp.sum(square_ref[at, :], axis=1, keepdims=True) * (1.0 / dout) + 1e-06)
        pos = (me * rows + r * step) % seq + lax.broadcasted_iota(jnp.int32, (step, 1), 0)
        weight = jnp.where(pos < length - 1, votes.astype(F32), 0.0)
        scaled = weight * (loss_scale * 2.0 / dout)
        miss = jnp.zeros((step, 128), F32)
        lean = jnp.zeros((step, 128), F32)
        for c in range(0, dout, 512):
            cs = slice(c, c + 512)
            normed = (part_ref if c < ready else joined_ref)[at, cs] * inv
            gain = gain_ref[:, cs]
            predicted = normed * gain
            hidden_ref[at, cs] = predicted.astype(BF)
            misfit = predicted - next_ref[at, cs].astype(F32)
            grad = scaled * misfit
            slope = grad * gain
            acc_ref[:, cs] += grad * normed
            slope_ref[:, cs] = slope
            sq = misfit * misfit
            ln = slope * normed
            miss += sum(sq[:, i : i + 128] for i in range(0, 512, 128))
            lean += sum(ln[:, i : i + 128] for i in range(0, 512, 128))
            joined_ref[at, cs] = normed
        lean = jnp.sum(lean, axis=1, keepdims=True) * (1.0 / dout)

        def gradient_at(cs):
            return (inv * (slope_ref[:, cs] - joined_ref[at, cs] * lean)).astype(BF)

        for j in range(chunks):
            for q in range(NEAR):
                for b in range(n_far):
                    to = slice(b * cw, (b + 1) * cw)
                    if cw % 128 == 0:
                        other = (far ^ b if xor_far else b) * NEAR + (near ^ q)
                        start = pl.multiple_of(other * slice_w + j * cw, 128)
                        grad_refs[j * NEAR + q][at, to] = gradient_at(pl.ds(start, cw))
                    else:
                        start = (b * NEAR + q) * slice_w + j * cw
                        grad_refs[j][near ^ q, at, to] = gradient_at(slice(start, start + cw))
        loss = loss + weight * (jnp.sum(miss, axis=1, keepdims=True) * (1.0 / dout))
        return loss, weights + weight

    zero = jnp.zeros((step, 1), F32)
    loss, weights = lax.fori_loop(0, rows // step, body, (zero, zero))
    wide = n_far * cw
    gain_sum = jnp.sum(acc_ref[...], axis=0, keepdims=True)
    gain_sum = jnp.concatenate([gain_sum[:, i : i + wide] for i in range(0, dout, wide)], 0)
    lane = lax.broadcasted_iota(jnp.int32, (1, wide), 1)
    loss = jnp.sum(loss, axis=0, keepdims=True)
    weights = jnp.sum(weights, axis=0, keepdims=True)
    scalars = jnp.where(lane == 0, loss, jnp.where(lane == 1, weights, 0.0))
    words = [*split_words(gain_sum), *split_words(scalars)]
    left = STAT_ROWS - sum(w.shape[0] for w in words)
    words = jnp.concatenate([*words, jnp.zeros((left, wide), F32)], 0).astype(BF)
    if cw % 128 == 0:
        for q in range(NEAR):
            grad_refs[q][rows:, :] = words
    else:
        for q in range(NEAR):
            grad_refs[0][q, rows:, :] = words


def join(plan, info, early, gain, next_hidden, late):
    n_dp, n_tensor, chunks, _, _ = plan
    _, rows, width = early[2].shape
    step = min(ROWS, rows)
    dout = gain.shape[1]
    wide = dout // NEAR // chunks
    tall = [rows + STAT_ROWS] + [rows] * (chunks - 1)
    aligned = dout // n_dp // chunks % 128 == 0
    if aligned:
        grads = [shape((n, wide)) for n in tall for _ in range(NEAR)]
    else:
        grads = [shape((NEAR, n, wide)) for n in tall]
    out = pl.pallas_call(
        functools.partial(join_body, plan, len(late)),
        in_specs=[SM] + [VM] * (5 + len(late)),
        out_specs=[VM] * (1 + len(grads)),
        out_shape=[shape((rows, dout)), *grads],
        scratch_shapes=[
            pltpu.VMEM((rows, dout), F32),
            pltpu.VMEM((rows, 128), F32),
            pltpu.VMEM((step, dout), F32),
            pltpu.VMEM((step, dout), F32),
        ],
        compiler_params=params(),
        cost_estimate=pl.CostEstimate(
            flops=rows * dout * width,
            bytes_accessed=2 * dout * (width + 5 * rows),
            transcendentals=rows,
        ),
        name="join",
    )(info, *early, gain, next_hidden, *late)
    if aligned:
        return out[0], [out[1 + j * NEAR : 1 + (j + 1) * NEAR] for j in range(chunks)]
    return out[0], [[g[q] for q in range(NEAR)] for g in out[1:]]


def stat_sizes(dout, wide, cw):
    in_block = dout // cw
    return dout // wide, in_block, -(-(2 * in_block + 2) // 16) * 16


def block_words(gains, scalars, tall, cw):
    words = [*split_words(gains), *split_words(scalars)]
    left = tall - sum(w.shape[0] for w in words)
    return jnp.concatenate([*words, jnp.zeros((left, cw), F32)], 0).astype(BF)


def block_sums(words, n):
    words = words.astype(F32)
    return words[:n] + words[n : 2 * n], words[2 * n : 2 * n + 1] + words[2 * n + 1 : 2 * n + 2]


def grad_body(plan, dout, counts, info_ref, *refs):
    n_dp, n_tensor, _, _, xor_far = plan
    keep_ref, send_ref = refs[-2:]
    ctx_refs, at = [], 0
    for n in counts:
        ctx_refs.append(refs[at : at + n])
        at += n
    g_refs = refs[at:-2]
    n_y, n_far, tall, cw = keep_ref.shape
    feats, rows = ctx_refs[0][0].shape[1:]
    wide = n_far * cw
    me = info_ref[0]
    core = me % 2
    if tall > feats:
        in_piece, in_block, stat_rows = stat_sizes(dout, wide, cw)
        sums = sum(ref[rows:, :].astype(F32) for ref in g_refs)
        gains, scalars = block_sums(sums, in_piece)
        gains = jnp.concatenate([gains[:, b * cw : (b + 1) * cw] for b in range(n_far)], 0)
        words = block_words(gains, scalars[:, :cw], stat_rows, cw)
    for s, ref in ((1, send_ref), (0, keep_ref)):
        for a in range(n_y):
            m = a * 2 + (s if xor_far else core ^ s)
            total = None
            for parts, g in zip(ctx_refs, g_refs):
                c = jnp.concatenate([part[m] for part in parts], 0) if len(parts) > 1 else parts[0][m]
                part = dot(c, g[:rows, :], ((1,), (0,)))
                total = part if total is None else total + part
            total = total.astype(BF)
            for b in range(n_far):
                ref[a, b, :feats, :] = total[:, b * cw : (b + 1) * cw]
                if tall > feats:
                    ref[a, b, feats:, :] = words


def gradient(plan, dout, info, ctxs, grads):
    n_dp, n_tensor, chunks, _, _ = plan
    _, feats, rows = ctxs[0][0].shape
    wide = grads[0].shape[1]
    cw = dout // n_dp // chunks
    tall = feats
    if grads[0].shape[0] > rows:
        tall += stat_sizes(dout, wide, cw)[2]
    block = shape((n_tensor // 2, n_dp // NEAR, tall, cw))
    return pl.pallas_call(
        functools.partial(grad_body, plan, dout, [len(c) for c in ctxs]),
        in_specs=[SM] + [VM] * (NEAR + sum(len(c) for c in ctxs)),
        out_specs=[VM, VM],
        out_shape=[block, block],
        compiler_params=params(),
        cost_estimate=pl.CostEstimate(
            flops=2 * NEAR * n_tensor * rows * feats * wide,
            bytes_accessed=2 * (NEAR * rows * (n_tensor * feats + wide) + n_tensor * feats * wide),
            transcendentals=0,
        ),
        name="gradient",
    )(info, *[part for parts in ctxs for part in parts], *grads)


def merge_body(in_block, feats, keep_ref, got_ref, *out_refs):
    n_y, n_far, tall, cw = keep_ref.shape
    if tall > feats:
        gains, scalars = block_sums(keep_ref[0, 0, feats:, :], in_block)
        more, others = block_sums(got_ref[0, 0, feats:, :], in_block)
        words = block_words(gains + more, scalars + others, tall - feats, cw)
    each = out_refs[0].shape[0] * out_refs[0].shape[1]
    for i in range(n_y * n_far):
        a, b = divmod(i, n_far)
        total = keep_ref[a, b, :feats, :].astype(F32) + got_ref[a, b, :feats, :].astype(F32)
        ref, at = out_refs[i // each], divmod(i % each, out_refs[0].shape[1])
        ref[(*at, slice(0, feats), slice(None))] = total.astype(BF)
        if tall > feats:
            ref[(*at, slice(feats, tall), slice(None))] = words


def merge(dims, dout, feats, keep, got):
    n_y, n_far, tall, cw = keep.shape
    outs = [shape((*dims, tall, cw))] * (n_y * n_far // math.prod(dims))
    return pl.pallas_call(
        functools.partial(merge_body, dout // cw, feats),
        in_specs=[VM, VM],
        out_specs=[VM] * len(outs),
        out_shape=outs,
        compiler_params=params(),
        cost_estimate=pl.CostEstimate(flops=keep.size, bytes_accessed=6 * keep.size, transcendentals=0),
        name="merge",
    )(keep, got)


def finish_body(counts, in_piece, n_far, *refs):
    grad_ref, gain_ref, loss_ref = refs[-3:]
    feats = grad_ref.shape[0]
    chunks, at = [], 0
    for n in counts:
        chunks.append(refs[at : at + n])
        at += n
    tall, cw = chunks[0][0].shape[2:]

    def total(blocks, rows):
        parts = [
            r[a, b, rows, :].astype(F32) for r in blocks for a in range(r.shape[0]) for b in range(r.shape[1])
        ]
        return sum(parts[1:], parts[0])

    gains, scalars = block_sums(total(chunks[0], slice(feats, tall)), in_piece * n_far)
    lane = lax.broadcasted_iota(jnp.int32, (1, cw), 1)
    weight = jnp.sum(jnp.where(lane == 1, scalars, 0.0), axis=1, keepdims=True)
    loss_ref[0, 0] = jnp.sum(jnp.where(lane == 0, scalars / weight, 0.0))
    gains = gains / weight
    for r in range(in_piece):
        for b in range(n_far):
            gain_ref[pl.ds(r * n_far + b, 1), :] = gains[b * in_piece + r : b * in_piece + r + 1, :]
    for j, blocks in enumerate(chunks):
        grad_ref[:, j * cw : (j + 1) * cw] = (total(blocks, slice(0, feats)) / weight).astype(BF)


def finish(plan, dout, feats, chunks):
    n_dp = plan[0]
    cw = chunks[0][0].shape[3]
    n_far = n_dp // NEAR
    return pl.pallas_call(
        functools.partial(finish_body, [len(c) for c in chunks], dout // (n_far * cw), n_far),
        in_specs=[VM] * sum(len(c) for c in chunks),
        out_specs=[VM, VM, SM],
        out_shape=[shape((feats, dout // n_dp)), shape((dout // cw, cw), F32), shape((1, 1), F32)],
        compiler_params=params(),
        name="finish",
    )(*[b for c in chunks for b in c])


def swap(x, axis, n, mask):
    return lax.ppermute(x, axis, [(i, i ^ mask) for i in range(n)])


def swap_far(x, n_dp, n_tensor, a, b):
    mask = b * NEAR * n_tensor + a * 2
    return lax.ppermute(x, ("dp", "tensor"), [(i, i ^ mask) for i in range(n_dp * n_tensor)])


def exchange_far(plan, two_steps, dout, feats, keep, got):
    n_dp, n_tensor, _, _, pairwise = plan
    n_y, n_far = n_tensor // 2, n_dp // NEAR
    if not pairwise:
        groups = [
            [(NEAR * f + q) * n_tensor + 2 * y + c for y in range(n_y) for f in range(n_far)]
            for q in range(NEAR)
            for c in range(2)
        ]
        (x,) = merge((n_y, n_far), dout, feats, keep, got)
        x = x.reshape(n_y * n_far, *x.shape[2:])
        x = lax.all_to_all(x, ("dp", "tensor"), 0, 0, tiled=True, axis_index_groups=groups)
        return [x.reshape(keep.shape)]

    def far(x, a, b):
        return swap_far(x, n_dp, n_tensor, a, b)

    if two_steps:
        own, across = merge((1, 2), dout, feats, keep, got)
        own, beyond = merge((1, 1), dout, feats, own, far(across, 1, 0))
        return [own, far(beyond, 0, 1)]
    blocks = merge((1, 1), dout, feats, keep, got)
    return [blocks[0], far(blocks[1], 0, 1), far(blocks[2], 1, 0), far(blocks[3], 1, 1)]


def gather_large(n_dp, n_tensor, _, info, weight, context):
    ctx = lax.all_to_all(context[0], "tensor", 0, 0, tiled=True)
    held = {0: weight}
    bit = n_tensor // 2
    while bit:
        held.update({m | bit: swap(w, "tensor", n_tensor, bit) for m, w in list(held.items())})
        bit //= 2
    ctxs = [[ctx]] + [[swap(ctx, "dp", n_dp, q)] for q in range(1, NEAR)]
    return ctxs, mix(info, ctx, [[held[m]] for m in range(n_tensor)], False), []


def gather_small(n_dp, n_tensor, side, info, weight, context):
    barrier = lax.optimization_barrier

    def dp(x, mask):
        return swap(x, "dp", n_dp, mask)

    def tensor(x, mask):
        return swap(x, "tensor", n_tensor, mask)

    dout = weight.shape[1]
    cut = dout // 4
    mine = tensor(lax.dynamic_slice_in_dim(weight, side * cut, cut, 1), 2)
    beside = tensor(weight, 1)
    rest = weight[:, 2 * cut :]
    mine, beside, context = barrier((mine, beside, context))
    ctx = jnp.stack([context[0]] + [tensor(context[m], m) for m in range(1, n_tensor)])
    other, mine_beside = dp(mine, 1), tensor(mine, 1)
    rest, other, mine_beside, ctx = barrier((rest, other, mine_beside, ctx))
    rest, other_beside = tensor(rest, 2), tensor(other, 1)
    ctx_x, ctx_z = dp(ctx, 1), dp(ctx, 2)
    early = mix(info, ctx, [[weight], [beside], [mine, other], [mine_beside, other_beside]], True)
    rest, early, ctx_x, ctx_z = barrier((rest, early, ctx_x, ctx_z))
    half = ctx.shape[1] // 2
    ctxs = [[ctx], [ctx_x], [ctx_z], [dp(ctx_x[:, :half], 2), dp(ctx_z[:, half:], 1)]]
    return ctxs, early, [rest, tensor(rest, 1)]


def on_device(
    n_dp,
    n_tensor,
    query_states,
    key_states,
    value_states,
    joining_weight,
    norm_gain,
    next_hidden,
    lengths,
    vote_counts,
):
    _, tokens, width = query_states.shape
    seq = tokens // lengths.shape[0]
    dout = norm_gain.shape[0]
    rows = next_hidden.shape[0]
    chunks = 2 if dout // n_dp >= 256 else 1
    xor_far = (n_tensor, n_dp // NEAR) == (4, 2)
    plan = (n_dp, n_tensor, chunks, seq, xor_far)
    me = lax.axis_index("tensor").astype(jnp.int32)
    group = lax.axis_index("dp").astype(jnp.int32)
    info = jnp.stack([me, group, lengths[0], vote_counts[0]])

    attended = attend(lengths, me.reshape(1), query_states[0], key_states[0], value_states[0], rows, xor_far)
    gather = gather_small if xor_far else gather_large
    ctxs, early, late = gather(n_dp, n_tensor, group & 1, info, joining_weight[0], attended)
    hidden, grads = join(plan, info, early, norm_gain[None, :], next_hidden, late)
    parts = []
    for j in range(chunks):
        near = [grads[j][0]] + [swap(grads[j][q], "dp", n_dp, q) for q in range(1, NEAR)]
        keep, send = gradient(plan, dout, info, ctxs, near)
        got = swap(send, "tensor", n_tensor, 1)
        parts.append(exchange_far(plan, j == chunks - 1, dout, width, keep, got))
    weight_grad, gain_grad, loss = finish(plan, dout, width, parts)
    return (hidden, weight_grad[None], gain_grad.reshape(dout), loss.reshape(()))


def solution(mesh):
    return jax.shard_map(
        functools.partial(on_device, mesh.shape["dp"], mesh.shape["tensor"]),
        mesh=mesh,
        in_specs=(
            P(None, "dp", "tensor"),
            P(None, "dp", "tensor"),
            P(None, "dp", "tensor"),
            P(None, "tensor", None),
            P(),
            P(("dp", "tensor"), None),
            P("dp"),
            P("dp"),
        ),
        out_specs=(P(("dp", "tensor"), None), P(None, "tensor", "dp"), P(), P()),
        check_vma=False,
    )
```

```python
import functools
import math

import jax
import jax.numpy as jnp
from jax import lax
from jax.experimental import pallas as pl
from jax.experimental.pallas import tpu as pltpu
from jax.sharding import PartitionSpec as P

HD = 128
QB = 128
ROWS = 256
COLS = 256
NEAR = 4
SHORTEST = 256
STAT_ROWS = 32

loss_scale = 65536.0
neg_large = -1e30
MIB = 1 << 20
BF = jnp.bfloat16
F32 = jnp.float32


def dot(a, b, dims):
    return lax.dot_general(a, b, (dims, ((), ())), preferred_element_type=F32)


def split_words(x):
    high = x.astype(BF).astype(F32)
    return high, (x - high).astype(BF).astype(F32)


def shape(dims, dtype=BF):
    return jax.ShapeDtypeStruct(dims, dtype)


def params():
    return pltpu.CompilerParams(vmem_limit_bytes=32 * MIB)


VM = pl.BlockSpec(memory_space=pltpu.VMEM)
SM = pl.BlockSpec(memory_space=pltpu.SMEM)


def attend_body(len_ref, me_ref, q_ref, k_ref, v_ref, *out_refs):
    seq = q_ref.shape[0]
    o_ref = out_refs[-1]
    rows = o_ref.shape[2]
    rate = math.log2(math.e) / math.sqrt(HD)
    length = len_ref[0]
    key = lax.broadcasted_iota(jnp.int32, (seq, 1), 0)
    hide = jnp.where(key < length, 0.0, neg_large)
    r = lax.broadcasted_iota(jnp.int32, (QB, QB), 0)
    c = lax.broadcasted_iota(jnp.int32, (QB, QB), 1)
    for h in range(q_ref.shape[1] // HD):
        at = slice(h * HD, (h + 1) * HD)
        q_t, v_t = q_ref[:, at].T, v_ref[:, at].T
        for i in range(seq // QB):
            keys = (i + 1) * QB
            scores = dot(k_ref[:keys, at], q_t[:, i * QB : keys], ((1,), (0,)))
            if keys > SHORTEST:
                scores = jnp.concatenate([scores[:SHORTEST], scores[SHORTEST:] + hide[SHORTEST:keys]], 0)
            last = jnp.where(r <= c, scores[keys - QB :], neg_large)
            scores = last if i == 0 else jnp.concatenate([scores[: keys - QB], last], 0)
            peak = jnp.max(scores, axis=0, keepdims=True)
            e = jnp.exp2((scores - peak) * rate)
            total = jnp.sum(e, axis=0, keepdims=True)
            out = (dot(v_t[:, :keys], e.astype(BF), ((1,), (0,))) / total).astype(BF)
            for n in range(0, QB, min(rows, QB)):
                block, first = divmod(i * QB + n, rows)
                o_ref[block, at, first : first + min(rows, QB)] = out[:, n : n + rows]
    for m, ref in enumerate(out_refs[:-1]):
        ref[...] = o_ref[me_ref[0] ^ m]


def attend(lengths, me, q, k, v, rows, split):
    seq, width = q.shape
    heads = width // HD
    blocks = seq // rows
    return pl.pallas_call(
        attend_body,
        in_specs=[SM, SM, VM, VM, VM],
        out_specs=[VM] * (blocks if split else 1),
        out_shape=[shape((width, rows))] * blocks if split else [shape((blocks, width, rows))],
        scratch_shapes=[pltpu.VMEM((blocks, width, rows), BF)] if split else [],
        compiler_params=pltpu.CompilerParams(vmem_limit_bytes=60 * MIB),
        cost_estimate=pl.CostEstimate(
            flops=4 * seq * seq * width, bytes_accessed=8 * seq * width, transcendentals=heads * seq * seq
        ),
        name="attend",
    )(lengths, me, q, k, v)


def mix_body(n_tensor, counts, split, info_ref, ctx_ref, *refs):
    w_refs, at = [], 0
    for n in counts:
        w_refs.append(refs[at : at + n])
        at += n
    part_ref, square_ref, turned_ref = refs[at:]
    dout = part_ref.shape[1]
    me, side = info_ref[0], info_ref[1] % 2
    for m in range(n_tensor):
        turned_ref[m] = ctx_ref[m if split else me ^ m].T
    columns = [(c, 0, c) for c in range(0, dout, COLS)]
    if max(counts) > 1:
        cut = w_refs[-1][0].shape[1]
        columns = [(pl.multiple_of(side * cut + c, COLS), 0, c) for c in range(0, cut, COLS)]
        columns += [(pl.multiple_of((1 - side) * cut + c, COLS), 1, c) for c in range(0, cut, COLS)]
        columns += [(c, None, c) for c in range(2 * cut, dout, COLS)]
    for step, (start, piece, first) in enumerate(columns):
        to = pl.ds(start, COLS)
        total = None
        for m in range(n_tensor):
            whole = len(w_refs[m]) == 1
            if not whole and piece is None:
                continue
            w = w_refs[m][0][:, to] if whole else w_refs[m][piece][:, first : first + COLS]
            part = dot(turned_ref[m], w, ((1,), (0,)))
            total = part if total is None else total + part
        part_ref[:, to] = total
        if piece is not None:
            sq = total * total
            lanes = sum(sq[:, i : i + 128] for i in range(0, COLS, 128))
            square_ref[...] = lanes if step == 0 else square_ref[...] + lanes


def mix(info, ctx, weights, split):
    n_tensor, width, rows = ctx.shape
    dout = weights[0][0].shape[1]
    counts = [len(w) for w in weights]
    return pl.pallas_call(
        functools.partial(mix_body, n_tensor, counts, split),
        in_specs=[SM] + [VM] * (1 + sum(counts)),
        out_specs=[VM] * 3,
        out_shape=[shape((rows, dout), F32), shape((rows, 128), F32), shape((n_tensor, rows, width))],
        compiler_params=params(),
        cost_estimate=pl.CostEstimate(
            flops=2 * rows * dout * width * n_tensor,
            bytes_accessed=2 * dout * (width * n_tensor + 2 * rows),
            transcendentals=0,
        ),
        name="mix",
    )(info, ctx, *[w for held in weights for w in held])


def join_body(plan, n_late, info_ref, part_ref, early_ref, turned_ref, gain_ref, next_ref, *refs):
    n_dp, n_tensor, chunks, seq, xor_far = plan
    late_refs, hidden_ref, grad_refs = refs[:n_late], refs[n_late], refs[n_late + 1 : -4]
    joined_ref, square_ref, acc_ref, slope_ref = refs[-4:]
    rows, dout = joined_ref.shape
    step = slope_ref.shape[0]
    me, group, length, votes = info_ref[0], info_ref[1], info_ref[2], info_ref[3]
    near, far = group % NEAR, group // NEAR
    square_ref[...] = early_ref[...]
    ready = dout - late_refs[0].shape[1] if n_late else dout
    for c in range(ready, dout, COLS):
        total = part_ref[:, c : c + COLS]
        for m, ref in enumerate(late_refs, n_tensor - n_late):
            total += dot(turned_ref[m], ref[:, c - ready : c - ready + COLS], ((1,), (0,)))
        joined_ref[:, c : c + COLS] = total
        sq = total * total
        square_ref[...] += sum(sq[:, i : i + 128] for i in range(0, COLS, 128))
    acc_ref[...] = jnp.zeros_like(acc_ref)
    slice_w = dout // n_dp
    cw = slice_w // chunks
    n_far = n_dp // NEAR

    def body(r, carry):
        loss, weights = carry
        at = pl.ds(pl.multiple_of(r * step, step), step)
        inv = lax.rsqrt(jnp.sum(square_ref[at, :], axis=1, keepdims=True) * (1.0 / dout) + 1e-06)
        pos = (me * rows + r * step) % seq + lax.broadcasted_iota(jnp.int32, (step, 1), 0)
        weight = jnp.where(pos < length - 1, votes.astype(F32), 0.0)
        scaled = weight * (loss_scale * 2.0 / dout)
        miss = jnp.zeros((step, 128), F32)
        lean = jnp.zeros((step, 128), F32)
        for c in range(0, dout, 512):
            cs = slice(c, c + 512)
            normed = (part_ref if c < ready else joined_ref)[at, cs] * inv
            gain = gain_ref[:, cs]
            predicted = normed * gain
            hidden_ref[at, cs] = predicted.astype(BF)
            misfit = predicted - next_ref[at, cs].astype(F32)
            grad = scaled * misfit
            slope = grad * gain
            acc_ref[:, cs] += jnp.sum((grad * normed).reshape(step // 8, 8, 512), axis=0)
            slope_ref[:, cs] = slope
            sq = misfit * misfit
            ln = slope * normed
            miss += sum(sq[:, i : i + 128] for i in range(0, 512, 128))
            lean += sum(ln[:, i : i + 128] for i in range(0, 512, 128))
            joined_ref[at, cs] = normed
        lean = jnp.sum(lean, axis=1, keepdims=True) * (1.0 / dout)

        def gradient_at(cs):
            return (inv * (slope_ref[:, cs] - joined_ref[at, cs] * lean)).astype(BF)

        for j in range(chunks):
            for q in range(NEAR):
                for b in range(n_far):
                    to = slice(b * cw, (b + 1) * cw)
                    if cw % 128 == 0:
                        other = (far ^ b if xor_far else b) * NEAR + (near ^ q)
                        start = pl.multiple_of(other * slice_w + j * cw, 128)
                        grad_refs[j * NEAR + q][at, to] = gradient_at(pl.ds(start, cw))
                    else:
                        start = (b * NEAR + q) * slice_w + j * cw
                        grad_refs[j][near ^ q, at, to] = gradient_at(slice(start, start + cw))
        loss = loss + weight * (jnp.sum(miss, axis=1, keepdims=True) * (1.0 / dout))
        return loss, weights + weight

    zero = jnp.zeros((step, 1), F32)
    loss, weights = lax.fori_loop(0, rows // step, body, (zero, zero))
    wide = n_far * cw
    gain_sum = jnp.sum(acc_ref[...], axis=0, keepdims=True)
    gain_sum = jnp.concatenate([gain_sum[:, i : i + wide] for i in range(0, dout, wide)], 0)
    lane = lax.broadcasted_iota(jnp.int32, (1, wide), 1)
    loss = jnp.sum(loss, axis=0, keepdims=True)
    weights = jnp.sum(weights, axis=0, keepdims=True)
    scalars = jnp.where(lane == 0, loss, jnp.where(lane == 1, weights, 0.0))
    words = [*split_words(gain_sum), *split_words(scalars)]
    left = STAT_ROWS - sum(w.shape[0] for w in words)
    words = jnp.concatenate([*words, jnp.zeros((left, wide), F32)], 0).astype(BF)
    if cw % 128 == 0:
        for q in range(NEAR):
            grad_refs[q][rows:, :] = words
    else:
        for q in range(NEAR):
            grad_refs[0][q, rows:, :] = words


def join(plan, info, early, gain, next_hidden, late):
    n_dp, n_tensor, chunks, _, _ = plan
    _, rows, width = early[2].shape
    step = min(ROWS, rows)
    dout = gain.shape[1]
    wide = dout // NEAR // chunks
    tall = [rows + STAT_ROWS] + [rows] * (chunks - 1)
    aligned = dout // n_dp // chunks % 128 == 0
    if aligned:
        grads = [shape((n, wide)) for n in tall for _ in range(NEAR)]
    else:
        grads = [shape((NEAR, n, wide)) for n in tall]
    out = pl.pallas_call(
        functools.partial(join_body, plan, len(late)),
        in_specs=[SM] + [VM] * (5 + len(late)),
        out_specs=[VM] * (1 + len(grads)),
        out_shape=[shape((rows, dout)), *grads],
        scratch_shapes=[
            pltpu.VMEM((rows, dout), F32),
            pltpu.VMEM((rows, 128), F32),
            pltpu.VMEM((8, dout), F32),
            pltpu.VMEM((step, dout), F32),
        ],
        compiler_params=params(),
        cost_estimate=pl.CostEstimate(
            flops=rows * dout * width,
            bytes_accessed=2 * dout * (width + 5 * rows),
            transcendentals=rows,
        ),
        name="join",
    )(info, *early, gain, next_hidden, *late)
    if aligned:
        return out[0], [out[1 + j * NEAR : 1 + (j + 1) * NEAR] for j in range(chunks)]
    return out[0], [[g[q] for q in range(NEAR)] for g in out[1:]]


def stat_sizes(dout, wide, cw):
    in_block = dout // cw
    return dout // wide, in_block, -(-(2 * in_block + 2) // 16) * 16


def block_words(gains, scalars, tall, cw):
    words = [*split_words(gains), *split_words(scalars)]
    left = tall - sum(w.shape[0] for w in words)
    return jnp.concatenate([*words, jnp.zeros((left, cw), F32)], 0).astype(BF)


def block_sums(words, n):
    words = words.astype(F32)
    return words[:n] + words[n : 2 * n], words[2 * n : 2 * n + 1] + words[2 * n + 1 : 2 * n + 2]


def grad_body(plan, dout, counts, info_ref, *refs):
    n_dp, n_tensor, _, _, xor_far = plan
    keep_ref, send_ref = refs[-2:]
    ctx_refs, at = [], 0
    for n in counts:
        ctx_refs.append(refs[at : at + n])
        at += n
    g_refs = refs[at:-2]
    n_y, n_far, tall, cw = keep_ref.shape
    feats, rows = ctx_refs[0][0].shape[1:]
    wide = n_far * cw
    me = info_ref[0]
    core = me % 2
    if tall > feats:
        in_piece, in_block, stat_rows = stat_sizes(dout, wide, cw)
        sums = sum(ref[rows:, :].astype(F32) for ref in g_refs)
        gains, scalars = block_sums(sums, in_piece)
        gains = jnp.concatenate([gains[:, b * cw : (b + 1) * cw] for b in range(n_far)], 0)
        words = block_words(gains, scalars[:, :cw], stat_rows, cw)
    for s, ref in ((1, send_ref), (0, keep_ref)):
        for a in range(n_y):
            m = a * 2 + (s if xor_far else core ^ s)
            total = None
            for parts, g in zip(ctx_refs, g_refs):
                c = jnp.concatenate([part[m] for part in parts], 0) if len(parts) > 1 else parts[0][m]
                part = dot(c, g[:rows, :], ((1,), (0,)))
                total = part if total is None else total + part
            total = total.astype(BF)
            for b in range(n_far):
                ref[a, b, :feats, :] = total[:, b * cw : (b + 1) * cw]
                if tall > feats:
                    ref[a, b, feats:, :] = words


def gradient(plan, dout, info, ctxs, grads):
    n_dp, n_tensor, chunks, _, _ = plan
    _, feats, rows = ctxs[0][0].shape
    wide = grads[0].shape[1]
    cw = dout // n_dp // chunks
    tall = feats
    if grads[0].shape[0] > rows:
        tall += stat_sizes(dout, wide, cw)[2]
    block = shape((n_tensor // 2, n_dp // NEAR, tall, cw))
    return pl.pallas_call(
        functools.partial(grad_body, plan, dout, [len(c) for c in ctxs]),
        in_specs=[SM] + [VM] * (NEAR + sum(len(c) for c in ctxs)),
        out_specs=[VM, VM],
        out_shape=[block, block],
        compiler_params=params(),
        cost_estimate=pl.CostEstimate(
            flops=2 * NEAR * n_tensor * rows * feats * wide,
            bytes_accessed=2 * (NEAR * rows * (n_tensor * feats + wide) + n_tensor * feats * wide),
            transcendentals=0,
        ),
        name="gradient",
    )(info, *[part for parts in ctxs for part in parts], *grads)


def merge_body(in_block, feats, keep_ref, got_ref, *out_refs):
    n_y, n_far, tall, cw = keep_ref.shape
    if tall > feats:
        gains, scalars = block_sums(keep_ref[0, 0, feats:, :], in_block)
        more, others = block_sums(got_ref[0, 0, feats:, :], in_block)
        words = block_words(gains + more, scalars + others, tall - feats, cw)
    each = out_refs[0].shape[0] * out_refs[0].shape[1]
    for i in range(n_y * n_far):
        a, b = divmod(i, n_far)
        total = keep_ref[a, b, :feats, :].astype(F32) + got_ref[a, b, :feats, :].astype(F32)
        ref, at = out_refs[i // each], divmod(i % each, out_refs[0].shape[1])
        ref[(*at, slice(0, feats), slice(None))] = total.astype(BF)
        if tall > feats:
            ref[(*at, slice(feats, tall), slice(None))] = words


def merge(dims, dout, feats, keep, got):
    n_y, n_far, tall, cw = keep.shape
    outs = [shape((*dims, tall, cw))] * (n_y * n_far // math.prod(dims))
    return pl.pallas_call(
        functools.partial(merge_body, dout // cw, feats),
        in_specs=[VM, VM],
        out_specs=[VM] * len(outs),
        out_shape=outs,
        compiler_params=params(),
        cost_estimate=pl.CostEstimate(flops=keep.size, bytes_accessed=6 * keep.size, transcendentals=0),
        name="merge",
    )(keep, got)


def finish_body(counts, in_piece, n_far, *refs):
    grad_ref, gain_ref, loss_ref = refs[-3:]
    feats = grad_ref.shape[0]
    chunks, at = [], 0
    for n in counts:
        chunks.append(refs[at : at + n])
        at += n
    tall, cw = chunks[0][0].shape[2:]

    def total(blocks, rows):
        parts = [
            r[a, b, rows, :].astype(F32) for r in blocks for a in range(r.shape[0]) for b in range(r.shape[1])
        ]
        return sum(parts[1:], parts[0])

    gains, scalars = block_sums(total(chunks[0], slice(feats, tall)), in_piece * n_far)
    lane = lax.broadcasted_iota(jnp.int32, (1, cw), 1)
    weight = jnp.sum(jnp.where(lane == 1, scalars, 0.0), axis=1, keepdims=True)
    loss_ref[0, 0] = jnp.sum(jnp.where(lane == 0, scalars / weight, 0.0))
    gains = gains / weight
    for r in range(in_piece):
        for b in range(n_far):
            gain_ref[pl.ds(r * n_far + b, 1), :] = gains[b * in_piece + r : b * in_piece + r + 1, :]
    for j, blocks in enumerate(chunks):
        grad_ref[:, j * cw : (j + 1) * cw] = (total(blocks, slice(0, feats)) / weight).astype(BF)


def finish(plan, dout, feats, chunks):
    n_dp = plan[0]
    cw = chunks[0][0].shape[3]
    n_far = n_dp // NEAR
    return pl.pallas_call(
        functools.partial(finish_body, [len(c) for c in chunks], dout // (n_far * cw), n_far),
        in_specs=[VM] * sum(len(c) for c in chunks),
        out_specs=[VM, VM, SM],
        out_shape=[shape((feats, dout // n_dp)), shape((dout // cw, cw), F32), shape((1, 1), F32)],
        compiler_params=params(),
        name="finish",
    )(*[b for c in chunks for b in c])


def swap(x, axis, n, mask):
    return lax.ppermute(x, axis, [(i, i ^ mask) for i in range(n)])


def swap_far(x, n_dp, n_tensor, a, b):
    mask = b * NEAR * n_tensor + a * 2
    return lax.ppermute(x, ("dp", "tensor"), [(i, i ^ mask) for i in range(n_dp * n_tensor)])


def exchange_far(plan, two_steps, dout, feats, keep, got):
    n_dp, n_tensor, _, _, pairwise = plan
    n_y, n_far = n_tensor // 2, n_dp // NEAR
    if not pairwise:
        groups = [
            [(NEAR * f + q) * n_tensor + 2 * y + c for y in range(n_y) for f in range(n_far)]
            for q in range(NEAR)
            for c in range(2)
        ]
        (x,) = merge((n_y, n_far), dout, feats, keep, got)
        x = x.reshape(n_y * n_far, *x.shape[2:])
        x = lax.all_to_all(x, ("dp", "tensor"), 0, 0, tiled=True, axis_index_groups=groups)
        return [x.reshape(keep.shape)]

    def far(x, a, b):
        return swap_far(x, n_dp, n_tensor, a, b)

    if two_steps:
        own, across = merge((1, 2), dout, feats, keep, got)
        own, beyond = merge((1, 1), dout, feats, own, far(across, 1, 0))
        return [own, far(beyond, 0, 1)]
    blocks = merge((1, 1), dout, feats, keep, got)
    return [blocks[0], far(blocks[1], 0, 1), far(blocks[2], 1, 0), far(blocks[3], 1, 1)]


def gather_large(n_dp, n_tensor, _, info, weight, context):
    ctx = lax.all_to_all(context[0], "tensor", 0, 0, tiled=True)
    held = {0: weight}
    bit = n_tensor // 2
    while bit:
        held.update({m | bit: swap(w, "tensor", n_tensor, bit) for m, w in list(held.items())})
        bit //= 2
    ctxs = [[ctx]] + [[swap(ctx, "dp", n_dp, q)] for q in range(1, NEAR)]
    return ctxs, mix(info, ctx, [[held[m]] for m in range(n_tensor)], False), []


def gather_small(n_dp, n_tensor, side, info, weight, context):
    barrier = lax.optimization_barrier

    def dp(x, mask):
        return swap(x, "dp", n_dp, mask)

    def tensor(x, mask):
        return swap(x, "tensor", n_tensor, mask)

    dout = weight.shape[1]
    cut = dout // 4
    mine = tensor(lax.dynamic_slice_in_dim(weight, side * cut, cut, 1), 2)
    beside = tensor(weight, 1)
    rest = weight[:, 2 * cut :]
    mine, beside, context = barrier((mine, beside, context))
    ctx = jnp.stack([context[0]] + [tensor(context[m], m) for m in range(1, n_tensor)])
    other, mine_beside = dp(mine, 1), tensor(mine, 1)
    rest, other, mine_beside, ctx = barrier((rest, other, mine_beside, ctx))
    rest, other_beside = tensor(rest, 2), tensor(other, 1)
    ctx_x, ctx_z = dp(ctx, 1), dp(ctx, 2)
    early = mix(info, ctx, [[weight], [beside], [mine, other], [mine_beside, other_beside]], True)
    rest, early, ctx_x, ctx_z = barrier((rest, early, ctx_x, ctx_z))
    half = ctx.shape[1] // 2
    ctxs = [[ctx], [ctx_x], [ctx_z], [dp(ctx_x[:, :half], 2), dp(ctx_z[:, half:], 1)]]
    return ctxs, early, [rest, tensor(rest, 1)]


def on_device(
    n_dp,
    n_tensor,
    query_states,
    key_states,
    value_states,
    joining_weight,
    norm_gain,
    next_hidden,
    lengths,
    vote_counts,
):
    _, tokens, width = query_states.shape
    seq = tokens // lengths.shape[0]
    dout = norm_gain.shape[0]
    rows = next_hidden.shape[0]
    chunks = 2 if dout // n_dp >= 256 else 1
    xor_far = (n_tensor, n_dp // NEAR) == (4, 2)
    plan = (n_dp, n_tensor, chunks, seq, xor_far)
    me = lax.axis_index("tensor").astype(jnp.int32)
    group = lax.axis_index("dp").astype(jnp.int32)
    info = jnp.stack([me, group, lengths[0], vote_counts[0]])

    attended = attend(lengths, me.reshape(1), query_states[0], key_states[0], value_states[0], rows, xor_far)
    gather = gather_small if xor_far else gather_large
    ctxs, early, late = gather(n_dp, n_tensor, group & 1, info, joining_weight[0], attended)
    hidden, grads = join(plan, info, early, norm_gain[None, :], next_hidden, late)
    parts = []
    for j in range(chunks):
        near = [grads[j][0]] + [swap(grads[j][q], "dp", n_dp, q) for q in range(1, NEAR)]
        keep, send = gradient(plan, dout, info, ctxs, near)
        got = swap(send, "tensor", n_tensor, 1)
        parts.append(exchange_far(plan, j == chunks - 1, dout, width, keep, got))
    weight_grad, gain_grad, loss = finish(plan, dout, width, parts)
    return (hidden, weight_grad[None], gain_grad.reshape(dout), loss.reshape(()))


def solution(mesh):
    return jax.shard_map(
        functools.partial(on_device, mesh.shape["dp"], mesh.shape["tensor"]),
        mesh=mesh,
        in_specs=(
            P(None, "dp", "tensor"),
            P(None, "dp", "tensor"),
            P(None, "dp", "tensor"),
            P(None, "tensor", None),
            P(),
            P(("dp", "tensor"), None),
            P("dp"),
            P("dp"),
        ),
        out_specs=(P(("dp", "tensor"), None), P(None, "tensor", "dp"), P(), P()),
        check_vma=False,
    )
```
